32 devices in a mesh: groups: 2 (over y), seq: 4 (over z), chan: 2 (over x), rep: 2 (over core).
Axes of the slice: x: 2, y: 2, z: 4, core: 2. Of those that a mesh axis runs over, the one named last changes fastest.
Arguments:
- projected: bfloat16 [4096, 3, 8192], P(('groups', 'seq'), None, ('chan', 'rep')), parts along dimension 0, may hold values from -6 to 6
- short_weight: float32 [3, 3, 8192], P(None, None, ('chan', 'rep')), may hold values from -3.5 to 3.5
- skip_gain: float32 [8192], P(('chan', 'rep')), may hold values from -4 to 4
- pole_rate: float32 [16, 512], P(None, ('chan', 'rep')), may hold values from 2.4414062e-06 to 0.03
- residue: float32 [16, 512], P(None, ('chan', 'rep')), may hold values from -0.088388346 to 0.088388346
- out_weight: bfloat16 [2, 2, 2048, 4096], P(None, 'rep', 'seq', 'chan'), may hold values from -0.0625 to 0.0625
Outputs:
- mixed: bfloat16 [4096, 4096], P(('groups', 'seq'), ('chan', 'rep')), parts along dimension 0
The draws below stay inside these ranges and needn't reach their ends.
There are 2 independent parts, one for each index of `groups`. The reference program is written for one: setup_inputs(seed, part) draws one part's arguments, and reference() takes and returns one part's arrays. A program takes and returns all parts, laid end to end along the dimension named above; an argument that names none is the same for every part. Nothing has to cross between parts.
All inputs are finite; a program needn't handle non-finite values.
Results may differ from the reference program's by a relative error of at most 0.005.
Values may be sent and summed in bfloat16 or wider, within the bound.
A program may use at most 128 MiB of HBM per device.

```python
import math
import jax
import jax.numpy as jnp
from jax import lax

D = 8192
ORDER = 16
DOUT = 4096
BLOCK = 128
SEQ_LEN = 2048
GROUPS = 512
N_CHAN = 2
N_REP = 2


def level_of(own_key, shape, shards, low, top_value):
    def one(dim, blocks):
        draws = jax.random.uniform(jax.random.fold_in(jax.random.fold_in(own_key, 6), dim), (blocks,), jnp.float32, low / len(shards), top_value / len(shards))
        return jnp.repeat(jnp.exp(draws), shape[dim] // blocks).reshape((-1,) + (1,) * (len(shape) - dim - 1))

    level = one(*shards[0])
    for cut in shards[1:]:
        level = level * one(*cut)
    return level


def bell_draw(own_key, shape, deviation, limit, cuts=(), kind=jnp.bfloat16):
    array = jax.random.normal(own_key, shape, jnp.float32) * deviation
    if len(cuts) > 0:
        array = level_of(own_key, shape, cuts, -0.22, 0.18) * array
    return jnp.clip(array, min=-limit, max=limit).astype(kind)


def setup_inputs(seed: int = 0, part: int = 0) -> dict:
    arg_keys = jax.random.split(jax.random.key(seed), 7)
    part_splits = jax.random.split(jax.random.fold_in(arg_keys[6], part), 7)
    return {
        "projected": bell_draw(part_splits[0], (SEQ_LEN, 3, D), 1.0, 6.0, ((0, 4), (2, 4))),
        "short_weight": bell_draw(arg_keys[1], (3, 3, D), 3 ** -0.5, 3.5, ((2, 4),), jnp.float32),
        "skip_gain": bell_draw(arg_keys[2], (D,), 1.0, 4.0, ((0, 4),), jnp.float32),
        "pole_rate": jnp.clip(jnp.exp(math.log(0.03) - 9.416378 * jax.random.uniform(arg_keys[3], (ORDER, GROUPS), jnp.float32) ** level_of(arg_keys[3], (ORDER, GROUPS), ((1, 4),), -0.2, 0.2)), 2.441406195430318e-06, 0.03),
        "residue": bell_draw(arg_keys[4], (ORDER, GROUPS), (0.3 * SEQ_LEN ** -0.5), 0.088388346, ((1, 4),), jnp.float32),
        "out_weight": bell_draw(arg_keys[5], (N_CHAN, N_REP, D // (N_CHAN * N_REP), DOUT), D ** -0.5, 0.0625, ((1, 2), (2, 4), (3, 2))),
    }


def filter_tables(decay_rate, residue, block_len):
    offsets = jnp.arange(block_len, dtype=jnp.int32)
    lag_diff = offsets[:, None] - offsets[None, :]
    lag_float = jnp.maximum(lag_diff, 0).astype(decay_rate.dtype)
    kernel = jnp.zeros((decay_rate.shape[1], block_len, block_len), decay_rate.dtype)
    for order_idx in range(decay_rate.shape[0]):
        kernel = kernel + residue[order_idx][:, None, None] * jnp.exp(-decay_rate[order_idx][:, None, None] * lag_float[None])
    kernel = jnp.where(lag_diff[None] >= 0, kernel, jnp.zeros_like(kernel))
    rate_t = decay_rate.T
    ahead = (offsets + 1).astype(decay_rate.dtype)
    readout = residue.T[:, None, :] * jnp.exp(-rate_t[:, None, :] * ahead[None, :, None])
    behind = (block_len - 1 - offsets).astype(decay_rate.dtype)
    intake = jnp.exp(-rate_t[:, :, None] * behind[None, None, :])
    return kernel, readout, intake


def block_conv(product, decay_rate, residue):
    groups = decay_rate.shape[1]
    group_size = product.shape[1] // groups
    kernel, readout, intake = filter_tables(decay_rate, residue, BLOCK)
    step_decay = jnp.exp(-decay_rate * BLOCK)[:, :, None]
    num_blocks = product.shape[0] // BLOCK
    blocks_in = product.reshape(num_blocks, BLOCK, groups, group_size)
    highest = lax.Precision.HIGHEST

    def block_step(carry_state, block_in):
        inside = jnp.einsum('gij,jgc->igc', kernel, block_in, precision=highest)
        across = jnp.einsum('gin,ngc->igc', readout, carry_state, precision=highest)
        updated = step_decay * carry_state + jnp.einsum('gnj,jgc->ngc', intake, block_in, precision=highest)
        return updated, inside + across

    start_state = jnp.zeros((decay_rate.shape[0], groups, group_size), jnp.float32)
    final_state, outputs = lax.scan(block_step, start_state, blocks_in)
    return outputs.reshape(product.shape)


def reference(projected, short_weight, skip_gain, pole_rate, residue, out_weight):
    features = projected.astype(jnp.float32)
    padded = jnp.pad(features, ((2, 0), (0, 0), (0, 0)))
    length = features.shape[0]
    filtered = short_weight[:, 0][None] * features + short_weight[:, 1][None] * padded[1:length + 1] + short_weight[:, 2][None] * padded[:length]
    query_part = filtered[:, 0]
    key_part = filtered[:, 1]
    value_part = filtered[:, 2]
    product = key_part * value_part
    conv = block_conv(product, pole_rate, residue)
    gated_out = (query_part * (conv + skip_gain[None] * product)).astype(jnp.bfloat16)
    full_weight = out_weight.reshape(-1, out_weight.shape[3])
    return jnp.dot(gated_out, full_weight, preferred_element_type=jnp.float32).astype(jnp.bfloat16)
```

```python
import functools

import jax
import jax.numpy as jnp
from jax import lax
from jax.experimental import pallas as pl
from jax.experimental.pallas import tpu as pltpu
from jax.sharding import PartitionSpec as P

GROUP = 16
LANES = 128
BLOCK = 128
PER_TILE = LANES // GROUP
WIDE = PER_TILE * BLOCK
HALO = 16
Y_SHARE = 7
GATE_PARTS = 4
MESH = pl.DeviceIdType.MESH
HIGHEST = lax.Precision.HIGHEST


def iota(shape, dim):
    return lax.broadcasted_iota(jnp.int32, shape, dim)


def masked_rows(rows):
    lane_group = iota(rows.shape, 1) // GROUP
    zero = jnp.zeros_like(rows)
    return jnp.concatenate(
        [jnp.where(lane_group == g, rows, zero) for g in range(PER_TILE)], axis=0
    )


def kernel(dims, x_hbm, sw_ref, skip_ref, rate_ref, res_ref, w_hbm, out_ref,
           xbuf, halo, ext, lhs, q_buf, base, ends, own_end, prior, rate_ch, readout, gated, wbuf,
           acc, peer, local_sem, halo_sem, end_send, end_recv, gate_send, gate_recv,
           zsend, zrecv, ysend, yrecv, rep_send, rep_recv):
    count, slabs, n_chan, n_rep, chunks, row_chunks = dims
    tok, chans = gated.shape[1], gated.shape[2]
    modes, groups = rate_ref.shape
    tiles = chans // LANES
    blocks = tok // BLOCK
    local_rows, out_cols = w_hbm.shape[2], w_hbm.shape[3]
    half = out_cols // slabs
    y_cols = out_cols // LANES * Y_SHARE // 16 * LANES
    z_cols = out_cols - y_cols
    rows = local_rows // row_chunks
    out_half = out_cols // n_rep
    slab = lax.axis_index("groups")
    seq = lax.axis_index("seq")
    chan = lax.axis_index("chan")
    rep = lax.axis_index("rep")
    other_slab = 1 - slab
    other_rep = 1 - rep

    barrier = pltpu.get_barrier_semaphore()

    def greet(target):
        pl.semaphore_signal(barrier, inc=1, device_id=target, device_id_type=MESH)

    for d in range(1, count):
        greet({"seq": lax.rem(seq + d, count)})
    for d in range(1, n_chan):
        greet({"chan": lax.rem(chan + d, n_chan)})
    greet({"groups": other_slab})
    greet({"rep": other_rep})
    pl.semaphore_wait(barrier, count + n_chan)

    def z_span(h):
        return pl.ds(pl.multiple_of(h * y_cols, LANES), z_cols)

    def y_span(h):
        return pl.ds(pl.multiple_of(h * z_cols, LANES), y_cols)

    def piece(ref, c, r, cols):
        if chunks == 1:
            return ref.at[:, :, cols]
        return ref.at[c, pl.ds(pl.multiple_of(r * rows, rows), rows), cols]

    def split(ch):
        return ch // row_chunks, ch % row_chunks

    def own_piece(ch):
        c, r = split(ch)
        return piece(w_hbm.at[:, 0], c, r, z_span(slab))

    def block_piece(b, ch, cols):
        c, r = split(ch)
        return piece(wbuf.at[b], c, r, cols)

    def target_of(direction):
        return seq + 1 if direction == 0 else seq - 1

    def can_send(direction):
        return seq < count - 1 if direction == 0 else seq > 0

    def origin(direction, k):
        return seq - 1 - k if direction == 0 else seq + 1 + k

    def has(direction, k):
        return seq - 1 - k >= 0 if direction == 0 else seq + 1 + k < count

    def z_copy(direction, k, ch, src, b):
        return pltpu.make_async_remote_copy(
            src_ref=src, dst_ref=block_piece(b, ch, z_span(slab)),
            send_sem=zsend.at[direction, k, ch], recv_sem=zrecv.at[direction, k, ch],
            device_id={"seq": target_of(direction)}, device_id_type=MESH,
        )

    def y_copy(direction, k, ch, h):
        b = origin(direction, k)
        ref = block_piece(b, ch, y_span(h))
        return pltpu.make_async_remote_copy(
            src_ref=ref, dst_ref=ref,
            send_sem=ysend.at[direction, k, ch], recv_sem=yrecv.at[direction, k, ch],
            device_id={"groups": other_slab}, device_id_type=MESH,
        )

    def halo_copy():
        return pltpu.make_async_remote_copy(
            src_ref=x_hbm.at[:, pl.ds(tok - HALO, HALO), :], dst_ref=halo,
            send_sem=halo_sem.at[0], recv_sem=halo_sem.at[1],
            device_id={"seq": seq + 1}, device_id_type=MESH,
        )

    @pl.when(seq < count - 1)
    def _():
        halo_copy().start()

    for ch in range(chunks):
        for direction in (0, 1):
            @pl.when(can_send(direction))
            def _():
                z_copy(direction, 0, ch, own_piece(ch), seq).start()

    x_copy = pltpu.make_async_copy(x_hbm, xbuf, local_sem.at[0])
    x_copy.start()
    w_copy = pltpu.make_async_copy(w_hbm.at[:, 0], wbuf.at[seq], local_sem.at[1])
    w_copy.start()
    x_copy.wait()

    @pl.when(seq > 0)
    def _():
        halo_copy().wait_recv()

    @pl.when(seq == 0)
    def _():
        halo[...] = jnp.zeros_like(halo)

    def pump(k, ch):
        for direction in (0, 1):
            @pl.when(has(direction, k))
            def _():
                b = origin(direction, k)
                landed = block_piece(b, ch, z_span(slab))
                z_copy(direction, k, ch, landed, b).wait_recv()

                @pl.when(can_send(direction))
                def _():
                    z_copy(direction, k + 1, ch, landed, b).start()

                y_copy(direction, k, ch, slab).start()

    def conv_tile(t, carry):
        cols = pl.ds(pl.multiple_of(t * LANES, LANES), LANES)

        def short(s):
            x = xbuf[s, :, cols].astype(jnp.float32)
            ext[HALO:, :] = x
            ext[:HALO, :] = halo[s, :, cols].astype(jnp.float32)
            return (
                sw_ref[s, 0:1, cols] * x
                + sw_ref[s, 1:2, cols] * ext[HALO - 1 : tok + HALO - 1, :]
                + sw_ref[s, 2:3, cols] * ext[HALO - 2 : tok + HALO - 2, :]
            )

        q_buf[:, cols] = short(0)
        product = short(1)
        product = product * short(2)

        pick_wide = (
            iota((groups, WIDE), 0) == t * PER_TILE + iota((groups, WIDE), 1) // BLOCK
        ).astype(jnp.float32)
        pick = (
            iota((groups, LANES), 0) == t * PER_TILE + iota((groups, LANES), 1) // GROUP
        ).astype(jnp.float32)

        def spread(table, which):
            return jnp.dot(table, which, precision=HIGHEST, preferred_element_type=jnp.float32)

        rate, res = rate_ref[...], res_ref[...]
        rate_rep, res_rep = spread(rate, pick_wide), spread(res, pick_wide)
        rate_c, res_c = spread(rate, pick), spread(res, pick)
        diagonal = iota((modes, LANES), 0) == iota((modes, LANES), 1) % GROUP
        rate_row = jnp.sum(jnp.where(diagonal, rate_c, 0.0), axis=0, keepdims=True)
        res_row = jnp.sum(jnp.where(diagonal, res_c, 0.0), axis=0, keepdims=True)
        ahead = (iota((BLOCK, LANES), 0) + 1).astype(jnp.float32)
        read = (res_row * jnp.exp(-rate_row * ahead)).astype(jnp.bfloat16)

        lane = iota((modes, WIDE), 1) % BLOCK
        back = ((BLOCK - lane) % BLOCK).astype(jnp.float32)
        row = jnp.sum(res_rep * jnp.exp(-rate_rep * back), axis=0, keepdims=True)
        lower = iota((BLOCK, BLOCK), 1) <= iota((BLOCK, BLOCK), 0)
        for g in range(PER_TILE):
            part = slice(g * BLOCK, (g + 1) * BLOCK)
            wide = jnp.broadcast_to(row[:, part], (BLOCK, BLOCK))
            table = pltpu.roll(wide, 0, 1, stride=1, stride_axis=0)
            lhs[:BLOCK, part] = jnp.where(lower, table, 0.0).astype(jnp.bfloat16)
        lhs[BLOCK:, :] = jnp.exp(-rate_rep * (BLOCK - 1 - lane).astype(jnp.float32)).astype(
            jnp.bfloat16
        )

        decay = jnp.exp(-rate_c * BLOCK)
        state = jnp.zeros((modes, LANES), jnp.float32)
        for b in range(blocks):
            rows_b = slice(b * BLOCK, (b + 1) * BLOCK)
            p_b = product[rows_b]
            made = jnp.dot(
                lhs[...], masked_rows(p_b.astype(jnp.bfloat16)), preferred_element_type=jnp.float32
            )
            value = made[:BLOCK] + skip_ref[:, cols] * p_b
            if b > 0:
                value = value + jnp.dot(
                    read, masked_rows(state.astype(jnp.bfloat16)), preferred_element_type=jnp.float32
                )
            base[rows_b, cols] = value
            state = decay * state + made[BLOCK:]
        own_end[:, cols] = state
        rate_ch[:, cols] = rate_c
        readout[:, cols] = read
        return carry

    steps = [(k, ch) for k in range(count - 1) for ch in range(chunks)]
    total = len(steps)
    early = 1
    part = tiles // (early + 1)
    for e in range(early + 1):
        stop = tiles if e == early else (e + 1) * part
        lax.fori_loop(e * part, stop, conv_tile, 0)
        if e < early:
            pump(*steps[e])

    def end_copy(d):
        return pltpu.make_async_remote_copy(
            src_ref=own_end, dst_ref=ends.at[seq],
            send_sem=end_send.at[d], recv_sem=end_recv.at[seq],
            device_id={"seq": seq + d}, device_id_type=MESH,
        )

    def arrived_end(source):
        return pltpu.make_async_remote_copy(
            src_ref=own_end, dst_ref=ends.at[source],
            send_sem=end_send.at[0], recv_sem=end_recv.at[source],
            device_id={"seq": seq - 1}, device_id_type=MESH,
        )

    for d in range(1, count):
        @pl.when(seq + d < count)
        def _():
            end_copy(d).start()

    pump(*steps[early])
    prior[...] = jnp.zeros_like(prior)
    for source in range(count - 1):
        @pl.when(source < seq)
        def _():
            arrived_end(source).wait_recv()
            prior[...] = prior[...] * jnp.exp(-rate_ch[...] * tok) + ends[source]

    def gate_tile(t, carry):
        cols = pl.ds(pl.multiple_of(t * LANES, LANES), LANES)
        read = readout[:, cols]
        decay = jnp.exp(-rate_ch[:, cols] * BLOCK)
        state = prior[:, cols]
        for b in range(blocks):
            rows_b = slice(b * BLOCK, (b + 1) * BLOCK)
            across = jnp.dot(
                read, masked_rows(state.astype(jnp.bfloat16)), preferred_element_type=jnp.float32
            )
            gated[chan, rows_b, cols] = (
                q_buf[rows_b, cols] * (base[rows_b, cols] + across)
            ).astype(jnp.bfloat16)
            state = decay * state
        return carry

    share = chans // GATE_PARTS

    def gate_copy(d, i):
        part_ref = gated.at[chan, :, pl.ds(i * share, share)]
        return pltpu.make_async_remote_copy(
            src_ref=part_ref, dst_ref=part_ref,
            send_sem=gate_send.at[d, i], recv_sem=gate_recv.at[chan, i],
            device_id={"chan": lax.rem(chan + d, n_chan)}, device_id_type=MESH,
        )

    def arrived_gate(d, i):
        source = lax.rem(chan + d, n_chan)
        part_ref = gated.at[source, :, pl.ds(i * share, share)]
        return pltpu.make_async_remote_copy(
            src_ref=part_ref, dst_ref=part_ref,
            send_sem=gate_send.at[0, i], recv_sem=gate_recv.at[source, i],
            device_id={"chan": source}, device_id_type=MESH,
        )

    for i in range(GATE_PARTS):
        lax.fori_loop(i * tiles // GATE_PARTS, (i + 1) * tiles // GATE_PARTS, gate_tile, 0)
        for d in range(1, n_chan):
            gate_copy(d, i).start()

    middle = max(min(2, total), total * 2 // 3)
    for e in range(early + 1, middle):
        pump(*steps[e])
    acc[...] = jnp.zeros_like(acc)
    w_copy.wait()
    for d in range(1, n_chan):
        for i in range(GATE_PARTS):
            arrived_gate(d, i).wait_recv()

    streamed = chunks > 1
    col_tile = min(512, out_cols)

    def multiply(b, ch):
        c, r = split(ch)
        a = gated[c, :, pl.ds(pl.multiple_of(b * local_rows + r * rows, LANES), rows)]

        def column(n, carry):
            cols = pl.ds(pl.multiple_of(n * col_tile, col_tile), col_tile)
            w = wbuf[b, c, pl.ds(pl.multiple_of(r * rows, rows), rows), cols]
            acc[:, cols] += jnp.dot(a, w, preferred_element_type=jnp.float32)
            return carry

        lax.fori_loop(0, out_cols // col_tile, column, 0)

    def consume(k, ch):
        for direction in (0, 1):
            @pl.when(has(direction, k))
            def _():
                y_copy(direction, k, ch, other_slab).wait_recv()
                if streamed:
                    multiply(origin(direction, k), ch)

    left_over = total - middle
    own_per = -(-chunks // left_over)
    per = -(-total // left_over)

    def both(j, carry):
        pump(j // chunks, j % chunks)
        if streamed:
            for i in range(own_per):
                ch = (j - middle) * own_per + i

                @pl.when(ch < chunks)
                def _():
                    multiply(seq, ch)

        def late(i, inner):
            old = (j - middle) * per + i

            @pl.when(old < total)
            def _():
                consume(old // chunks, old % chunks)

            return inner

        lax.fori_loop(0, per, late, 0)
        return carry

    lax.fori_loop(middle, total, both, 0)

    if not streamed:
        def whole_column(n, carry):
            cols = pl.ds(pl.multiple_of(n * half, half), half)
            for c in range(n_chan):
                w = wbuf[:, c, :, cols].reshape(count * local_rows, half)
                acc[:, cols] += jnp.dot(gated[c], w, preferred_element_type=jnp.float32)
            return carry

        lax.fori_loop(0, slabs, whole_column, 0)

    quarter = tok // 4

    def rep_copy(i, side):
        return pltpu.make_async_remote_copy(
            src_ref=acc.at[
                pl.ds(i * quarter, quarter), pl.ds(pl.multiple_of(side * out_half, LANES), out_half)
            ],
            dst_ref=peer.at[pl.ds(i * quarter, quarter), :],
            send_sem=rep_send.at[i], recv_sem=rep_recv.at[i],
            device_id={"rep": other_rep}, device_id_type=MESH,
        )

    for i in range(4):
        rep_copy(i, other_rep).start()
    mine = pl.ds(pl.multiple_of(rep * out_half, LANES), out_half)
    for i in range(4):
        rep_copy(i, other_rep).wait_recv()
        rows_i = pl.ds(i * quarter, quarter)
        out_ref[rows_i, :] = (acc[rows_i, mine] + peer[rows_i, :]).astype(jnp.bfloat16)

    for i in range(4):
        rep_copy(i, other_rep).wait_send()
    for d in range(1, n_chan):
        for i in range(GATE_PARTS):
            gate_copy(d, i).wait_send()
    for d in range(1, count):
        @pl.when(seq + d < count)
        def _():
            end_copy(d).wait_send()

    @pl.when(seq < count - 1)
    def _():
        halo_copy().wait_send()

    for ch in range(chunks):
        for direction in (0, 1):
            @pl.when(can_send(direction))
            def _():
                z_copy(direction, 0, ch, own_piece(ch), seq).wait_send()

    def drain(j, carry):
        k, ch = j // chunks, j % chunks
        for direction in (0, 1):
            @pl.when(has(direction, k))
            def _():
                y_copy(direction, k, ch, slab).wait_send()

                @pl.when(can_send(direction))
                def _():
                    b = origin(direction, k)
                    z_copy(direction, k + 1, ch, block_piece(b, ch, z_span(slab)), b).wait_send()
        return carry

    lax.fori_loop(0, total, drain, 0)


def per_device(projected, short_weight, skip_gain, pole_rate, residue, out_weight):
    tok, _, chans = projected.shape
    modes, groups = pole_rate.shape
    n_chan, _, local_rows, out_cols = out_weight.shape
    count, slabs = lax.axis_size("seq"), lax.axis_size("groups")
    n_rep = lax.axis_size("rep")
    row_chunks = max(1, local_rows // 256)
    chunks = n_chan * row_chunks if local_rows % LANES == 0 else 1
    dims = (count, slabs, n_chan, n_rep, chunks, row_chunks)
    f32, bf16 = jnp.float32, jnp.bfloat16
    dma = pltpu.SemaphoreType.DMA
    anywhere = pl.BlockSpec(memory_space=pl.ANY)
    vmem = pl.BlockSpec(memory_space=pltpu.VMEM)
    return pl.pallas_call(
        functools.partial(kernel, dims),
        in_specs=[anywhere, vmem, vmem, vmem, vmem, anywhere],
        out_specs=vmem,
        out_shape=jax.ShapeDtypeStruct((tok, out_cols // n_rep), bf16),
        scratch_shapes=[
            pltpu.VMEM((3, tok, chans), bf16),
            pltpu.VMEM((3, HALO, chans), bf16),
            pltpu.VMEM((tok + HALO, LANES), f32),
            pltpu.VMEM((BLOCK + modes, WIDE), bf16),
            pltpu.VMEM((tok, chans), f32),
            pltpu.VMEM((tok, chans), f32),
            pltpu.VMEM((count, modes, chans), f32),
            pltpu.VMEM((modes, chans), f32),
            pltpu.VMEM((modes, chans), f32),
            pltpu.VMEM((modes, chans), f32),
            pltpu.VMEM((BLOCK, chans), bf16),
            pltpu.VMEM((n_chan, tok, chans), bf16),
            pltpu.VMEM((count, n_chan, local_rows, out_cols), bf16),
            pltpu.VMEM((tok, out_cols), f32),
            pltpu.VMEM((tok, out_cols // n_rep), f32),
            dma((2,)),
            dma((2,)),
            dma((count,)),
            dma((count,)),
            dma((n_chan, GATE_PARTS)),
            dma((n_chan, GATE_PARTS)),
            dma((2, count, chunks)),
            dma((2, count, chunks)),
            dma((2, count, chunks)),
            dma((2, count, chunks)),
            dma((4,)),
            dma((4,)),
        ],
        compiler_params=pltpu.CompilerParams(
            collective_id=0, has_side_effects=True, vmem_limit_bytes=60 * 1024 * 1024
        ),
        name="hyena",
    )(
        projected.transpose(1, 0, 2), short_weight, skip_gain[None], pole_rate, residue, out_weight
    )


PARTS = 4
FAR_AFTER = 7


def lag_table(rate_ref, res_ref, lag_rows):
    rate, res = rate_ref[...], res_ref[...]
    modes, groups = rate.shape
    back = ((BLOCK - iota((BLOCK, groups), 0)) % BLOCK).astype(jnp.float32)
    total = jnp.zeros((BLOCK, groups), jnp.float32)
    for n in range(modes):
        total = total + res[n : n + 1] * jnp.exp(-rate[n : n + 1] * back)
    lag_rows[...] = total.T


def by_channel(table, t):
    index = t * PER_TILE + iota(table.shape, 1) // GROUP
    return jnp.take_along_axis(table, index, axis=1)


def by_mode(spread):
    diagonal = iota(spread.shape, 0) == iota(spread.shape, 1) % GROUP
    return jnp.sum(jnp.where(diagonal, spread, 0.0), axis=0, keepdims=True)


def fill(ext, halo, xbuf, s, cols):
    ext[HALO:, :] = xbuf[s, :, cols].astype(jnp.float32)
    ext[:HALO, :] = halo[s, :, cols].astype(jnp.float32)


def short(ext, sw_ref, s, cols, b):
    start = HALO + b * BLOCK
    total = sw_ref[s, 0:1, cols] * ext[start : start + BLOCK, :]
    for j in (1, 2):
        total = total + sw_ref[s, j : j + 1, cols] * ext[start - j : start - j + BLOCK, :]
    return total


def intake_tile(t, xbuf, halo, sw_ref, rate_ref, ext, ext2, product, made, own_end):
    cols = pl.ds(pl.multiple_of(t * LANES, LANES), LANES)
    blocks = xbuf.shape[1] // BLOCK
    fill(ext, halo, xbuf, 1, cols)
    fill(ext2, halo, xbuf, 2, cols)
    rate_c = by_channel(rate_ref[...], t)
    rate_row = by_mode(rate_c)
    behind = (BLOCK - 1 - iota((BLOCK, LANES), 0)).astype(jnp.float32)
    intake = jnp.exp(-rate_row * behind).T.astype(jnp.bfloat16)
    parts = []
    for b in range(blocks):
        p = short(ext, sw_ref, 1, cols, b) * short(ext2, sw_ref, 2, cols, b)
        product[b * BLOCK : (b + 1) * BLOCK, cols] = p
        parts.append(p.astype(jnp.bfloat16))
    every = jnp.dot(
        intake, jnp.concatenate(parts, axis=1), preferred_element_type=jnp.float32
    )
    decay = jnp.exp(-rate_c * BLOCK)
    lane_group = iota((GROUP, LANES), 1) // GROUP
    state = None
    for b in range(blocks):
        part = every[:, b * LANES : (b + 1) * LANES]
        own = jnp.zeros((GROUP, LANES), jnp.float32)
        for g in range(PER_TILE):
            own = jnp.where(lane_group == g, part[g * GROUP : (g + 1) * GROUP], own)
        if b < blocks - 1:
            made[b, :, cols] = own
        state = own if state is None else decay * state + own
    own_end[:, cols] = state


def gate_tile(t, xbuf, halo, sw_ref, skip_ref, rate_ref, res_ref, lag_rows, ext, product, made,
              prior, dst, dst_cols):
    cols = pl.ds(pl.multiple_of(t * LANES, LANES), LANES)
    blocks = xbuf.shape[1] // BLOCK
    fill(ext, halo, xbuf, 0, cols)
    rate_c = by_channel(rate_ref[...], t)
    rate_row, res_row = by_mode(rate_c), by_mode(by_channel(res_ref[...], t))
    ahead = (iota((BLOCK, LANES), 0) + 1).astype(jnp.float32)
    read = (res_row * jnp.exp(-rate_row * ahead)).astype(jnp.bfloat16)
    lower = iota((BLOCK, BLOCK), 1) <= iota((BLOCK, BLOCK), 0)
    rows = lag_rows[pl.ds(pl.multiple_of(t * PER_TILE, PER_TILE), PER_TILE), :]
    tables = []
    for g in range(PER_TILE):
        wide = jnp.broadcast_to(rows[g : g + 1], (BLOCK, BLOCK))
        table = pltpu.roll(wide, 0, 1, stride=1, stride_axis=0)
        tables.append(jnp.where(lower, table, 0.0).astype(jnp.bfloat16))
    lhs = jnp.concatenate(tables + [read], axis=1)
    decay = jnp.exp(-rate_c * BLOCK)
    state = prior[:, cols]
    for pair in range(0, blocks, 2):
        sides = []
        for b in range(pair, pair + 2):
            p = product[b * BLOCK : (b + 1) * BLOCK, cols].astype(jnp.bfloat16)
            sides.append(
                jnp.concatenate([masked_rows(p), masked_rows(state.astype(jnp.bfloat16))], axis=0)
            )
            if b < blocks - 1:
                state = decay * state + made[b, :, cols]
        value = jnp.dot(lhs, jnp.concatenate(sides, axis=1), preferred_element_type=jnp.float32)
        for b in range(pair, pair + 2):
            rows_b = slice(b * BLOCK, (b + 1) * BLOCK)
            v = value[:, (b - pair) * LANES : (b - pair + 1) * LANES]
            v = v + skip_ref[:, cols] * product[rows_b, cols]
            dst[rows_b, dst_cols] = (short(ext, sw_ref, 0, cols, b) * v).astype(jnp.bfloat16)


def half_kernel(x_hbm, sw_ref, skip_ref, rate_ref, res_ref, w_hbm, out_ref,
                xbuf, halo, ext, ext2, product, made, own_end, ends, prior, lag_rows,
                away, held, wbuf, mine, theirs, peer, outgoing, incoming,
                local_sem, halo_sem, end_send, end_recv, wz_send, wz_recv, wy_send, wy_recv,
                own_send, own_recv, z_send, z_recv, x_send, x_recv,
                core_send, core_recv, back_send, back_recv):
    count = 4
    tok, chans = product.shape
    half = chans // 2
    local_rows, out_cols = w_hbm.shape[2], w_hbm.shape[3]
    out_half = out_cols // 2
    wide = out_half // PARTS
    share = half // PARTS
    tiles = half // LANES
    slab = lax.axis_index("groups")
    seq = lax.axis_index("seq")
    chan = lax.axis_index("chan")
    rep = lax.axis_index("rep")
    side = seq // 2
    mate = seq + 1 - 2 * (seq % 2)
    worker = 2 - side
    is_worker = jnp.logical_or(seq == 1, seq == 2)
    is_far = jnp.logical_or(seq == 0, seq == 3)
    sources = (3 - seq, 6 - 3 * seq)
    near_slot = jnp.where(is_worker, 0, 1)

    barrier = pltpu.get_barrier_semaphore()

    def greet(target):
        pl.semaphore_signal(barrier, inc=1, device_id=target, device_id_type=MESH)

    for d in range(1, count):
        greet({"seq": lax.rem(seq + d, count)})
    greet({"chan": 1 - chan})
    greet({"groups": 1 - slab})
    greet({"rep": 1 - rep})
    pl.semaphore_wait(barrier, count + 2)

    def span(start, size):
        return pl.ds(pl.multiple_of(start, LANES), size)

    def remote(src, dst, send, recv, target):
        return pltpu.make_async_remote_copy(
            src_ref=src, dst_ref=dst, send_sem=send, recv_sem=recv,
            device_id=target, device_id_type=MESH,
        )

    def halo_copy():
        return remote(
            x_hbm.at[:, pl.ds(tok - HALO, HALO), :], halo, halo_sem.at[0], halo_sem.at[1],
            {"seq": seq + 1},
        )

    def w_cols(h, j):
        return span(h * out_half + j * wide, wide)

    def w_rows(owner):
        return span((owner % 2) * local_rows, local_rows)

    weight_parts = [(j, c) for j in range(PARTS) for c in range(2)]

    def wz_copy(i):
        j, c = weight_parts[i]
        return remote(
            w_hbm.at[c, 0, :, w_cols(slab, j)], wbuf.at[c, w_rows(seq), w_cols(slab, j)],
            wz_send.at[i], wz_recv.at[i], {"seq": mate},
        )

    def wz_arrived(i):
        j, c = weight_parts[i]
        ref = wbuf.at[c, w_rows(mate), w_cols(slab, j)]
        return remote(ref, ref, wz_send.at[i], wz_recv.at[i], {"seq": mate})

    def wy_copy(i, h):
        j, c = weight_parts[i]
        ref = wbuf.at[c, w_rows(mate), w_cols(h, j)]
        return remote(ref, ref, wy_send.at[i], wy_recv.at[i], {"groups": 1 - slab})

    def pass_weight(i):
        wz_arrived(i).wait_recv()
        wy_copy(i, slab).start()

    @pl.when(seq < count - 1)
    def _():
        halo_copy().start()

    def x_copy(h):
        cols = span(h * half, half)
        return pltpu.make_async_copy(x_hbm.at[:, :, cols], xbuf.at[:, :, cols], local_sem.at[h])

    first = 1 - seq % 2
    x_copy(first).start()
    x_copy(1 - first).start()
    for i in range(len(weight_parts)):
        wz_copy(i).start()
    w_copy = pltpu.make_async_copy(
        w_hbm.at[:, 0], wbuf.at[:, w_rows(seq), :], local_sem.at[2]
    )
    w_copy.start()
    lag_table(rate_ref, res_ref, lag_rows)

    @pl.when(seq > 0)
    def _():
        remote(halo, halo, halo_sem.at[0], halo_sem.at[1], {"seq": seq - 1}).wait_recv()

    @pl.when(seq == 0)
    def _():
        halo[...] = jnp.zeros_like(halo)

    def end_copy(d, h):
        cols = span(h * half, half)
        return remote(
            own_end.at[:, cols], ends.at[seq, :, cols], end_send.at[d, h], end_recv.at[seq, h],
            {"seq": seq + d},
        )

    def end_arrived(source, h):
        ref = ends.at[source, :, span(h * half, half)]
        return remote(ref, ref, end_send.at[0, h], end_recv.at[source, h], {"seq": seq - 1})

    for h in (first, 1 - first):
        x_copy(h).wait()

        def intake(t, carry):
            intake_tile(
                h * tiles + t, xbuf, halo, sw_ref, rate_ref, ext, ext2, product, made, own_end
            )
            return carry

        lax.fori_loop(0, tiles, intake, 0)
        for d in range(1, count):
            @pl.when(seq + d < count)
            def _():
                end_copy(d, h).start()

    pass_weight(0)

    def z_copy(i):
        cols = pl.ds(i * share, share)
        return remote(
            away.at[:, cols], held.at[near_slot, 0, :, cols], z_send.at[i],
            z_recv.at[near_slot, i], {"seq": worker},
        )

    def z_arrived(slot, i):
        ref = held.at[slot, 0, :, pl.ds(i * share, share)]
        return remote(ref, ref, z_send.at[i], z_recv.at[slot, i], {"seq": sources[slot]})

    def own_copy(i):
        cols = pl.ds(i * share, share)
        return remote(
            held.at[2, 0, :, cols], held.at[2, 1, :, cols], own_send.at[i], own_recv.at[i],
            {"chan": 1 - chan},
        )

    def across_copy(slot, i):
        cols = pl.ds(i * share, share)
        return remote(
            held.at[slot, 0, :, cols], held.at[slot, 1, :, cols], x_send.at[slot, i],
            x_recv.at[slot, i], {"chan": 1 - chan},
        )

    def set_prior(h):
        cols = span(h * half, half)
        rate_c = jnp.concatenate(
            [by_channel(rate_ref[...], h * tiles + t) for t in range(tiles)], axis=1
        )
        decay = jnp.exp(-rate_c * tok)
        prior[:, cols] = jnp.zeros((prior.shape[0], half), jnp.float32)
        for source in range(count - 1):
            @pl.when(source < seq)
            def _():
                end_arrived(source, h).wait_recv()
                prior[:, cols] = prior[:, cols] * decay + ends[source, :, cols]

    def gate(h, i, dst):
        def one(t, carry):
            gate_tile(
                h * tiles + t, xbuf, halo, sw_ref, skip_ref, rate_ref, res_ref, lag_rows, ext,
                product, made, prior, dst, span(t * LANES, LANES),
            )
            return carry

        lax.fori_loop(i * tiles // PARTS, (i + 1) * tiles // PARTS, one, 0)

    set_prior(1 - side)
    for i in range(PARTS):
        gate(1 - side, i, away)

        @pl.when(is_worker)
        def _():
            z_copy(i).start()

    pass_weight(1)
    set_prior(side)
    for i in range(PARTS):
        gate(side, i, held.at[2, 0])
        own_copy(i).start()

    def pass_gated(slot, i):
        z_arrived(slot, i).wait_recv()
        across_copy(slot, i).start()

    def core_copy(slot, j):
        return remote(
            theirs.at[slot, :, pl.ds(j * wide, wide)], peer.at[slot, :, pl.ds(j * wide, wide)],
            core_send.at[slot, j], core_recv.at[slot, j], {"rep": 1 - rep},
        )

    def multiply(slot, j):
        cols = pl.ds(j * wide, wide)

        def one(h):
            w_at = w_cols(h, j)
            total = jnp.dot(
                held[slot, 0], wbuf[chan, :, w_at], preferred_element_type=jnp.float32
            )
            return total + jnp.dot(
                held[slot, 1], wbuf[1 - chan, :, w_at], preferred_element_type=jnp.float32
            )

        theirs[slot, :, cols] = one(1 - rep)
        core_copy(slot, j).start()
        mine[slot, :, cols] = one(rep)

    def back_copy(slot, j):
        cols = pl.ds(j * wide, wide)
        return remote(
            outgoing.at[slot, :, cols], incoming.at[:, cols], back_send.at[slot, j],
            back_recv.at[j], {"seq": sources[slot]},
        )

    def back_arrived(j):
        ref = incoming.at[:, pl.ds(j * wide, wide)]
        return remote(ref, ref, back_send.at[0, j], back_recv.at[j], {"seq": worker})

    def finish(slot, j):
        cols = pl.ds(j * wide, wide)
        core_copy(slot, j).wait_recv()
        total = mine[slot, :, cols] + peer[slot, :, cols]
        if slot == 2:
            mine[slot, :, cols] = total
        else:
            outgoing[slot, :, cols] = total.astype(jnp.bfloat16)
            back_copy(slot, j).start()

    def weight_ready(j):
        for i, (part, _) in enumerate(weight_parts):
            if part == j:
                wy_copy(i, 1 - slab).wait_recv()

    def on(condition, steps):
        @pl.when(condition)
        def _():
            for step, *args in steps:
                step(*args)

    def gated_ready(slot):
        for i in range(PARTS):
            across_copy(slot, i).wait_recv()

    def own_ready():
        for i in range(PARTS):
            own_copy(i).wait_recv()

    def start_far():
        for i in range(PARTS):
            z_copy(i).start()

    own_steps = [(multiply, 2, 0)]
    for j in range(1, PARTS):
        own_steps += [(multiply, 2, j), (finish, 2, j - 1)]
    own_steps += [(finish, 2, PARTS - 1)]

    last = len(weight_parts)
    far = [(pass_weight, i) for i in range(2, FAR_AFTER)] + [(start_far,)]
    far += [(pass_weight, i) for i in range(FAR_AFTER, last)]
    far += [(weight_ready, j) for j in range(PARTS)]
    far += [(w_copy.wait,), (own_ready,)] + own_steps
    on(is_far, far)

    near = [
        (pass_weight, 2), (pass_gated, 0, 0), (pass_weight, 3), (pass_gated, 0, 1),
        (pass_weight, 4), (pass_gated, 0, 2), (pass_weight, 5), (pass_gated, 0, 3),
        (w_copy.wait,), (gated_ready, 0), (weight_ready, 0), (multiply, 0, 0),
        (weight_ready, 1), (finish, 0, 0), (multiply, 0, 1), (pass_weight, 6), (finish, 0, 1),
        (weight_ready, 2), (multiply, 0, 2), (pass_weight, 7), (finish, 0, 2),
        (own_ready,), (multiply, 2, 0), (multiply, 2, 1), (finish, 2, 0), (finish, 2, 1),
        (weight_ready, 3), (multiply, 0, 3), (finish, 0, 3),
        (multiply, 2, 2), (pass_gated, 1, 0), (multiply, 2, 3), (finish, 2, 2),
        (pass_gated, 1, 1), (finish, 2, 3), (pass_gated, 1, 2), (pass_gated, 1, 3),
        (gated_ready, 1), (multiply, 1, 0),
    ]
    for j in range(1, PARTS):
        near += [(multiply, 1, j), (finish, 1, j - 1)]
    near += [(finish, 1, PARTS - 1)]
    on(is_worker, near)

    for j in range(PARTS):
        cols = pl.ds(j * wide, wide)
        back_arrived(j).wait_recv()
        out_ref[:, cols] = (mine[2, :, cols] + incoming[:, cols].astype(jnp.float32)).astype(
            jnp.bfloat16
        )

    @pl.when(seq < count - 1)
    def _():
        halo_copy().wait_send()

    for d in range(1, count):
        @pl.when(seq + d < count)
        def _():
            for h in range(2):
                end_copy(d, h).wait_send()

    for i in range(last):
        wz_copy(i).wait_send()
        wy_copy(i, slab).wait_send()
    for i in range(PARTS):
        own_copy(i).wait_send()
        z_copy(i).wait_send()
        core_copy(2, i).wait_send()

    @pl.when(is_worker)
    def _():
        for slot in range(2):
            for i in range(PARTS):
                across_copy(slot, i).wait_send()
                core_copy(slot, i).wait_send()
                back_copy(slot, i).wait_send()


def by_halves(projected, short_weight, skip_gain, pole_rate, residue, out_weight):
    tok, _, chans = projected.shape
    modes, groups = pole_rate.shape
    local_rows, out_cols = out_weight.shape[2], out_weight.shape[3]
    count, half, out_half = 4, chans // 2, out_cols // 2
    blocks = tok // BLOCK
    f32, bf16 = jnp.float32, jnp.bfloat16
    dma = pltpu.SemaphoreType.DMA
    anywhere = pl.BlockSpec(memory_space=pl.ANY)
    vmem = pl.BlockSpec(memory_space=pltpu.VMEM)
    return pl.pallas_call(
        half_kernel,
        in_specs=[anywhere, vmem, vmem, vmem, vmem, anywhere],
        out_specs=vmem,
        out_shape=jax.ShapeDtypeStruct((tok, out_half), bf16),
        scratch_shapes=[
            pltpu.VMEM((3, tok, chans), bf16),
            pltpu.VMEM((3, HALO, chans), bf16),
            pltpu.VMEM((tok + HALO, LANES), f32),
            pltpu.VMEM((tok + HALO, LANES), f32),
            pltpu.VMEM((tok, chans), f32),
            pltpu.VMEM((blocks, modes, chans), f32),
            pltpu.VMEM((modes, chans), f32),
            pltpu.VMEM((count, modes, chans), f32),
            pltpu.VMEM((modes, chans), f32),
            pltpu.VMEM((groups, BLOCK), f32),
            pltpu.VMEM((tok, half), bf16),
            pltpu.VMEM((3, 2, tok, half), bf16),
            pltpu.VMEM((2, half, out_cols), bf16),
            pltpu.VMEM((3, tok, out_half), f32),
            pltpu.VMEM((3, tok, out_half), f32),
            pltpu.VMEM((3, tok, out_half), f32),
            pltpu.VMEM((2, tok, out_half), bf16),
            pltpu.VMEM((tok, out_half), bf16),
            dma((3,)),
            dma((2,)),
            dma((count, 2)),
            dma((count, 2)),
            dma((2 * PARTS,)),
            dma((2 * PARTS,)),
            dma((2 * PARTS,)),
            dma((2 * PARTS,)),
            dma((PARTS,)),
            dma((PARTS,)),
            dma((PARTS,)),
            dma((2, PARTS)),
            dma((2, PARTS)),
            dma((2, PARTS)),
            dma((3, PARTS)),
            dma((3, PARTS)),
            dma((2, PARTS)),
            dma((PARTS,)),
        ],
        compiler_params=pltpu.CompilerParams(
            collective_id=0, has_side_effects=True, vmem_limit_bytes=60 * 1024 * 1024
        ),
        name="hyena_halves",
    )(
        projected.transpose(1, 0, 2), short_weight, skip_gain[None], pole_rate, residue, out_weight
    )


def solution(mesh):
    sizes = tuple(mesh.shape[name] for name in ("groups", "seq", "chan", "rep"))
    return jax.shard_map(
        by_halves if sizes == (2, 4, 2, 2) else per_device,
        mesh=mesh,
        in_specs=(
            P(("groups", "seq"), None, ("chan", "rep")),
            P(None, None, ("chan", "rep")),
            P(("chan", "rep")),
            P(None, ("chan", "rep")),
            P(None, ("chan", "rep")),
            P(None, "rep", "seq", "chan"),
        ),
        out_specs=P(("groups", "seq"), ("chan", "rep")),
        check_vma=False,
    )
```

```python
import functools

import jax
import jax.numpy as jnp
from jax import lax
from jax.experimental import pallas as pl
from jax.experimental.pallas import tpu as pltpu
from jax.sharding import PartitionSpec as P

GROUP = 16
LANES = 128
BLOCK = 128
PER_TILE = LANES // GROUP
WIDE = PER_TILE * BLOCK
HALO = 16
Y_SHARE = 7
GATE_PARTS = 4
MESH = pl.DeviceIdType.MESH
HIGHEST = lax.Precision.HIGHEST


def iota(shape, dim):
    return lax.broadcasted_iota(jnp.int32, shape, dim)


def masked_rows(rows):
    lane_group = iota(rows.shape, 1) // GROUP
    zero = jnp.zeros_like(rows)
    return jnp.concatenate(
        [jnp.where(lane_group == g, rows, zero) for g in range(PER_TILE)], axis=0
    )


def kernel(dims, x_hbm, sw_ref, skip_ref, rate_ref, res_ref, w_hbm, out_ref,
           xbuf, halo, ext, lhs, q_buf, base, ends, own_end, prior, rate_ch, readout, gated, wbuf,
           acc, peer, local_sem, halo_sem, end_send, end_recv, gate_send, gate_recv,
           zsend, zrecv, ysend, yrecv, rep_send, rep_recv):
    count, slabs, n_chan, n_rep, chunks, row_chunks = dims
    tok, chans = gated.shape[1], gated.shape[2]
    modes, groups = rate_ref.shape
    tiles = chans // LANES
    blocks = tok // BLOCK
    local_rows, out_cols = w_hbm.shape[2], w_hbm.shape[3]
    half = out_cols // slabs
    y_cols = out_cols // LANES * Y_SHARE // 16 * LANES
    z_cols = out_cols - y_cols
    rows = local_rows // row_chunks
    out_half = out_cols // n_rep
    slab = lax.axis_index("groups")
    seq = lax.axis_index("seq")
    chan = lax.axis_index("chan")
    rep = lax.axis_index("rep")
    other_slab = 1 - slab
    other_rep = 1 - rep

    barrier = pltpu.get_barrier_semaphore()

    def greet(target):
        pl.semaphore_signal(barrier, inc=1, device_id=target, device_id_type=MESH)

    for d in range(1, count):
        greet({"seq": lax.rem(seq + d, count)})
    for d in range(1, n_chan):
        greet({"chan": lax.rem(chan + d, n_chan)})
    greet({"groups": other_slab})
    greet({"rep": other_rep})
    pl.semaphore_wait(barrier, count + n_chan)

    def z_span(h):
        return pl.ds(pl.multiple_of(h * y_cols, LANES), z_cols)

    def y_span(h):
        return pl.ds(pl.multiple_of(h * z_cols, LANES), y_cols)

    def piece(ref, c, r, cols):
        if chunks == 1:
            return ref.at[:, :, cols]
        return ref.at[c, pl.ds(pl.multiple_of(r * rows, rows), rows), cols]

    def split(ch):
        return ch // row_chunks, ch % row_chunks

    def own_piece(ch):
        c, r = split(ch)
        return piece(w_hbm.at[:, 0], c, r, z_span(slab))

    def block_piece(b, ch, cols):
        c, r = split(ch)
        return piece(wbuf.at[b], c, r, cols)

    def target_of(direction):
        return seq + 1 if direction == 0 else seq - 1

    def can_send(direction):
        return seq < count - 1 if direction == 0 else seq > 0

    def origin(direction, k):
        return seq - 1 - k if direction == 0 else seq + 1 + k

    def has(direction, k):
        return seq - 1 - k >= 0 if direction == 0 else seq + 1 + k < count

    def z_copy(direction, k, ch, src, b):
        return pltpu.make_async_remote_copy(
            src_ref=src, dst_ref=block_piece(b, ch, z_span(slab)),
            send_sem=zsend.at[direction, k, ch], recv_sem=zrecv.at[direction, k, ch],
            device_id={"seq": target_of(direction)}, device_id_type=MESH,
        )

    def y_copy(direction, k, ch, h):
        b = origin(direction, k)
        ref = block_piece(b, ch, y_span(h))
        return pltpu.make_async_remote_copy(
            src_ref=ref, dst_ref=ref,
            send_sem=ysend.at[direction, k, ch], recv_sem=yrecv.at[direction, k, ch],
            device_id={"groups": other_slab}, device_id_type=MESH,
        )

    def halo_copy():
        return pltpu.make_async_remote_copy(
            src_ref=x_hbm.at[:, pl.ds(tok - HALO, HALO), :], dst_ref=halo,
            send_sem=halo_sem.at[0], recv_sem=halo_sem.at[1],
            device_id={"seq": seq + 1}, device_id_type=MESH,
        )

    @pl.when(seq < count - 1)
    def _():
        halo_copy().start()

    for ch in range(chunks):
        for direction in (0, 1):
            @pl.when(can_send(direction))
            def _():
                z_copy(direction, 0, ch, own_piece(ch), seq).start()

    x_copy = pltpu.make_async_copy(x_hbm, xbuf, local_sem.at[0])
    x_copy.start()
    w_copy = pltpu.make_async_copy(w_hbm.at[:, 0], wbuf.at[seq], local_sem.at[1])
    w_copy.start()
    x_copy.wait()

    @pl.when(seq > 0)
    def _():
        halo_copy().wait_recv()

    @pl.when(seq == 0)
    def _():
        halo[...] = jnp.zeros_like(halo)

    def pump(k, ch):
        for direction in (0, 1):
            @pl.when(has(direction, k))
            def _():
                b = origin(direction, k)
                landed = block_piece(b, ch, z_span(slab))
                z_copy(direction, k, ch, landed, b).wait_recv()

                @pl.when(can_send(direction))
                def _():
                    z_copy(direction, k + 1, ch, landed, b).start()

                y_copy(direction, k, ch, slab).start()

    def conv_tile(t, carry):
        cols = pl.ds(pl.multiple_of(t * LANES, LANES), LANES)

        def short(s):
            x = xbuf[s, :, cols].astype(jnp.float32)
            ext[HALO:, :] = x
            ext[:HALO, :] = halo[s, :, cols].astype(jnp.float32)
            return (
                sw_ref[s, 0:1, cols] * x
                + sw_ref[s, 1:2, cols] * ext[HALO - 1 : tok + HALO - 1, :]
                + sw_ref[s, 2:3, cols] * ext[HALO - 2 : tok + HALO - 2, :]
            )

        q_buf[:, cols] = short(0)
        product = short(1)
        product = product * short(2)

        pick_wide = (
            iota((groups, WIDE), 0) == t * PER_TILE + iota((groups, WIDE), 1) // BLOCK
        ).astype(jnp.float32)
        pick = (
            iota((groups, LANES), 0) == t * PER_TILE + iota((groups, LANES), 1) // GROUP
        ).astype(jnp.float32)

        def spread(table, which):
            return jnp.dot(table, which, precision=HIGHEST, preferred_element_type=jnp.float32)

        rate, res = rate_ref[...], res_ref[...]
        rate_rep, res_rep = spread(rate, pick_wide), spread(res, pick_wide)
        rate_c, res_c = spread(rate, pick), spread(res, pick)
        diagonal = iota((modes, LANES), 0) == iota((modes, LANES), 1) % GROUP
        rate_row = jnp.sum(jnp.where(diagonal, rate_c, 0.0), axis=0, keepdims=True)
        res_row = jnp.sum(jnp.where(diagonal, res_c, 0.0), axis=0, keepdims=True)
        ahead = (iota((BLOCK, LANES), 0) + 1).astype(jnp.float32)
        read = (res_row * jnp.exp(-rate_row * ahead)).astype(jnp.bfloat16)

        lane = iota((modes, WIDE), 1) % BLOCK
        back = ((BLOCK - lane) % BLOCK).astype(jnp.float32)
        row = jnp.sum(res_rep * jnp.exp(-rate_rep * back), axis=0, keepdims=True)
        lower = iota((BLOCK, BLOCK), 1) <= iota((BLOCK, BLOCK), 0)
        for g in range(PER_TILE):
            part = slice(g * BLOCK, (g + 1) * BLOCK)
            wide = jnp.broadcast_to(row[:, part], (BLOCK, BLOCK))
            table = pltpu.roll(wide, 0, 1, stride=1, stride_axis=0)
            lhs[:BLOCK, part] = jnp.where(lower, table, 0.0).astype(jnp.bfloat16)
        lhs[BLOCK:, :] = jnp.exp(-rate_rep * (BLOCK - 1 - lane).astype(jnp.float32)).astype(
            jnp.bfloat16
        )

        decay = jnp.exp(-rate_c * BLOCK)
        state = jnp.zeros((modes, LANES), jnp.float32)
        for b in range(blocks):
            rows_b = slice(b * BLOCK, (b + 1) * BLOCK)
            p_b = product[rows_b]
            made = jnp.dot(
                lhs[...], masked_rows(p_b.astype(jnp.bfloat16)), preferred_element_type=jnp.float32
            )
            value = made[:BLOCK] + skip_ref[:, cols] * p_b
            if b > 0:
                value = value + jnp.dot(
                    read, masked_rows(state.astype(jnp.bfloat16)), preferred_element_type=jnp.float32
                )
            base[rows_b, cols] = value
            state = decay * state + made[BLOCK:]
        own_end[:, cols] = state
        rate_ch[:, cols] = rate_c
        readout[:, cols] = read
        return carry

    steps = [(k, ch) for k in range(count - 1) for ch in range(chunks)]
    total = len(steps)
    early = 1
    part = tiles // (early + 1)
    for e in range(early + 1):
        stop = tiles if e == early else (e + 1) * part
        lax.fori_loop(e * part, stop, conv_tile, 0)
        if e < early:
            pump(*steps[e])

    def end_copy(d):
        return pltpu.make_async_remote_copy(
            src_ref=own_end, dst_ref=ends.at[seq],
            send_sem=end_send.at[d], recv_sem=end_recv.at[seq],
            device_id={"seq": seq + d}, device_id_type=MESH,
        )

    def arrived_end(source):
        return pltpu.make_async_remote_copy(
            src_ref=own_end, dst_ref=ends.at[source],
            send_sem=end_send.at[0], recv_sem=end_recv.at[source],
            device_id={"seq": seq - 1}, device_id_type=MESH,
        )

    for d in range(1, count):
        @pl.when(seq + d < count)
        def _():
            end_copy(d).start()

    pump(*steps[early])
    prior[...] = jnp.zeros_like(prior)
    for source in range(count - 1):
        @pl.when(source < seq)
        def _():
            arrived_end(source).wait_recv()
            prior[...] = prior[...] * jnp.exp(-rate_ch[...] * tok) + ends[source]

    def gate_tile(t, carry):
        cols = pl.ds(pl.multiple_of(t * LANES, LANES), LANES)
        read = readout[:, cols]
        decay = jnp.exp(-rate_ch[:, cols] * BLOCK)
        state = prior[:, cols]
        for b in range(blocks):
            rows_b = slice(b * BLOCK, (b + 1) * BLOCK)
            across = jnp.dot(
                read, masked_rows(state.astype(jnp.bfloat16)), preferred_element_type=jnp.float32
            )
            gated[chan, rows_b, cols] = (
                q_buf[rows_b, cols] * (base[rows_b, cols] + across)
            ).astype(jnp.bfloat16)
            state = decay * state
        return carry

    share = chans // GATE_PARTS

    def gate_copy(d, i):
        part_ref = gated.at[chan, :, pl.ds(i * share, share)]
        return pltpu.make_async_remote_copy(
            src_ref=part_ref, dst_ref=part_ref,
            send_sem=gate_send.at[d, i], recv_sem=gate_recv.at[chan, i],
            device_id={"chan": lax.rem(chan + d, n_chan)}, device_id_type=MESH,
        )

    def arrived_gate(d, i):
        source = lax.rem(chan + d, n_chan)
        part_ref = gated.at[source, :, pl.ds(i * share, share)]
        return pltpu.make_async_remote_copy(
            src_ref=part_ref, dst_ref=part_ref,
            send_sem=gate_send.at[0, i], recv_sem=gate_recv.at[source, i],
            device_id={"chan": source}, device_id_type=MESH,
        )

    for i in range(GATE_PARTS):
        lax.fori_loop(i * tiles // GATE_PARTS, (i + 1) * tiles // GATE_PARTS, gate_tile, 0)
        for d in range(1, n_chan):
            gate_copy(d, i).start()

    middle = max(min(2, total), total * 2 // 3)
    for e in range(early + 1, middle):
        pump(*steps[e])
    acc[...] = jnp.zeros_like(acc)
    w_copy.wait()
    for d in range(1, n_chan):
        for i in range(GATE_PARTS):
            arrived_gate(d, i).wait_recv()

    streamed = chunks > 1
    col_tile = min(512, out_cols)

    def multiply(b, ch):
        c, r = split(ch)
        a = gated[c, :, pl.ds(pl.multiple_of(b * local_rows + r * rows, LANES), rows)]

        def column(n, carry):
            cols = pl.ds(pl.multiple_of(n * col_tile, col_tile), col_tile)
            w = wbuf[b, c, pl.ds(pl.multiple_of(r * rows, rows), rows), cols]
            acc[:, cols] += jnp.dot(a, w, preferred_element_type=jnp.float32)
            return carry

        lax.fori_loop(0, out_cols // col_tile, column, 0)

    def consume(k, ch):
        for direction in (0, 1):
            @pl.when(has(direction, k))
            def _():
                y_copy(direction, k, ch, other_slab).wait_recv()
                if streamed:
                    multiply(origin(direction, k), ch)

    left_over = total - middle
    own_per = -(-chunks // left_over)
    per = -(-total // left_over)

    def both(j, carry):
        pump(j // chunks, j % chunks)
        if streamed:
            for i in range(own_per):
                ch = (j - middle) * own_per + i

                @pl.when(ch < chunks)
                def _():
                    multiply(seq, ch)

        def late(i, inner):
            old = (j - middle) * per + i

            @pl.when(old < total)
            def _():
                consume(old // chunks, old % chunks)

            return inner

        lax.fori_loop(0, per, late, 0)
        return carry

    lax.fori_loop(middle, total, both, 0)

    if not streamed:
        def whole_column(n, carry):
            cols = pl.ds(pl.multiple_of(n * half, half), half)
            for c in range(n_chan):
                w = wbuf[:, c, :, cols].reshape(count * local_rows, half)
                acc[:, cols] += jnp.dot(gated[c], w, preferred_element_type=jnp.float32)
            return carry

        lax.fori_loop(0, slabs, whole_column, 0)

    quarter = tok // 4

    def rep_copy(i, side):
        return pltpu.make_async_remote_copy(
            src_ref=acc.at[
                pl.ds(i * quarter, quarter), pl.ds(pl.multiple_of(side * out_half, LANES), out_half)
            ],
            dst_ref=peer.at[pl.ds(i * quarter, quarter), :],
            send_sem=rep_send.at[i], recv_sem=rep_recv.at[i],
            device_id={"rep": other_rep}, device_id_type=MESH,
        )

    for i in range(4):
        rep_copy(i, other_rep).start()
    mine = pl.ds(pl.multiple_of(rep * out_half, LANES), out_half)
    for i in range(4):
        rep_copy(i, other_rep).wait_recv()
        rows_i = pl.ds(i * quarter, quarter)
        out_ref[rows_i, :] = (acc[rows_i, mine] + peer[rows_i, :]).astype(jnp.bfloat16)

    for i in range(4):
        rep_copy(i, other_rep).wait_send()
    for d in range(1, n_chan):
        for i in range(GATE_PARTS):
            gate_copy(d, i).wait_send()
    for d in range(1, count):
        @pl.when(seq + d < count)
        def _():
            end_copy(d).wait_send()

    @pl.when(seq < count - 1)
    def _():
        halo_copy().wait_send()

    for ch in range(chunks):
        for direction in (0, 1):
            @pl.when(can_send(direction))
            def _():
                z_copy(direction, 0, ch, own_piece(ch), seq).wait_send()

    def drain(j, carry):
        k, ch = j // chunks, j % chunks
        for direction in (0, 1):
            @pl.when(has(direction, k))
            def _():
                y_copy(direction, k, ch, slab).wait_send()

                @pl.when(can_send(direction))
                def _():
                    b = origin(direction, k)
                    z_copy(direction, k + 1, ch, block_piece(b, ch, z_span(slab)), b).wait_send()
        return carry

    lax.fori_loop(0, total, drain, 0)


def per_device(projected, short_weight, skip_gain, pole_rate, residue, out_weight):
    tok, _, chans = projected.shape
    modes, groups = pole_rate.shape
    n_chan, _, local_rows, out_cols = out_weight.shape
    count, slabs = lax.axis_size("seq"), lax.axis_size("groups")
    n_rep = lax.axis_size("rep")
    row_chunks = max(1, local_rows // 256)
    chunks = n_chan * row_chunks if local_rows % LANES == 0 else 1
    dims = (count, slabs, n_chan, n_rep, chunks, row_chunks)
    f32, bf16 = jnp.float32, jnp.bfloat16
    dma = pltpu.SemaphoreType.DMA
    anywhere = pl.BlockSpec(memory_space=pl.ANY)
    vmem = pl.BlockSpec(memory_space=pltpu.VMEM)
    return pl.pallas_call(
        functools.partial(kernel, dims),
        in_specs=[anywhere, vmem, vmem, vmem, vmem, anywhere],
        out_specs=vmem,
        out_shape=jax.ShapeDtypeStruct((tok, out_cols // n_rep), bf16),
        scratch_shapes=[
            pltpu.VMEM((3, tok, chans), bf16),
            pltpu.VMEM((3, HALO, chans), bf16),
            pltpu.VMEM((tok + HALO, LANES), f32),
            pltpu.VMEM((BLOCK + modes, WIDE), bf16),
            pltpu.VMEM((tok, chans), f32),
            pltpu.VMEM((tok, chans), f32),
            pltpu.VMEM((count, modes, chans), f32),
            pltpu.VMEM((modes, chans), f32),
            pltpu.VMEM((modes, chans), f32),
            pltpu.VMEM((modes, chans), f32),
            pltpu.VMEM((BLOCK, chans), bf16),
            pltpu.VMEM((n_chan, tok, chans), bf16),
            pltpu.VMEM((count, n_chan, local_rows, out_cols), bf16),
            pltpu.VMEM((tok, out_cols), f32),
            pltpu.VMEM((tok, out_cols // n_rep), f32),
            dma((2,)),
            dma((2,)),
            dma((count,)),
            dma((count,)),
            dma((n_chan, GATE_PARTS)),
            dma((n_chan, GATE_PARTS)),
            dma((2, count, chunks)),
            dma((2, count, chunks)),
            dma((2, count, chunks)),
            dma((2, count, chunks)),
            dma((4,)),
            dma((4,)),
        ],
        compiler_params=pltpu.CompilerParams(
            collective_id=0, has_side_effects=True, vmem_limit_bytes=60 * 1024 * 1024
        ),
        name="hyena",
    )(
        projected.transpose(1, 0, 2), short_weight, skip_gain[None], pole_rate, residue, out_weight
    )


PARTS = 4
LEAD = 8


def lag_table(rate_ref, res_ref, lag_rows):
    rate, res = rate_ref[...], res_ref[...]
    modes, groups = rate.shape
    back = ((BLOCK - iota((BLOCK, groups), 0)) % BLOCK).astype(jnp.float32)
    total = jnp.zeros((BLOCK, groups), jnp.float32)
    for n in range(modes):
        total = total + res[n : n + 1] * jnp.exp(-rate[n : n + 1] * back)
    lag_rows[...] = total.T


def by_channel(table, t):
    index = t * PER_TILE + iota(table.shape, 1) // GROUP
    return jnp.take_along_axis(table, index, axis=1)


def by_mode(spread):
    diagonal = iota(spread.shape, 0) == iota(spread.shape, 1) % GROUP
    return jnp.sum(jnp.where(diagonal, spread, 0.0), axis=0, keepdims=True)


def fill(ext, halo, xbuf, s, cols):
    ext[LEAD:, :] = xbuf[s, :, cols].astype(jnp.float32)
    ext[LEAD - 2 : LEAD, :] = halo[2 * s : 2 * s + 2, cols]


def short(ext, sw_ref, s, cols, b):
    start = LEAD + b * BLOCK
    total = sw_ref[s, 0:1, cols] * ext[start : start + BLOCK, :]
    for j in (1, 2):
        total = total + sw_ref[s, j : j + 1, cols] * ext[start - j : start - j + BLOCK, :]
    return total


def intake_tile(t, xbuf, halo, sw_ref, rate_ref, ext, ext2, product, made, own_end):
    cols = pl.ds(pl.multiple_of(t * LANES, LANES), LANES)
    blocks = xbuf.shape[1] // BLOCK
    fill(ext, halo, xbuf, 1, cols)
    fill(ext2, halo, xbuf, 2, cols)
    rate_c = by_channel(rate_ref[...], t)
    rate_row = by_mode(rate_c)
    behind = (BLOCK - 1 - iota((BLOCK, LANES), 0)).astype(jnp.float32)
    intake = jnp.exp(-rate_row * behind).T.astype(jnp.bfloat16)
    parts = []
    for b in range(blocks):
        p = short(ext, sw_ref, 1, cols, b) * short(ext2, sw_ref, 2, cols, b)
        product[b * BLOCK : (b + 1) * BLOCK, cols] = p
        parts.append(p.astype(jnp.bfloat16))
    every = jnp.dot(
        intake, jnp.concatenate(parts, axis=1), preferred_element_type=jnp.float32
    )
    decay = jnp.exp(-rate_c * BLOCK)
    lane_group = iota((GROUP, LANES), 1) // GROUP
    state = None
    for b in range(blocks):
        part = every[:, b * LANES : (b + 1) * LANES]
        own = jnp.zeros((GROUP, LANES), jnp.float32)
        for g in range(PER_TILE):
            own = jnp.where(lane_group == g, part[g * GROUP : (g + 1) * GROUP], own)
        if b < blocks - 1:
            made[b, :, cols] = own
        state = own if state is None else decay * state + own
    own_end[:, cols] = state


def table_tile(t, lag_rows, tables):
    lower = iota((BLOCK, BLOCK), 1) <= iota((BLOCK, BLOCK), 0)
    rows = lag_rows[pl.ds(pl.multiple_of(t * PER_TILE, PER_TILE), PER_TILE), :]
    for g in range(PER_TILE):
        wide = jnp.broadcast_to(rows[g : g + 1], (BLOCK, BLOCK))
        table = pltpu.roll(wide, 0, 1, stride=1, stride_axis=0)
        tables[t, :, g * BLOCK : (g + 1) * BLOCK] = jnp.where(lower, table, 0.0).astype(
            jnp.bfloat16
        )


def gate_tile(t, xbuf, halo, sw_ref, skip_ref, rate_ref, res_ref, tables, ext, product, made,
              prior, dst, dst_cols):
    cols = pl.ds(pl.multiple_of(t * LANES, LANES), LANES)
    blocks = xbuf.shape[1] // BLOCK
    fill(ext, halo, xbuf, 0, cols)
    rate_c = by_channel(rate_ref[...], t)
    rate_row, res_row = by_mode(rate_c), by_mode(by_channel(res_ref[...], t))
    ahead = (iota((BLOCK, LANES), 0) + 1).astype(jnp.float32)
    read = (res_row * jnp.exp(-rate_row * ahead)).astype(jnp.bfloat16)
    lhs = jnp.concatenate([tables[t], read], axis=1)
    decay = jnp.exp(-rate_c * BLOCK)
    state = prior[:, cols]
    for pair in range(0, blocks, 2):
        sides = []
        for b in range(pair, pair + 2):
            p = product[b * BLOCK : (b + 1) * BLOCK, cols].astype(jnp.bfloat16)
            sides.append(
                jnp.concatenate([masked_rows(p), masked_rows(state.astype(jnp.bfloat16))], axis=0)
            )
            if b < blocks - 1:
                state = decay * state + made[b, :, cols]
        value = jnp.dot(lhs, jnp.concatenate(sides, axis=1), preferred_element_type=jnp.float32)
        for b in range(pair, pair + 2):
            rows_b = slice(b * BLOCK, (b + 1) * BLOCK)
            v = value[:, (b - pair) * LANES : (b - pair + 1) * LANES]
            v = v + skip_ref[:, cols] * product[rows_b, cols]
            dst[rows_b, dst_cols] = (short(ext, sw_ref, 0, cols, b) * v).astype(jnp.bfloat16)


def half_kernel(x_hbm, sw_ref, skip_ref, rate_ref, res_ref, w_hbm, out_ref,
                xbuf, tail, halo_out, halo, ext, ext2, product, made, own_end, prior, lag_rows,
                tables, away, held, wbuf, mine, theirs, peer, outgoing, incoming,
                local_sem, halo_sem, end_send, end_recv, wz_send, wz_recv, wy_send, wy_recv,
                own_send, own_recv, z_send, z_recv, x_send, x_recv,
                core_send, core_recv, back_send, back_recv):
    count = 4
    tok, chans = product.shape
    half = chans // 2
    local_rows, out_cols = w_hbm.shape[2], w_hbm.shape[3]
    out_half = out_cols // 2
    wide = out_half // PARTS
    tiles = half // LANES
    slab = lax.axis_index("groups")
    seq = lax.axis_index("seq")
    chan = lax.axis_index("chan")
    rep = lax.axis_index("rep")
    side = seq // 2
    mate = seq + 1 - 2 * (seq % 2)
    worker = 2 - side
    is_worker = jnp.logical_or(seq == 1, seq == 2)
    is_far = jnp.logical_or(seq == 0, seq == 3)
    sources = (3 - seq, 6 - 3 * seq)
    to_slot = jnp.where(is_worker, 0, 1)

    barrier = pltpu.get_barrier_semaphore()

    def greet(target):
        pl.semaphore_signal(barrier, inc=1, device_id=target, device_id_type=MESH)

    def span(start, size):
        return pl.ds(pl.multiple_of(start, LANES), size)

    def remote(src, dst, send, recv, target):
        return pltpu.make_async_remote_copy(
            src_ref=src, dst_ref=dst, send_sem=send, recv_sem=recv,
            device_id=target, device_id_type=MESH,
        )

    def on(condition, steps):
        @pl.when(condition)
        def _():
            for step, *args in steps:
                step(*args)

    def x_copy(h):
        cols = span(h * half, half)
        return pltpu.make_async_copy(x_hbm.at[:, :, cols], xbuf.at[:, :, cols], local_sem.at[h])

    tail_copy = pltpu.make_async_copy(
        x_hbm.at[:, pl.ds(tok - HALO, HALO), :], tail, local_sem.at[3]
    )
    tail_copy.start()
    x_copy(0).start()
    x_copy(1).start()

    for d in range(1, count):
        greet({"seq": lax.rem(seq + d, count)})
    greet({"chan": 1 - chan})
    greet({"groups": 1 - slab})
    greet({"rep": 1 - rep})
    pl.semaphore_wait(barrier, count + 2)

    def w_cols(h, j):
        return span(h * out_half + j * wide, wide)

    def w_rows(owner):
        return span((owner % 2) * local_rows, local_rows)

    weight_parts = [(j, c) for j in range(PARTS) for c in range(2)]
    last = len(weight_parts)

    def wz_copy(i):
        j, c = weight_parts[i]
        return remote(
            w_hbm.at[c, 0, :, w_cols(slab, j)], wbuf.at[c, w_rows(seq), w_cols(slab, j)],
            wz_send.at[i], wz_recv.at[i], {"seq": mate},
        )

    def wz_arrived(i):
        j, c = weight_parts[i]
        ref = wbuf.at[c, w_rows(mate), w_cols(slab, j)]
        return remote(ref, ref, wz_send.at[i], wz_recv.at[i], {"seq": mate})

    def wy_copy(i, h):
        j, c = weight_parts[i]
        ref = wbuf.at[c, w_rows(mate), w_cols(h, j)]
        return remote(ref, ref, wy_send.at[i], wy_recv.at[i], {"groups": 1 - slab})

    def pass_weight(i):
        wz_arrived(i).wait_recv()
        wy_copy(i, slab).start()

    def send_weights(start, stop):
        for i in range(start, stop):
            wz_copy(i).start()

    def halo_copy():
        return remote(halo_out, halo, halo_sem.at[0], halo_sem.at[1], {"seq": seq + 1})

    tail_copy.wait()

    @pl.when(seq < count - 1)
    def _():
        halo_out[...] = jnp.zeros_like(halo_out)
        for s in range(3):
            halo_out[2 * s : 2 * s + 2, :] = tail[s].astype(jnp.float32)[HALO - 2 :]
        halo_copy().start()

    on(seq == 0, [(send_weights, 0, 1)])
    on(seq == 1, [(send_weights, 0, last)])
    on(seq == 2, [(send_weights, 0, 3)])
    on(seq == 3, [(send_weights, 0, 5)])
    w_copy = pltpu.make_async_copy(
        w_hbm.at[:, 0], wbuf.at[:, w_rows(seq), :], local_sem.at[2]
    )
    w_copy.start()

    def make_tables(h):
        def one(t, carry):
            table_tile(h * tiles + t, lag_rows, tables)
            return carry

        lax.fori_loop(0, tiles, one, 0)

    lag_table(rate_ref, res_ref, lag_rows)
    make_tables(0)

    @pl.when(seq > 0)
    def _():
        remote(halo, halo, halo_sem.at[0], halo_sem.at[1], {"seq": seq - 1}).wait_recv()

    @pl.when(seq == 0)
    def _():
        halo[...] = jnp.zeros_like(halo)
        prior[...] = jnp.zeros_like(prior)

    def end_copy(h):
        cols = span(h * half, half)
        return remote(
            own_end.at[:, cols], prior.at[:, cols], end_send.at[h], end_recv.at[h],
            {"seq": seq + 1},
        )

    for h in range(2):
        x_copy(h).wait()

        def intake(t, carry):
            intake_tile(
                h * tiles + t, xbuf, halo, sw_ref, rate_ref, ext, ext2, product, made, own_end
            )
            return carry

        lax.fori_loop(0, tiles, intake, 0)

        @pl.when(seq == 0)
        def _():
            end_copy(h).start()

    on(seq == 0, [(send_weights, 1, 5)])
    pass_weight(0)
    make_tables(1)

    def hand_on(h):
        cols = span(h * half, half)
        ref = prior.at[:, cols]

        @pl.when(seq > 0)
        def _():
            remote(ref, ref, end_send.at[h], end_recv.at[h], {"seq": seq - 1}).wait_recv()

        @pl.when(is_worker)
        def _():
            rate_c = jnp.concatenate(
                [by_channel(rate_ref[...], h * tiles + t) for t in range(tiles)], axis=1
            )
            own_end[:, cols] = own_end[:, cols] + prior[:, cols] * jnp.exp(-rate_c * tok)
            end_copy(h).start()

    def z_copy(i):
        cols = pl.ds(i * LANES, LANES)
        return remote(
            away.at[:, cols], held.at[to_slot, 0, :, cols], z_send.at[i],
            z_recv.at[to_slot, i], {"seq": worker},
        )

    def z_arrived(slot, i):
        ref = held.at[slot, 0, :, pl.ds(i * LANES, LANES)]
        return remote(ref, ref, z_send.at[i], z_recv.at[slot, i], {"seq": sources[slot]})

    def own_copy(i):
        cols = pl.ds(i * LANES, LANES)
        return remote(
            held.at[2, 0, :, cols], held.at[2, 1, :, cols], own_send.at[i], own_recv.at[i],
            {"chan": 1 - chan},
        )

    def across_copy(slot, i):
        cols = pl.ds(i * LANES, LANES)
        return remote(
            held.at[slot, 0, :, cols], held.at[slot, 1, :, cols], x_send.at[slot, i],
            x_recv.at[slot, i], {"chan": 1 - chan},
        )

    def pass_gated(slot, start, stop):
        for i in range(start, stop):
            z_arrived(slot, i).wait_recv()
            across_copy(slot, i).start()

    def send_away(start, stop):
        for i in range(start, stop):
            z_copy(i).start()

    def send_own(start, stop):
        for i in range(start, stop):
            own_copy(i).start()

    def gate(h, start, stop, dst):
        def one(t, carry):
            gate_tile(
                h * tiles + t, xbuf, halo, sw_ref, skip_ref, rate_ref, res_ref, tables, ext,
                product, made, prior, dst, span(t * LANES, LANES),
            )
            return carry

        lax.fori_loop(start, stop, one, 0)

    hand_on(0)

    @pl.when(seq < 2)
    def _():
        hand_on(1)

    for i in range(0, tiles, 2):
        gate(1 - side, i, i + 2, away)
        on(is_worker, [(send_away, i, i + 2)])

    @pl.when(seq >= 2)
    def _():
        hand_on(1)

    on(seq == 2, [(send_weights, 3, last)])
    far_sends = [
        (send_away, 0, 2), (send_weights, 5, 6), (send_away, 2, 4), (send_weights, 6, 7),
        (send_away, 4, 8), (send_weights, 7, 8),
    ]
    on(is_far, far_sends)
    pass_weight(1)
    gate(side, 0, tiles // 2, held.at[2, 0])
    on(is_worker, [(pass_gated, 0, 0, 1)])
    gate(side, tiles // 2, tiles, held.at[2, 0])

    def core_copy(slot, j):
        return remote(
            theirs.at[slot, :, pl.ds(j * wide, wide)], peer.at[slot, :, pl.ds(j * wide, wide)],
            core_send.at[slot, j], core_recv.at[slot, j], {"rep": 1 - rep},
        )

    def multiply(slot, j):
        cols = pl.ds(j * wide, wide)

        def one(h, dst):
            w_at = w_cols(h, j)

            def block(m, carry):
                rows = span(m * BLOCK, BLOCK)
                total = jnp.dot(
                    held[slot, 0, rows, :], wbuf[chan, :, w_at], preferred_element_type=jnp.float32
                )
                dst[slot, rows, cols] = total + jnp.dot(
                    held[slot, 1, rows, :], wbuf[1 - chan, :, w_at],
                    preferred_element_type=jnp.float32,
                )
                return carry

            lax.fori_loop(0, tok // BLOCK, block, 0)

        one(1 - rep, theirs)
        core_copy(slot, j).start()
        one(rep, mine)

    def back_copy(slot, j):
        cols = pl.ds(j * wide, wide)
        return remote(
            outgoing.at[slot, :, cols], incoming.at[:, cols], back_send.at[slot, j],
            back_recv.at[j], {"seq": sources[slot]},
        )

    def back_arrived(j):
        ref = incoming.at[:, pl.ds(j * wide, wide)]
        return remote(ref, ref, back_send.at[0, j], back_recv.at[j], {"seq": worker})

    def finish(slot, j):
        cols = pl.ds(j * wide, wide)
        core_copy(slot, j).wait_recv()
        total = mine[slot, :, cols] + peer[slot, :, cols]
        if slot == 2:
            mine[slot, :, cols] = total
        else:
            outgoing[slot, :, cols] = total.astype(jnp.bfloat16)
            back_copy(slot, j).start()

    def weight_ready(j):
        for i, (part, _) in enumerate(weight_parts):
            if part == j:
                wy_copy(i, 1 - slab).wait_recv()

    def gated_ready(slot):
        for i in range(tiles):
            across_copy(slot, i).wait_recv()

    def own_ready():
        for i in range(tiles):
            own_copy(i).wait_recv()

    far = [(send_own, 0, tiles)] + [(pass_weight, i) for i in range(2, last)]
    far += [(w_copy.wait,), (own_ready,)]
    for j in range(PARTS):
        far += [(weight_ready, j), (multiply, 2, j), (finish, 2, j)]
    on(is_far, far)

    near = [
        (pass_gated, 0, 1, 2), (pass_weight, 2), (pass_gated, 0, 2, 4), (pass_weight, 3),
        (pass_gated, 0, 4, 6), (pass_weight, 4), (pass_gated, 0, 6, 8),
        (pass_gated, 1, 0, 2), (send_own, 0, 2), (w_copy.wait,),
        (gated_ready, 0), (weight_ready, 0), (multiply, 0, 0),
        (weight_ready, 1), (multiply, 0, 1), (finish, 0, 0), (finish, 0, 1),
        (pass_weight, 5), (send_own, 2, 4), (pass_gated, 1, 2, 4),
        (weight_ready, 2), (multiply, 0, 2), (finish, 0, 2),
        (pass_weight, 6), (pass_gated, 1, 4, 8), (pass_weight, 7), (gated_ready, 1),
        (multiply, 1, 0), (send_own, 4, 8), (multiply, 1, 1), (finish, 1, 0),
        (weight_ready, 3), (multiply, 0, 3), (finish, 1, 1), (finish, 0, 3),
        (multiply, 1, 2), (multiply, 1, 3), (finish, 1, 2), (finish, 1, 3),
        (own_ready,), (multiply, 2, 0), (multiply, 2, 1), (finish, 2, 0), (multiply, 2, 2),
        (finish, 2, 1), (multiply, 2, 3), (finish, 2, 2), (finish, 2, 3),
    ]
    on(is_worker, near)

    for j in range(PARTS):
        cols = pl.ds(j * wide, wide)
        back_arrived(j).wait_recv()
        out_ref[:, cols] = (mine[2, :, cols] + incoming[:, cols].astype(jnp.float32)).astype(
            jnp.bfloat16
        )

    @pl.when(seq < count - 1)
    def _():
        halo_copy().wait_send()
        for h in range(2):
            end_copy(h).wait_send()

    for i in range(last):
        wz_copy(i).wait_send()
        wy_copy(i, slab).wait_send()
    for i in range(tiles):
        own_copy(i).wait_send()
        z_copy(i).wait_send()
    for j in range(PARTS):
        core_copy(2, j).wait_send()

    @pl.when(is_worker)
    def _():
        for slot in range(2):
            for i in range(tiles):
                across_copy(slot, i).wait_send()
            for j in range(PARTS):
                core_copy(slot, j).wait_send()
                back_copy(slot, j).wait_send()


def by_halves(projected, short_weight, skip_gain, pole_rate, residue, out_weight):
    tok, _, chans = projected.shape
    modes, groups = pole_rate.shape
    local_rows, out_cols = out_weight.shape[2], out_weight.shape[3]
    half, out_half = chans // 2, out_cols // 2
    tiles = half // LANES
    blocks = tok // BLOCK
    f32, bf16 = jnp.float32, jnp.bfloat16
    dma = pltpu.SemaphoreType.DMA
    anywhere = pl.BlockSpec(memory_space=pl.ANY)
    vmem = pl.BlockSpec(memory_space=pltpu.VMEM)
    return pl.pallas_call(
        half_kernel,
        in_specs=[anywhere, vmem, vmem, vmem, vmem, anywhere],
        out_specs=vmem,
        out_shape=jax.ShapeDtypeStruct((tok, out_half), bf16),
        scratch_shapes=[
            pltpu.VMEM((3, tok, chans), bf16),
            pltpu.VMEM((3, HALO, chans), bf16),
            pltpu.VMEM((8, chans), f32),
            pltpu.VMEM((8, chans), f32),
            pltpu.VMEM((tok + LEAD, LANES), f32),
            pltpu.VMEM((tok + LEAD, LANES), f32),
            pltpu.VMEM((tok, chans), f32),
            pltpu.VMEM((blocks, modes, chans), f32),
            pltpu.VMEM((modes, chans), f32),
            pltpu.VMEM((modes, chans), f32),
            pltpu.VMEM((groups, BLOCK), f32),
            pltpu.VMEM((chans // LANES, BLOCK, WIDE), bf16),
            pltpu.VMEM((tok, half), bf16),
            pltpu.VMEM((3, 2, tok, half), bf16),
            pltpu.VMEM((2, half, out_cols), bf16),
            pltpu.VMEM((3, tok, out_half), f32),
            pltpu.VMEM((3, tok, out_half), f32),
            pltpu.VMEM((3, tok, out_half), f32),
            pltpu.VMEM((2, tok, out_half), bf16),
            pltpu.VMEM((tok, out_half), bf16),
            dma((4,)),
            dma((2,)),
            dma((2,)),
            dma((2,)),
            dma((2 * PARTS,)),
            dma((2 * PARTS,)),
            dma((2 * PARTS,)),
            dma((2 * PARTS,)),
            dma((tiles,)),
            dma((tiles,)),
            dma((tiles,)),
            dma((2, tiles)),
            dma((2, tiles)),
            dma((2, tiles)),
            dma((3, PARTS)),
            dma((3, PARTS)),
            dma((2, PARTS)),
            dma((PARTS,)),
        ],
        compiler_params=pltpu.CompilerParams(
            collective_id=0, has_side_effects=True, vmem_limit_bytes=60 * 1024 * 1024
        ),
        name="hyena_halves",
    )(
        projected.transpose(1, 0, 2), short_weight, skip_gain[None], pole_rate, residue, out_weight
    )


def solution(mesh):
    sizes = tuple(mesh.shape[name] for name in ("groups", "seq", "chan", "rep"))
    return jax.shard_map(
        by_halves if sizes == (2, 4, 2, 2) else per_device,
        mesh=mesh,
        in_specs=(
            P(("groups", "seq"), None, ("chan", "rep")),
            P(None, None, ("chan", "rep")),
            P(("chan", "rep")),
            P(None, ("chan", "rep")),
            P(None, ("chan", "rep")),
            P(None, "rep", "seq", "chan"),
        ),
        out_specs=P(("groups", "seq"), ("chan", "rep")),
        check_vma=False,
    )
```

```python
import functools

import jax
import jax.numpy as jnp
from jax import lax
from jax.experimental import pallas as pl
from jax.experimental.pallas import tpu as pltpu
from jax.sharding import PartitionSpec as P

GROUP = 16
LANES = 128
BLOCK = 128
PER_TILE = LANES // GROUP
WIDE = PER_TILE * BLOCK
HALO = 16
Y_SHARE = 7
GATE_PARTS = 4
MESH = pl.DeviceIdType.MESH
HIGHEST = lax.Precision.HIGHEST


def iota(shape, dim):
    return lax.broadcasted_iota(jnp.int32, shape, dim)


def masked_rows(rows):
    lane_group = iota(rows.shape, 1) // GROUP
    zero = jnp.zeros_like(rows)
    return jnp.concatenate(
        [jnp.where(lane_group == g, rows, zero) for g in range(PER_TILE)], axis=0
    )


def kernel(dims, x_hbm, sw_ref, skip_ref, rate_ref, res_ref, w_hbm, out_ref,
           xbuf, halo, ext, lhs, q_buf, base, ends, own_end, prior, rate_ch, readout, gated, wbuf,
           acc, peer, local_sem, halo_sem, end_send, end_recv, gate_send, gate_recv,
           zsend, zrecv, ysend, yrecv, rep_send, rep_recv):
    count, slabs, n_chan, n_rep, chunks, row_chunks = dims
    tok, chans = gated.shape[1], gated.shape[2]
    modes, groups = rate_ref.shape
    tiles = chans // LANES
    blocks = tok // BLOCK
    local_rows, out_cols = w_hbm.shape[2], w_hbm.shape[3]
    half = out_cols // slabs
    y_cols = out_cols // LANES * Y_SHARE // 16 * LANES
    z_cols = out_cols - y_cols
    rows = local_rows // row_chunks
    out_half = out_cols // n_rep
    slab = lax.axis_index("groups")
    seq = lax.axis_index("seq")
    chan = lax.axis_index("chan")
    rep = lax.axis_index("rep")
    other_slab = 1 - slab
    other_rep = 1 - rep

    barrier = pltpu.get_barrier_semaphore()

    def greet(target):
        pl.semaphore_signal(barrier, inc=1, device_id=target, device_id_type=MESH)

    for d in range(1, count):
        greet({"seq": lax.rem(seq + d, count)})
    for d in range(1, n_chan):
        greet({"chan": lax.rem(chan + d, n_chan)})
    greet({"groups": other_slab})
    greet({"rep": other_rep})
    pl.semaphore_wait(barrier, count + n_chan)

    def z_span(h):
        return pl.ds(pl.multiple_of(h * y_cols, LANES), z_cols)

    def y_span(h):
        return pl.ds(pl.multiple_of(h * z_cols, LANES), y_cols)

    def piece(ref, c, r, cols):
        if chunks == 1:
            return ref.at[:, :, cols]
        return ref.at[c, pl.ds(pl.multiple_of(r * rows, rows), rows), cols]

    def split(ch):
        return ch // row_chunks, ch % row_chunks

    def own_piece(ch):
        c, r = split(ch)
        return piece(w_hbm.at[:, 0], c, r, z_span(slab))

    def block_piece(b, ch, cols):
        c, r = split(ch)
        return piece(wbuf.at[b], c, r, cols)

    def target_of(direction):
        return seq + 1 if direction == 0 else seq - 1

    def can_send(direction):
        return seq < count - 1 if direction == 0 else seq > 0

    def origin(direction, k):
        return seq - 1 - k if direction == 0 else seq + 1 + k

    def has(direction, k):
        return seq - 1 - k >= 0 if direction == 0 else seq + 1 + k < count

    def z_copy(direction, k, ch, src, b):
        return pltpu.make_async_remote_copy(
            src_ref=src, dst_ref=block_piece(b, ch, z_span(slab)),
            send_sem=zsend.at[direction, k, ch], recv_sem=zrecv.at[direction, k, ch],
            device_id={"seq": target_of(direction)}, device_id_type=MESH,
        )

    def y_copy(direction, k, ch, h):
        b = origin(direction, k)
        ref = block_piece(b, ch, y_span(h))
        return pltpu.make_async_remote_copy(
            src_ref=ref, dst_ref=ref,
            send_sem=ysend.at[direction, k, ch], recv_sem=yrecv.at[direction, k, ch],
            device_id={"groups": other_slab}, device_id_type=MESH,
        )

    def halo_copy():
        return pltpu.make_async_remote_copy(
            src_ref=x_hbm.at[:, pl.ds(tok - HALO, HALO), :], dst_ref=halo,
            send_sem=halo_sem.at[0], recv_sem=halo_sem.at[1],
            device_id={"seq": seq + 1}, device_id_type=MESH,
        )

    @pl.when(seq < count - 1)
    def _():
        halo_copy().start()

    for ch in range(chunks):
        for direction in (0, 1):
            @pl.when(can_send(direction))
            def _():
                z_copy(direction, 0, ch, own_piece(ch), seq).start()

    x_copy = pltpu.make_async_copy(x_hbm, xbuf, local_sem.at[0])
    x_copy.start()
    w_copy = pltpu.make_async_copy(w_hbm.at[:, 0], wbuf.at[seq], local_sem.at[1])
    w_copy.start()
    x_copy.wait()

    @pl.when(seq > 0)
    def _():
        halo_copy().wait_recv()

    @pl.when(seq == 0)
    def _():
        halo[...] = jnp.zeros_like(halo)

    def pump(k, ch):
        for direction in (0, 1):
            @pl.when(has(direction, k))
            def _():
                b = origin(direction, k)
                landed = block_piece(b, ch, z_span(slab))
                z_copy(direction, k, ch, landed, b).wait_recv()

                @pl.when(can_send(direction))
                def _():
                    z_copy(direction, k + 1, ch, landed, b).start()

                y_copy(direction, k, ch, slab).start()

    def conv_tile(t, carry):
        cols = pl.ds(pl.multiple_of(t * LANES, LANES), LANES)

        def short(s):
            x = xbuf[s, :, cols].astype(jnp.float32)
            ext[HALO:, :] = x
            ext[:HALO, :] = halo[s, :, cols].astype(jnp.float32)
            return (
                sw_ref[s, 0:1, cols] * x
                + sw_ref[s, 1:2, cols] * ext[HALO - 1 : tok + HALO - 1, :]
                + sw_ref[s, 2:3, cols] * ext[HALO - 2 : tok + HALO - 2, :]
            )

        q_buf[:, cols] = short(0)
        product = short(1)
        product = product * short(2)

        pick_wide = (
            iota((groups, WIDE), 0) == t * PER_TILE + iota((groups, WIDE), 1) // BLOCK
        ).astype(jnp.float32)
        pick = (
            iota((groups, LANES), 0) == t * PER_TILE + iota((groups, LANES), 1) // GROUP
        ).astype(jnp.float32)

        def spread(table, which):
            return jnp.dot(table, which, precision=HIGHEST, preferred_element_type=jnp.float32)

        rate, res = rate_ref[...], res_ref[...]
        rate_rep, res_rep = spread(rate, pick_wide), spread(res, pick_wide)
        rate_c, res_c = spread(rate, pick), spread(res, pick)
        diagonal = iota((modes, LANES), 0) == iota((modes, LANES), 1) % GROUP
        rate_row = jnp.sum(jnp.where(diagonal, rate_c, 0.0), axis=0, keepdims=True)
        res_row = jnp.sum(jnp.where(diagonal, res_c, 0.0), axis=0, keepdims=True)
        ahead = (iota((BLOCK, LANES), 0) + 1).astype(jnp.float32)
        read = (res_row * jnp.exp(-rate_row * ahead)).astype(jnp.bfloat16)

        lane = iota((modes, WIDE), 1) % BLOCK
        back = ((BLOCK - lane) % BLOCK).astype(jnp.float32)
        row = jnp.sum(res_rep * jnp.exp(-rate_rep * back), axis=0, keepdims=True)
        lower = iota((BLOCK, BLOCK), 1) <= iota((BLOCK, BLOCK), 0)
        for g in range(PER_TILE):
            part = slice(g * BLOCK, (g + 1) * BLOCK)
            wide = jnp.broadcast_to(row[:, part], (BLOCK, BLOCK))
            table = pltpu.roll(wide, 0, 1, stride=1, stride_axis=0)
            lhs[:BLOCK, part] = jnp.where(lower, table, 0.0).astype(jnp.bfloat16)
        lhs[BLOCK:, :] = jnp.exp(-rate_rep * (BLOCK - 1 - lane).astype(jnp.float32)).astype(
            jnp.bfloat16
        )

        decay = jnp.exp(-rate_c * BLOCK)
        state = jnp.zeros((modes, LANES), jnp.float32)
        for b in range(blocks):
            rows_b = slice(b * BLOCK, (b + 1) * BLOCK)
            p_b = product[rows_b]
            made = jnp.dot(
                lhs[...], masked_rows(p_b.astype(jnp.bfloat16)), preferred_element_type=jnp.float32
            )
            value = made[:BLOCK] + skip_ref[:, cols] * p_b
            if b > 0:
                value = value + jnp.dot(
                    read, masked_rows(state.astype(jnp.bfloat16)), preferred_element_type=jnp.float32
                )
            base[rows_b, cols] = value
            state = decay * state + made[BLOCK:]
        own_end[:, cols] = state
        rate_ch[:, cols] = rate_c
        readout[:, cols] = read
        return carry

    steps = [(k, ch) for k in range(count - 1) for ch in range(chunks)]
    total = len(steps)
    early = 1
    part = tiles // (early + 1)
    for e in range(early + 1):
        stop = tiles if e == early else (e + 1) * part
        lax.fori_loop(e * part, stop, conv_tile, 0)
        if e < early:
            pump(*steps[e])

    def end_copy(d):
        return pltpu.make_async_remote_copy(
            src_ref=own_end, dst_ref=ends.at[seq],
            send_sem=end_send.at[d], recv_sem=end_recv.at[seq],
            device_id={"seq": seq + d}, device_id_type=MESH,
        )

    def arrived_end(source):
        return pltpu.make_async_remote_copy(
            src_ref=own_end, dst_ref=ends.at[source],
            send_sem=end_send.at[0], recv_sem=end_recv.at[source],
            device_id={"seq": seq - 1}, device_id_type=MESH,
        )

    for d in range(1, count):
        @pl.when(seq + d < count)
        def _():
            end_copy(d).start()

    pump(*steps[early])
    prior[...] = jnp.zeros_like(prior)
    for source in range(count - 1):
        @pl.when(source < seq)
        def _():
            arrived_end(source).wait_recv()
            prior[...] = prior[...] * jnp.exp(-rate_ch[...] * tok) + ends[source]

    def gate_tile(t, carry):
        cols = pl.ds(pl.multiple_of(t * LANES, LANES), LANES)
        read = readout[:, cols]
        decay = jnp.exp(-rate_ch[:, cols] * BLOCK)
        state = prior[:, cols]
        for b in range(blocks):
            rows_b = slice(b * BLOCK, (b + 1) * BLOCK)
            across = jnp.dot(
                read, masked_rows(state.astype(jnp.bfloat16)), preferred_element_type=jnp.float32
            )
            gated[chan, rows_b, cols] = (
                q_buf[rows_b, cols] * (base[rows_b, cols] + across)
            ).astype(jnp.bfloat16)
            state = decay * state
        return carry

    share = chans // GATE_PARTS

    def gate_copy(d, i):
        part_ref = gated.at[chan, :, pl.ds(i * share, share)]
        return pltpu.make_async_remote_copy(
            src_ref=part_ref, dst_ref=part_ref,
            send_sem=gate_send.at[d, i], recv_sem=gate_recv.at[chan, i],
            device_id={"chan": lax.rem(chan + d, n_chan)}, device_id_type=MESH,
        )

    def arrived_gate(d, i):
        source = lax.rem(chan + d, n_chan)
        part_ref = gated.at[source, :, pl.ds(i * share, share)]
        return pltpu.make_async_remote_copy(
            src_ref=part_ref, dst_ref=part_ref,
            send_sem=gate_send.at[0, i], recv_sem=gate_recv.at[source, i],
            device_id={"chan": source}, device_id_type=MESH,
        )

    for i in range(GATE_PARTS):
        lax.fori_loop(i * tiles // GATE_PARTS, (i + 1) * tiles // GATE_PARTS, gate_tile, 0)
        for d in range(1, n_chan):
            gate_copy(d, i).start()

    middle = max(min(2, total), total * 2 // 3)
    for e in range(early + 1, middle):
        pump(*steps[e])
    acc[...] = jnp.zeros_like(acc)
    w_copy.wait()
    for d in range(1, n_chan):
        for i in range(GATE_PARTS):
            arrived_gate(d, i).wait_recv()

    streamed = chunks > 1
    col_tile = min(512, out_cols)

    def multiply(b, ch):
        c, r = split(ch)
        a = gated[c, :, pl.ds(pl.multiple_of(b * local_rows + r * rows, LANES), rows)]

        def column(n, carry):
            cols = pl.ds(pl.multiple_of(n * col_tile, col_tile), col_tile)
            w = wbuf[b, c, pl.ds(pl.multiple_of(r * rows, rows), rows), cols]
            acc[:, cols] += jnp.dot(a, w, preferred_element_type=jnp.float32)
            return carry

        lax.fori_loop(0, out_cols // col_tile, column, 0)

    def consume(k, ch):
        for direction in (0, 1):
            @pl.when(has(direction, k))
            def _():
                y_copy(direction, k, ch, other_slab).wait_recv()
                if streamed:
                    multiply(origin(direction, k), ch)

    left_over = total - middle
    own_per = -(-chunks // left_over)
    per = -(-total // left_over)

    def both(j, carry):
        pump(j // chunks, j % chunks)
        if streamed:
            for i in range(own_per):
                ch = (j - middle) * own_per + i

                @pl.when(ch < chunks)
                def _():
                    multiply(seq, ch)

        def late(i, inner):
            old = (j - middle) * per + i

            @pl.when(old < total)
            def _():
                consume(old // chunks, old % chunks)

            return inner

        lax.fori_loop(0, per, late, 0)
        return carry

    lax.fori_loop(middle, total, both, 0)

    if not streamed:
        def whole_column(n, carry):
            cols = pl.ds(pl.multiple_of(n * half, half), half)
            for c in range(n_chan):
                w = wbuf[:, c, :, cols].reshape(count * local_rows, half)
                acc[:, cols] += jnp.dot(gated[c], w, preferred_element_type=jnp.float32)
            return carry

        lax.fori_loop(0, slabs, whole_column, 0)

    quarter = tok // 4

    def rep_copy(i, side):
        return pltpu.make_async_remote_copy(
            src_ref=acc.at[
                pl.ds(i * quarter, quarter), pl.ds(pl.multiple_of(side * out_half, LANES), out_half)
            ],
            dst_ref=peer.at[pl.ds(i * quarter, quarter), :],
            send_sem=rep_send.at[i], recv_sem=rep_recv.at[i],
            device_id={"rep": other_rep}, device_id_type=MESH,
        )

    for i in range(4):
        rep_copy(i, other_rep).start()
    mine = pl.ds(pl.multiple_of(rep * out_half, LANES), out_half)
    for i in range(4):
        rep_copy(i, other_rep).wait_recv()
        rows_i = pl.ds(i * quarter, quarter)
        out_ref[rows_i, :] = (acc[rows_i, mine] + peer[rows_i, :]).astype(jnp.bfloat16)

    for i in range(4):
        rep_copy(i, other_rep).wait_send()
    for d in range(1, n_chan):
        for i in range(GATE_PARTS):
            gate_copy(d, i).wait_send()
    for d in range(1, count):
        @pl.when(seq + d < count)
        def _():
            end_copy(d).wait_send()

    @pl.when(seq < count - 1)
    def _():
        halo_copy().wait_send()

    for ch in range(chunks):
        for direction in (0, 1):
            @pl.when(can_send(direction))
            def _():
                z_copy(direction, 0, ch, own_piece(ch), seq).wait_send()

    def drain(j, carry):
        k, ch = j // chunks, j % chunks
        for direction in (0, 1):
            @pl.when(has(direction, k))
            def _():
                y_copy(direction, k, ch, slab).wait_send()

                @pl.when(can_send(direction))
                def _():
                    b = origin(direction, k)
                    z_copy(direction, k + 1, ch, block_piece(b, ch, z_span(slab)), b).wait_send()
        return carry

    lax.fori_loop(0, total, drain, 0)


def per_device(projected, short_weight, skip_gain, pole_rate, residue, out_weight):
    tok, _, chans = projected.shape
    modes, groups = pole_rate.shape
    n_chan, _, local_rows, out_cols = out_weight.shape
    count, slabs = lax.axis_size("seq"), lax.axis_size("groups")
    n_rep = lax.axis_size("rep")
    row_chunks = max(1, local_rows // 256)
    chunks = n_chan * row_chunks if local_rows % LANES == 0 else 1
    dims = (count, slabs, n_chan, n_rep, chunks, row_chunks)
    f32, bf16 = jnp.float32, jnp.bfloat16
    dma = pltpu.SemaphoreType.DMA
    anywhere = pl.BlockSpec(memory_space=pl.ANY)
    vmem = pl.BlockSpec(memory_space=pltpu.VMEM)
    return pl.pallas_call(
        functools.partial(kernel, dims),
        in_specs=[anywhere, vmem, vmem, vmem, vmem, anywhere],
        out_specs=vmem,
        out_shape=jax.ShapeDtypeStruct((tok, out_cols // n_rep), bf16),
        scratch_shapes=[
            pltpu.VMEM((3, tok, chans), bf16),
            pltpu.VMEM((3, HALO, chans), bf16),
            pltpu.VMEM((tok + HALO, LANES), f32),
            pltpu.VMEM((BLOCK + modes, WIDE), bf16),
            pltpu.VMEM((tok, chans), f32),
            pltpu.VMEM((tok, chans), f32),
            pltpu.VMEM((count, modes, chans), f32),
            pltpu.VMEM((modes, chans), f32),
            pltpu.VMEM((modes, chans), f32),
            pltpu.VMEM((modes, chans), f32),
            pltpu.VMEM((BLOCK, chans), bf16),
            pltpu.VMEM((n_chan, tok, chans), bf16),
            pltpu.VMEM((count, n_chan, local_rows, out_cols), bf16),
            pltpu.VMEM((tok, out_cols), f32),
            pltpu.VMEM((tok, out_cols // n_rep), f32),
            dma((2,)),
            dma((2,)),
            dma((count,)),
            dma((count,)),
            dma((n_chan, GATE_PARTS)),
            dma((n_chan, GATE_PARTS)),
            dma((2, count, chunks)),
            dma((2, count, chunks)),
            dma((2, count, chunks)),
            dma((2, count, chunks)),
            dma((4,)),
            dma((4,)),
        ],
        compiler_params=pltpu.CompilerParams(
            collective_id=0, has_side_effects=True, vmem_limit_bytes=60 * 1024 * 1024
        ),
        name="hyena",
    )(
        projected.transpose(1, 0, 2), short_weight, skip_gain[None], pole_rate, residue, out_weight
    )


PARTS = 4
LEAD = 8


def lag_table(rate_ref, res_ref, lag_rows):
    rate, res = rate_ref[...], res_ref[...]
    modes, groups = rate.shape
    back = ((BLOCK - iota((BLOCK, groups), 0)) % BLOCK).astype(jnp.float32)
    total = jnp.zeros((BLOCK, groups), jnp.float32)
    for n in range(modes):
        total = total + res[n : n + 1] * jnp.exp(-rate[n : n + 1] * back)
    lag_rows[...] = total.T


def by_channel(table, t):
    index = t * PER_TILE + iota(table.shape, 1) // GROUP
    return jnp.take_along_axis(table, index, axis=1)


def by_mode(spread):
    diagonal = iota(spread.shape, 0) == iota(spread.shape, 1) % GROUP
    return jnp.sum(jnp.where(diagonal, spread, 0.0), axis=0, keepdims=True)


def fill(ext, halo, xbuf, s, cols):
    ext[LEAD:, :] = xbuf[s, :, cols].astype(jnp.float32)
    ext[LEAD - 2 : LEAD, :] = halo[2 * s : 2 * s + 2, cols]


def short(ext, sw_ref, s, cols, b):
    start = LEAD + b * BLOCK
    total = sw_ref[s, 0:1, cols] * ext[start : start + BLOCK, :]
    for j in (1, 2):
        total = total + sw_ref[s, j : j + 1, cols] * ext[start - j : start - j + BLOCK, :]
    return total


def intake_tile(t, xbuf, halo, sw_ref, rate_ref, ext, ext2, product, made, own_end):
    cols = pl.ds(pl.multiple_of(t * LANES, LANES), LANES)
    blocks = xbuf.shape[1] // BLOCK
    fill(ext, halo, xbuf, 1, cols)
    fill(ext2, halo, xbuf, 2, cols)
    rate_c = by_channel(rate_ref[...], t)
    rate_row = by_mode(rate_c)
    behind = (BLOCK - 1 - iota((BLOCK, LANES), 0)).astype(jnp.float32)
    intake = jnp.exp(-rate_row * behind).T.astype(jnp.bfloat16)
    parts = []
    for b in range(blocks):
        p = short(ext, sw_ref, 1, cols, b) * short(ext2, sw_ref, 2, cols, b)
        product[b * BLOCK : (b + 1) * BLOCK, cols] = p
        parts.append(p.astype(jnp.bfloat16))
    every = jnp.dot(
        intake, jnp.concatenate(parts, axis=1), preferred_element_type=jnp.float32
    )
    decay = jnp.exp(-rate_c * BLOCK)
    lane_group = iota((GROUP, LANES), 1) // GROUP
    state = None
    for b in range(blocks):
        part = every[:, b * LANES : (b + 1) * LANES]
        own = jnp.zeros((GROUP, LANES), jnp.float32)
        for g in range(PER_TILE):
            own = jnp.where(lane_group == g, part[g * GROUP : (g + 1) * GROUP], own)
        if b < blocks - 1:
            made[b, :, cols] = own
        state = own if state is None else decay * state + own
    own_end[:, cols] = state


def table_tile(t, lag_rows, tables):
    lower = iota((BLOCK, BLOCK), 1) <= iota((BLOCK, BLOCK), 0)
    rows = lag_rows[pl.ds(pl.multiple_of(t * PER_TILE, PER_TILE), PER_TILE), :]
    for g in range(PER_TILE):
        wide = jnp.broadcast_to(rows[g : g + 1], (BLOCK, BLOCK))
        table = pltpu.roll(wide, 0, 1, stride=1, stride_axis=0)
        tables[t, :, g * BLOCK : (g + 1) * BLOCK] = jnp.where(lower, table, 0.0).astype(
            jnp.bfloat16
        )


def gate_tile(t, xbuf, halo, sw_ref, skip_ref, rate_ref, res_ref, tables, ext, product, made,
              prior, dst, dst_cols):
    cols = pl.ds(pl.multiple_of(t * LANES, LANES), LANES)
    blocks = xbuf.shape[1] // BLOCK
    fill(ext, halo, xbuf, 0, cols)
    rate_c = by_channel(rate_ref[...], t)
    rate_row, res_row = by_mode(rate_c), by_mode(by_channel(res_ref[...], t))
    ahead = (iota((BLOCK, LANES), 0) + 1).astype(jnp.float32)
    read = (res_row * jnp.exp(-rate_row * ahead)).astype(jnp.bfloat16)
    lhs = jnp.concatenate([tables[t], read], axis=1)
    decay = jnp.exp(-rate_c * BLOCK)
    state = prior[:, cols]
    for pair in range(0, blocks, 2):
        sides = []
        for b in range(pair, pair + 2):
            p = product[b * BLOCK : (b + 1) * BLOCK, cols].astype(jnp.bfloat16)
            sides.append(
                jnp.concatenate([masked_rows(p), masked_rows(state.astype(jnp.bfloat16))], axis=0)
            )
            if b < blocks - 1:
                state = decay * state + made[b, :, cols]
        value = jnp.dot(lhs, jnp.concatenate(sides, axis=1), preferred_element_type=jnp.float32)
        for b in range(pair, pair + 2):
            rows_b = slice(b * BLOCK, (b + 1) * BLOCK)
            v = value[:, (b - pair) * LANES : (b - pair + 1) * LANES]
            v = v + skip_ref[:, cols] * product[rows_b, cols]
            dst[rows_b, dst_cols] = (short(ext, sw_ref, 0, cols, b) * v).astype(jnp.bfloat16)


def half_kernel(x_hbm, sw_ref, skip_ref, rate_ref, res_ref, w_hbm, out_ref,
                xbuf, tail, halo_out, halo, ext, ext2, product, made, own_end, prior, lag_rows,
                tables, away, held, wbuf, mine, theirs, peer, outgoing, incoming,
                local_sem, halo_sem, end_send, end_recv, wz_send, wz_recv, wy_send, wy_recv,
                own_send, own_recv, z_send, z_recv, x_send, x_recv,
                core_send, core_recv, back_send, back_recv):
    count = 4
    tok, chans = product.shape
    half = chans // 2
    local_rows, out_cols = w_hbm.shape[2], w_hbm.shape[3]
    out_half = out_cols // 2
    wide = out_half // PARTS
    tiles = half // LANES
    slab = lax.axis_index("groups")
    seq = lax.axis_index("seq")
    chan = lax.axis_index("chan")
    rep = lax.axis_index("rep")
    side = seq // 2
    mate = seq + 1 - 2 * (seq % 2)
    worker = 2 - side
    is_worker = jnp.logical_or(seq == 1, seq == 2)
    is_far = jnp.logical_or(seq == 0, seq == 3)
    sources = (3 - seq, 6 - 3 * seq)
    to_slot = jnp.where(is_worker, 0, 1)

    barrier = pltpu.get_barrier_semaphore()

    def greet(target):
        pl.semaphore_signal(barrier, inc=1, device_id=target, device_id_type=MESH)

    def span(start, size):
        return pl.ds(pl.multiple_of(start, LANES), size)

    def remote(src, dst, send, recv, target):
        return pltpu.make_async_remote_copy(
            src_ref=src, dst_ref=dst, send_sem=send, recv_sem=recv,
            device_id=target, device_id_type=MESH,
        )

    def on(condition, steps):
        @pl.when(condition)
        def _():
            for step, *args in steps:
                step(*args)

    def x_copy(h):
        cols = span(h * half, half)
        return pltpu.make_async_copy(x_hbm.at[:, :, cols], xbuf.at[:, :, cols], local_sem.at[h])

    tail_copy = pltpu.make_async_copy(
        x_hbm.at[:, pl.ds(tok - HALO, HALO), :], tail, local_sem.at[3]
    )
    tail_copy.start()
    x_copy(0).start()
    x_copy(1).start()

    for d in range(1, count):
        greet({"seq": lax.rem(seq + d, count)})
    greet({"chan": 1 - chan})
    greet({"groups": 1 - slab})
    greet({"rep": 1 - rep})
    tail_copy.wait()
    halo_out[...] = jnp.zeros_like(halo_out)
    for s in range(3):
        halo_out[2 * s : 2 * s + 2, :] = tail[s].astype(jnp.float32)[HALO - 2 :]
    pl.semaphore_wait(barrier, count + 2)

    def w_cols(h, j):
        return span(h * out_half + j * wide, wide)

    def w_rows(owner):
        return span((owner % 2) * local_rows, local_rows)

    weight_parts = [(j, c) for j in range(PARTS) for c in range(2)]
    last = len(weight_parts)

    def wz_copy(i):
        j, c = weight_parts[i]
        return remote(
            w_hbm.at[c, 0, :, w_cols(slab, j)], wbuf.at[c, w_rows(seq), w_cols(slab, j)],
            wz_send.at[i], wz_recv.at[i], {"seq": mate},
        )

    def wz_arrived(i):
        j, c = weight_parts[i]
        ref = wbuf.at[c, w_rows(mate), w_cols(slab, j)]
        return remote(ref, ref, wz_send.at[i], wz_recv.at[i], {"seq": mate})

    def wy_copy(i, h):
        j, c = weight_parts[i]
        ref = wbuf.at[c, w_rows(mate), w_cols(h, j)]
        return remote(ref, ref, wy_send.at[i], wy_recv.at[i], {"groups": 1 - slab})

    def pass_weight(i):
        wz_arrived(i).wait_recv()
        wy_copy(i, slab).start()

    def send_weights(start, stop):
        for i in range(start, stop):
            wz_copy(i).start()

    def halo_copy():
        return remote(halo_out, halo, halo_sem.at[0], halo_sem.at[1], {"seq": seq + 1})

    @pl.when(seq < count - 1)
    def _():
        halo_copy().start()

    on(seq == 1, [(send_weights, 0, last)])
    on(seq == 2, [(send_weights, 0, 3)])
    on(seq == 3, [(send_weights, 0, 6)])
    w_copy = pltpu.make_async_copy(
        w_hbm.at[:, 0], wbuf.at[:, w_rows(seq), :], local_sem.at[2]
    )
    w_copy.start()

    def make_tables(h):
        def one(t, carry):
            table_tile(h * tiles + t, lag_rows, tables)
            return carry

        lax.fori_loop(0, tiles, one, 0)

    lag_table(rate_ref, res_ref, lag_rows)
    on(seq > 0, [(make_tables, 1 - side)])

    @pl.when(seq > 0)
    def _():
        remote(halo, halo, halo_sem.at[0], halo_sem.at[1], {"seq": seq - 1}).wait_recv()

    @pl.when(seq == 0)
    def _():
        halo[...] = jnp.zeros_like(halo)
        prior[...] = jnp.zeros_like(prior)

    def end_copy(h):
        cols = span(h * half, half)
        return remote(
            own_end.at[:, cols], prior.at[:, cols], end_send.at[h], end_recv.at[h],
            {"seq": seq + 1},
        )

    def intake(h):
        x_copy(h).wait()

        def one(t, carry):
            intake_tile(
                h * tiles + t, xbuf, halo, sw_ref, rate_ref, ext, ext2, product, made, own_end
            )
            return carry

        lax.fori_loop(0, tiles, one, 0)

    def hand_on(h):
        cols = span(h * half, half)
        ref = prior.at[:, cols]

        @pl.when(seq > 0)
        def _():
            remote(ref, ref, end_send.at[h], end_recv.at[h], {"seq": seq - 1}).wait_recv()

        @pl.when(seq == 0)
        def _():
            end_copy(h).start()

        @pl.when(is_worker)
        def _():
            rate_c = jnp.concatenate(
                [by_channel(rate_ref[...], h * tiles + t) for t in range(tiles)], axis=1
            )
            own_end[:, cols] = own_end[:, cols] + prior[:, cols] * jnp.exp(-rate_c * tok)
            end_copy(h).start()

    def z_copy(i):
        cols = pl.ds(i * LANES, LANES)
        return remote(
            away.at[:, cols], held.at[to_slot, 0, :, cols], z_send.at[i],
            z_recv.at[to_slot, i], {"seq": worker},
        )

    def z_arrived(slot, i):
        ref = held.at[slot, 0, :, pl.ds(i * LANES, LANES)]
        return remote(ref, ref, z_send.at[i], z_recv.at[slot, i], {"seq": sources[slot]})

    def own_copy(i):
        cols = pl.ds(i * LANES, LANES)
        return remote(
            held.at[2, 0, :, cols], held.at[2, 1, :, cols], own_send.at[i], own_recv.at[i],
            {"chan": 1 - chan},
        )

    def across_copy(slot, i):
        cols = pl.ds(i * LANES, LANES)
        return remote(
            held.at[slot, 0, :, cols], held.at[slot, 1, :, cols], x_send.at[slot, i],
            x_recv.at[slot, i], {"chan": 1 - chan},
        )

    def pass_gated(slot, start, stop):
        for i in range(start, stop):
            z_arrived(slot, i).wait_recv()
            across_copy(slot, i).start()

    def send_away(start, stop):
        for i in range(start, stop):
            z_copy(i).start()

    def send_own(start, stop):
        for i in range(start, stop):
            own_copy(i).start()

    def gate(h, start, stop, dst):
        def one(t, carry):
            gate_tile(
                h * tiles + t, xbuf, halo, sw_ref, skip_ref, rate_ref, res_ref, tables, ext,
                product, made, prior, dst, span(t * LANES, LANES),
            )
            return carry

        lax.fori_loop(start, stop, one, 0)

    intake(0)
    on(seq >= 2, [(make_tables, side)])
    hand_on(0)
    on(seq < 2, [(intake, 1), (hand_on, 1)])
    on(seq == 0, [(send_weights, 0, 5), (make_tables, 1 - side)])
    for i in range(0, tiles, 2):
        gate(1 - side, i, i + 2, away)
        on(is_worker, [(send_away, i, i + 2)])

    on(seq == 0, [
        (send_away, 0, 4), (send_weights, 5, 6), (send_away, 4, 8), (send_weights, 6, last),
    ])
    on(seq == 3, [(send_away, 0, 8), (send_weights, 6, last)])
    on(seq < 2, [(make_tables, side)])
    on(seq >= 2, [(intake, 1), (hand_on, 1)])
    on(seq == 2, [(send_weights, 3, last)])
    pass_weight(0)
    on(is_worker, [(pass_gated, 0, 0, 1)])
    gate(side, 0, tiles // 2, held.at[2, 0])
    on(is_worker, [(pass_gated, 0, 1, 2)])
    gate(side, tiles // 2, tiles, held.at[2, 0])

    def core_copy(slot, j):
        return remote(
            theirs.at[slot, :, span(j * wide, wide)], peer.at[slot, :, span(j * wide, wide)],
            core_send.at[slot, j], core_recv.at[slot, j], {"rep": 1 - rep},
        )

    def multiply(slot, j):
        cols = span(j * wide, wide)

        def one(h, dst):
            w_at = w_cols(h, j)
            total = jnp.dot(
                held[slot, 0], wbuf[chan, :, w_at], preferred_element_type=jnp.float32
            )
            dst[slot, :, cols] = total + jnp.dot(
                held[slot, 1], wbuf[1 - chan, :, w_at], preferred_element_type=jnp.float32
            )

        one(1 - rep, theirs)
        core_copy(slot, j).start()
        one(rep, mine)

    def back_copy(slot, j):
        cols = pl.ds(j * wide, wide)
        return remote(
            outgoing.at[slot, :, cols], incoming.at[:, cols], back_send.at[slot, j],
            back_recv.at[j], {"seq": sources[slot]},
        )

    def back_arrived(j):
        ref = incoming.at[:, pl.ds(j * wide, wide)]
        return remote(ref, ref, back_send.at[0, j], back_recv.at[j], {"seq": worker})

    def finish(slot, j):
        cols = span(j * wide, wide)
        core_copy(slot, j).wait_recv()
        total = mine[slot, :, cols] + peer[slot, :, cols]
        if slot == 2:
            mine[slot, :, cols] = total
        else:
            outgoing[slot, :, cols] = total.astype(jnp.bfloat16)
            back_copy(slot, j).start()

    def weight_ready(j):
        for i, (part, _) in enumerate(weight_parts):
            if part == j:
                wy_copy(i, 1 - slab).wait_recv()

    def gated_ready(slot):
        for i in range(tiles):
            across_copy(slot, i).wait_recv()

    def own_ready():
        for i in range(tiles):
            own_copy(i).wait_recv()

    far = [(send_own, 0, tiles)] + [(pass_weight, i) for i in range(1, last)]
    far += [(w_copy.wait,)] + [(weight_ready, j) for j in range(PARTS)]
    on(is_far, far)

    near = [
        (pass_gated, 0, 2, 3), (pass_weight, 1), (pass_gated, 0, 3, 5), (pass_weight, 2),
        (pass_gated, 0, 5, 7), (pass_weight, 3), (pass_gated, 0, 7, 8), (pass_gated, 1, 0, 1),
        (pass_weight, 4), (pass_gated, 1, 1, 2), (w_copy.wait,),
        (gated_ready, 0), (weight_ready, 0), (multiply, 0, 0), (finish, 0, 0),
        (pass_gated, 1, 2, 4), (send_own, 0, 1), (weight_ready, 1), (multiply, 0, 1),
        (finish, 0, 1), (pass_weight, 5), (pass_gated, 1, 4, 8),
        (weight_ready, 2), (multiply, 0, 2), (finish, 0, 2), (gated_ready, 1), (send_own, 1, 8),
        (multiply, 1, 0), (finish, 1, 0), (pass_weight, 6), (multiply, 1, 1), (finish, 1, 1),
        (multiply, 1, 2), (finish, 1, 2), (pass_weight, 7), (weight_ready, 3),
        (multiply, 0, 3), (multiply, 1, 3), (finish, 0, 3), (finish, 1, 3),
    ]
    on(is_worker, near)
    own_ready()

    def own_multiply(j, carry):
        multiply(2, j)

        @pl.when(j > 0)
        def _():
            finish(2, j - 1)

        return carry

    lax.fori_loop(0, PARTS, own_multiply, 0)
    finish(2, PARTS - 1)

    for j in range(PARTS):
        cols = pl.ds(j * wide, wide)
        back_arrived(j).wait_recv()
        out_ref[:, cols] = (mine[2, :, cols] + incoming[:, cols].astype(jnp.float32)).astype(
            jnp.bfloat16
        )

    @pl.when(seq < count - 1)
    def _():
        halo_copy().wait_send()
        for h in range(2):
            end_copy(h).wait_send()

    for i in range(last):
        wz_copy(i).wait_send()
        wy_copy(i, slab).wait_send()
    for i in range(tiles):
        own_copy(i).wait_send()
        z_copy(i).wait_send()
    for j in range(PARTS):
        core_copy(2, j).wait_send()

    @pl.when(is_worker)
    def _():
        for slot in range(2):
            for i in range(tiles):
                across_copy(slot, i).wait_send()
            for j in range(PARTS):
                core_copy(slot, j).wait_send()
                back_copy(slot, j).wait_send()


def by_halves(projected, short_weight, skip_gain, pole_rate, residue, out_weight):
    tok, _, chans = projected.shape
    modes, groups = pole_rate.shape
    local_rows, out_cols = out_weight.shape[2], out_weight.shape[3]
    half, out_half = chans // 2, out_cols // 2
    tiles = half // LANES
    blocks = tok // BLOCK
    f32, bf16 = jnp.float32, jnp.bfloat16
    dma = pltpu.SemaphoreType.DMA
    anywhere = pl.BlockSpec(memory_space=pl.ANY)
    vmem = pl.BlockSpec(memory_space=pltpu.VMEM)
    return pl.pallas_call(
        half_kernel,
        in_specs=[anywhere, vmem, vmem, vmem, vmem, anywhere],
        out_specs=vmem,
        out_shape=jax.ShapeDtypeStruct((tok, out_half), bf16),
        scratch_shapes=[
            pltpu.VMEM((3, tok, chans), bf16),
            pltpu.VMEM((3, HALO, chans), bf16),
            pltpu.VMEM((8, chans), f32),
            pltpu.VMEM((8, chans), f32),
            pltpu.VMEM((tok + LEAD, LANES), f32),
            pltpu.VMEM((tok + LEAD, LANES), f32),
            pltpu.VMEM((tok, chans), f32),
            pltpu.VMEM((blocks, modes, chans), f32),
            pltpu.VMEM((modes, chans), f32),
            pltpu.VMEM((modes, chans), f32),
            pltpu.VMEM((groups, BLOCK), f32),
            pltpu.VMEM((chans // LANES, BLOCK, WIDE), bf16),
            pltpu.VMEM((tok, half), bf16),
            pltpu.VMEM((3, 2, tok, half), bf16),
            pltpu.VMEM((2, half, out_cols), bf16),
            pltpu.VMEM((3, tok, out_half), f32),
            pltpu.VMEM((3, tok, out_half), f32),
            pltpu.VMEM((3, tok, out_half), f32),
            pltpu.VMEM((2, tok, out_half), bf16),
            pltpu.VMEM((tok, out_half), bf16),
            dma((4,)),
            dma((2,)),
            dma((2,)),
            dma((2,)),
            dma((2 * PARTS,)),
            dma((2 * PARTS,)),
            dma((2 * PARTS,)),
            dma((2 * PARTS,)),
            dma((tiles,)),
            dma((tiles,)),
            dma((tiles,)),
            dma((2, tiles)),
            dma((2, tiles)),
            dma((2, tiles)),
            dma((3, PARTS)),
            dma((3, PARTS)),
            dma((2, PARTS)),
            dma((PARTS,)),
        ],
        compiler_params=pltpu.CompilerParams(
            collective_id=0, has_side_effects=True, vmem_limit_bytes=60 * 1024 * 1024
        ),
        name="hyena_halves",
    )(
        projected.transpose(1, 0, 2), short_weight, skip_gain[None], pole_rate, residue, out_weight
    )


def solution(mesh):
    sizes = tuple(mesh.shape[name] for name in ("groups", "seq", "chan", "rep"))
    return jax.shard_map(
        by_halves if sizes == (2, 4, 2, 2) else per_device,
        mesh=mesh,
        in_specs=(
            P(("groups", "seq"), None, ("chan", "rep")),
            P(None, None, ("chan", "rep")),
            P(("chan", "rep")),
            P(None, ("chan", "rep")),
            P(None, ("chan", "rep")),
            P(None, "rep", "seq", "chan"),
        ),
        out_specs=P(("groups", "seq"), ("chan", "rep")),
        check_vma=False,
    )
```

```python
import functools

import jax
import jax.numpy as jnp
from jax import lax
from jax.experimental import pallas as pl
from jax.experimental.pallas import tpu as pltpu
from jax.sharding import PartitionSpec as P

GROUP = 16
LANES = 128
BLOCK = 128
PER_TILE = LANES // GROUP
WIDE = PER_TILE * BLOCK
HALO = 16
Y_SHARE = 7
GATE_PARTS = 4
MESH = pl.DeviceIdType.MESH
HIGHEST = lax.Precision.HIGHEST


def iota(shape, dim):
    return lax.broadcasted_iota(jnp.int32, shape, dim)


def masked_rows(rows):
    lane_group = iota(rows.shape, 1) // GROUP
    zero = jnp.zeros_like(rows)
    return jnp.concatenate(
        [jnp.where(lane_group == g, rows, zero) for g in range(PER_TILE)], axis=0
    )


def kernel(dims, x_hbm, sw_ref, skip_ref, rate_ref, res_ref, w_hbm, out_ref,
           xbuf, halo, ext, lhs, q_buf, base, ends, own_end, prior, rate_ch, readout, gated, wbuf,
           acc, peer, local_sem, halo_sem, end_send, end_recv, gate_send, gate_recv,
           zsend, zrecv, ysend, yrecv, rep_send, rep_recv):
    count, slabs, n_chan, n_rep, chunks, row_chunks = dims
    tok, chans = gated.shape[1], gated.shape[2]
    modes, groups = rate_ref.shape
    tiles = chans // LANES
    blocks = tok // BLOCK
    local_rows, out_cols = w_hbm.shape[2], w_hbm.shape[3]
    half = out_cols // slabs
    y_cols = out_cols // LANES * Y_SHARE // 16 * LANES
    z_cols = out_cols - y_cols
    rows = local_rows // row_chunks
    out_half = out_cols // n_rep
    slab = lax.axis_index("groups")
    seq = lax.axis_index("seq")
    chan = lax.axis_index("chan")
    rep = lax.axis_index("rep")
    other_slab = 1 - slab
    other_rep = 1 - rep

    barrier = pltpu.get_barrier_semaphore()

    def greet(target):
        pl.semaphore_signal(barrier, inc=1, device_id=target, device_id_type=MESH)

    for d in range(1, count):
        greet({"seq": lax.rem(seq + d, count)})
    for d in range(1, n_chan):
        greet({"chan": lax.rem(chan + d, n_chan)})
    greet({"groups": other_slab})
    greet({"rep": other_rep})
    pl.semaphore_wait(barrier, count + n_chan)

    def z_span(h):
        return pl.ds(pl.multiple_of(h * y_cols, LANES), z_cols)

    def y_span(h):
        return pl.ds(pl.multiple_of(h * z_cols, LANES), y_cols)

    def piece(ref, c, r, cols):
        if chunks == 1:
            return ref.at[:, :, cols]
        return ref.at[c, pl.ds(pl.multiple_of(r * rows, rows), rows), cols]

    def split(ch):
        return ch // row_chunks, ch % row_chunks

    def own_piece(ch):
        c, r = split(ch)
        return piece(w_hbm.at[:, 0], c, r, z_span(slab))

    def block_piece(b, ch, cols):
        c, r = split(ch)
        return piece(wbuf.at[b], c, r, cols)

    def target_of(direction):
        return seq + 1 if direction == 0 else seq - 1

    def can_send(direction):
        return seq < count - 1 if direction == 0 else seq > 0

    def origin(direction, k):
        return seq - 1 - k if direction == 0 else seq + 1 + k

    def has(direction, k):
        return seq - 1 - k >= 0 if direction == 0 else seq + 1 + k < count

    def z_copy(direction, k, ch, src, b):
        return pltpu.make_async_remote_copy(
            src_ref=src, dst_ref=block_piece(b, ch, z_span(slab)),
            send_sem=zsend.at[direction, k, ch], recv_sem=zrecv.at[direction, k, ch],
            device_id={"seq": target_of(direction)}, device_id_type=MESH,
        )

    def y_copy(direction, k, ch, h):
        b = origin(direction, k)
        ref = block_piece(b, ch, y_span(h))
        return pltpu.make_async_remote_copy(
            src_ref=ref, dst_ref=ref,
            send_sem=ysend.at[direction, k, ch], recv_sem=yrecv.at[direction, k, ch],
            device_id={"groups": other_slab}, device_id_type=MESH,
        )

    def halo_copy():
        return pltpu.make_async_remote_copy(
            src_ref=x_hbm.at[:, pl.ds(tok - HALO, HALO), :], dst_ref=halo,
            send_sem=halo_sem.at[0], recv_sem=halo_sem.at[1],
            device_id={"seq": seq + 1}, device_id_type=MESH,
        )

    @pl.when(seq < count - 1)
    def _():
        halo_copy().start()

    for ch in range(chunks):
        for direction in (0, 1):
            @pl.when(can_send(direction))
            def _():
                z_copy(direction, 0, ch, own_piece(ch), seq).start()

    x_copy = pltpu.make_async_copy(x_hbm, xbuf, local_sem.at[0])
    x_copy.start()
    w_copy = pltpu.make_async_copy(w_hbm.at[:, 0], wbuf.at[seq], local_sem.at[1])
    w_copy.start()
    x_copy.wait()

    @pl.when(seq > 0)
    def _():
        halo_copy().wait_recv()

    @pl.when(seq == 0)
    def _():
        halo[...] = jnp.zeros_like(halo)

    def pump(k, ch):
        for direction in (0, 1):
            @pl.when(has(direction, k))
            def _():
                b = origin(direction, k)
                landed = block_piece(b, ch, z_span(slab))
                z_copy(direction, k, ch, landed, b).wait_recv()

                @pl.when(can_send(direction))
                def _():
                    z_copy(direction, k + 1, ch, landed, b).start()

                y_copy(direction, k, ch, slab).start()

    def conv_tile(t, carry):
        cols = pl.ds(pl.multiple_of(t * LANES, LANES), LANES)

        def short(s):
            x = xbuf[s, :, cols].astype(jnp.float32)
            ext[HALO:, :] = x
            ext[:HALO, :] = halo[s, :, cols].astype(jnp.float32)
            return (
                sw_ref[s, 0:1, cols] * x
                + sw_ref[s, 1:2, cols] * ext[HALO - 1 : tok + HALO - 1, :]
                + sw_ref[s, 2:3, cols] * ext[HALO - 2 : tok + HALO - 2, :]
            )

        q_buf[:, cols] = short(0)
        product = short(1)
        product = product * short(2)

        pick_wide = (
            iota((groups, WIDE), 0) == t * PER_TILE + iota((groups, WIDE), 1) // BLOCK
        ).astype(jnp.float32)
        pick = (
            iota((groups, LANES), 0) == t * PER_TILE + iota((groups, LANES), 1) // GROUP
        ).astype(jnp.float32)

        def spread(table, which):
            return jnp.dot(table, which, precision=HIGHEST, preferred_element_type=jnp.float32)

        rate, res = rate_ref[...], res_ref[...]
        rate_rep, res_rep = spread(rate, pick_wide), spread(res, pick_wide)
        rate_c, res_c = spread(rate, pick), spread(res, pick)
        diagonal = iota((modes, LANES), 0) == iota((modes, LANES), 1) % GROUP
        rate_row = jnp.sum(jnp.where(diagonal, rate_c, 0.0), axis=0, keepdims=True)
        res_row = jnp.sum(jnp.where(diagonal, res_c, 0.0), axis=0, keepdims=True)
        ahead = (iota((BLOCK, LANES), 0) + 1).astype(jnp.float32)
        read = (res_row * jnp.exp(-rate_row * ahead)).astype(jnp.bfloat16)

        lane = iota((modes, WIDE), 1) % BLOCK
        back = ((BLOCK - lane) % BLOCK).astype(jnp.float32)
        row = jnp.sum(res_rep * jnp.exp(-rate_rep * back), axis=0, keepdims=True)
        lower = iota((BLOCK, BLOCK), 1) <= iota((BLOCK, BLOCK), 0)
        for g in range(PER_TILE):
            part = slice(g * BLOCK, (g + 1) * BLOCK)
            wide = jnp.broadcast_to(row[:, part], (BLOCK, BLOCK))
            table = pltpu.roll(wide, 0, 1, stride=1, stride_axis=0)
            lhs[:BLOCK, part] = jnp.where(lower, table, 0.0).astype(jnp.bfloat16)
        lhs[BLOCK:, :] = jnp.exp(-rate_rep * (BLOCK - 1 - lane).astype(jnp.float32)).astype(
            jnp.bfloat16
        )

        decay = jnp.exp(-rate_c * BLOCK)
        state = jnp.zeros((modes, LANES), jnp.float32)
        for b in range(blocks):
            rows_b = slice(b * BLOCK, (b + 1) * BLOCK)
            p_b = product[rows_b]
            made = jnp.dot(
                lhs[...], masked_rows(p_b.astype(jnp.bfloat16)), preferred_element_type=jnp.float32
            )
            value = made[:BLOCK] + skip_ref[:, cols] * p_b
            if b > 0:
                value = value + jnp.dot(
                    read, masked_rows(state.astype(jnp.bfloat16)), preferred_element_type=jnp.float32
                )
            base[rows_b, cols] = value
            state = decay * state + made[BLOCK:]
        own_end[:, cols] = state
        rate_ch[:, cols] = rate_c
        readout[:, cols] = read
        return carry

    steps = [(k, ch) for k in range(count - 1) for ch in range(chunks)]
    total = len(steps)
    early = 1
    part = tiles // (early + 1)
    for e in range(early + 1):
        stop = tiles if e == early else (e + 1) * part
        lax.fori_loop(e * part, stop, conv_tile, 0)
        if e < early:
            pump(*steps[e])

    def end_copy(d):
        return pltpu.make_async_remote_copy(
            src_ref=own_end, dst_ref=ends.at[seq],
            send_sem=end_send.at[d], recv_sem=end_recv.at[seq],
            device_id={"seq": seq + d}, device_id_type=MESH,
        )

    def arrived_end(source):
        return pltpu.make_async_remote_copy(
            src_ref=own_end, dst_ref=ends.at[source],
            send_sem=end_send.at[0], recv_sem=end_recv.at[source],
            device_id={"seq": seq - 1}, device_id_type=MESH,
        )

    for d in range(1, count):
        @pl.when(seq + d < count)
        def _():
            end_copy(d).start()

    pump(*steps[early])
    prior[...] = jnp.zeros_like(prior)
    for source in range(count - 1):
        @pl.when(source < seq)
        def _():
            arrived_end(source).wait_recv()
            prior[...] = prior[...] * jnp.exp(-rate_ch[...] * tok) + ends[source]

    def gate_tile(t, carry):
        cols = pl.ds(pl.multiple_of(t * LANES, LANES), LANES)
        read = readout[:, cols]
        decay = jnp.exp(-rate_ch[:, cols] * BLOCK)
        state = prior[:, cols]
        for b in range(blocks):
            rows_b = slice(b * BLOCK, (b + 1) * BLOCK)
            across = jnp.dot(
                read, masked_rows(state.astype(jnp.bfloat16)), preferred_element_type=jnp.float32
            )
            gated[chan, rows_b, cols] = (
                q_buf[rows_b, cols] * (base[rows_b, cols] + across)
            ).astype(jnp.bfloat16)
            state = decay * state
        return carry

    share = chans // GATE_PARTS

    def gate_copy(d, i):
        part_ref = gated.at[chan, :, pl.ds(i * share, share)]
        return pltpu.make_async_remote_copy(
            src_ref=part_ref, dst_ref=part_ref,
            send_sem=gate_send.at[d, i], recv_sem=gate_recv.at[chan, i],
            device_id={"chan": lax.rem(chan + d, n_chan)}, device_id_type=MESH,
        )

    def arrived_gate(d, i):
        source = lax.rem(chan + d, n_chan)
        part_ref = gated.at[source, :, pl.ds(i * share, share)]
        return pltpu.make_async_remote_copy(
            src_ref=part_ref, dst_ref=part_ref,
            send_sem=gate_send.at[0, i], recv_sem=gate_recv.at[source, i],
            device_id={"chan": source}, device_id_type=MESH,
        )

    for i in range(GATE_PARTS):
        lax.fori_loop(i * tiles // GATE_PARTS, (i + 1) * tiles // GATE_PARTS, gate_tile, 0)
        for d in range(1, n_chan):
            gate_copy(d, i).start()

    middle = max(min(2, total), total * 2 // 3)
    for e in range(early + 1, middle):
        pump(*steps[e])
    acc[...] = jnp.zeros_like(acc)
    w_copy.wait()
    for d in range(1, n_chan):
        for i in range(GATE_PARTS):
            arrived_gate(d, i).wait_recv()

    streamed = chunks > 1
    col_tile = min(512, out_cols)

    def multiply(b, ch):
        c, r = split(ch)
        a = gated[c, :, pl.ds(pl.multiple_of(b * local_rows + r * rows, LANES), rows)]

        def column(n, carry):
            cols = pl.ds(pl.multiple_of(n * col_tile, col_tile), col_tile)
            w = wbuf[b, c, pl.ds(pl.multiple_of(r * rows, rows), rows), cols]
            acc[:, cols] += jnp.dot(a, w, preferred_element_type=jnp.float32)
            return carry

        lax.fori_loop(0, out_cols // col_tile, column, 0)

    def consume(k, ch):
        for direction in (0, 1):
            @pl.when(has(direction, k))
            def _():
                y_copy(direction, k, ch, other_slab).wait_recv()
                if streamed:
                    multiply(origin(direction, k), ch)

    left_over = total - middle
    own_per = -(-chunks // left_over)
    per = -(-total // left_over)

    def both(j, carry):
        pump(j // chunks, j % chunks)
        if streamed:
            for i in range(own_per):
                ch = (j - middle) * own_per + i

                @pl.when(ch < chunks)
                def _():
                    multiply(seq, ch)

        def late(i, inner):
            old = (j - middle) * per + i

            @pl.when(old < total)
            def _():
                consume(old // chunks, old % chunks)

            return inner

        lax.fori_loop(0, per, late, 0)
        return carry

    lax.fori_loop(middle, total, both, 0)

    if not streamed:
        def whole_column(n, carry):
            cols = pl.ds(pl.multiple_of(n * half, half), half)
            for c in range(n_chan):
                w = wbuf[:, c, :, cols].reshape(count * local_rows, half)
                acc[:, cols] += jnp.dot(gated[c], w, preferred_element_type=jnp.float32)
            return carry

        lax.fori_loop(0, slabs, whole_column, 0)

    quarter = tok // 4

    def rep_copy(i, side):
        return pltpu.make_async_remote_copy(
            src_ref=acc.at[
                pl.ds(i * quarter, quarter), pl.ds(pl.multiple_of(side * out_half, LANES), out_half)
            ],
            dst_ref=peer.at[pl.ds(i * quarter, quarter), :],
            send_sem=rep_send.at[i], recv_sem=rep_recv.at[i],
            device_id={"rep": other_rep}, device_id_type=MESH,
        )

    for i in range(4):
        rep_copy(i, other_rep).start()
    mine = pl.ds(pl.multiple_of(rep * out_half, LANES), out_half)
    for i in range(4):
        rep_copy(i, other_rep).wait_recv()
        rows_i = pl.ds(i * quarter, quarter)
        out_ref[rows_i, :] = (acc[rows_i, mine] + peer[rows_i, :]).astype(jnp.bfloat16)

    for i in range(4):
        rep_copy(i, other_rep).wait_send()
    for d in range(1, n_chan):
        for i in range(GATE_PARTS):
            gate_copy(d, i).wait_send()
    for d in range(1, count):
        @pl.when(seq + d < count)
        def _():
            end_copy(d).wait_send()

    @pl.when(seq < count - 1)
    def _():
        halo_copy().wait_send()

    for ch in range(chunks):
        for direction in (0, 1):
            @pl.when(can_send(direction))
            def _():
                z_copy(direction, 0, ch, own_piece(ch), seq).wait_send()

    def drain(j, carry):
        k, ch = j // chunks, j % chunks
        for direction in (0, 1):
            @pl.when(has(direction, k))
            def _():
                y_copy(direction, k, ch, slab).wait_send()

                @pl.when(can_send(direction))
                def _():
                    b = origin(direction, k)
                    z_copy(direction, k + 1, ch, block_piece(b, ch, z_span(slab)), b).wait_send()
        return carry

    lax.fori_loop(0, total, drain, 0)


def per_device(projected, short_weight, skip_gain, pole_rate, residue, out_weight):
    tok, _, chans = projected.shape
    modes, groups = pole_rate.shape
    n_chan, _, local_rows, out_cols = out_weight.shape
    count, slabs = lax.axis_size("seq"), lax.axis_size("groups")
    n_rep = lax.axis_size("rep")
    row_chunks = max(1, local_rows // 256)
    chunks = n_chan * row_chunks if local_rows % LANES == 0 else 1
    dims = (count, slabs, n_chan, n_rep, chunks, row_chunks)
    f32, bf16 = jnp.float32, jnp.bfloat16
    dma = pltpu.SemaphoreType.DMA
    anywhere = pl.BlockSpec(memory_space=pl.ANY)
    vmem = pl.BlockSpec(memory_space=pltpu.VMEM)
    return pl.pallas_call(
        functools.partial(kernel, dims),
        in_specs=[anywhere, vmem, vmem, vmem, vmem, anywhere],
        out_specs=vmem,
        out_shape=jax.ShapeDtypeStruct((tok, out_cols // n_rep), bf16),
        scratch_shapes=[
            pltpu.VMEM((3, tok, chans), bf16),
            pltpu.VMEM((3, HALO, chans), bf16),
            pltpu.VMEM((tok + HALO, LANES), f32),
            pltpu.VMEM((BLOCK + modes, WIDE), bf16),
            pltpu.VMEM((tok, chans), f32),
            pltpu.VMEM((tok, chans), f32),
            pltpu.VMEM((count, modes, chans), f32),
            pltpu.VMEM((modes, chans), f32),
            pltpu.VMEM((modes, chans), f32),
            pltpu.VMEM((modes, chans), f32),
            pltpu.VMEM((BLOCK, chans), bf16),
            pltpu.VMEM((n_chan, tok, chans), bf16),
            pltpu.VMEM((count, n_chan, local_rows, out_cols), bf16),
            pltpu.VMEM((tok, out_cols), f32),
            pltpu.VMEM((tok, out_cols // n_rep), f32),
            dma((2,)),
            dma((2,)),
            dma((count,)),
            dma((count,)),
            dma((n_chan, GATE_PARTS)),
            dma((n_chan, GATE_PARTS)),
            dma((2, count, chunks)),
            dma((2, count, chunks)),
            dma((2, count, chunks)),
            dma((2, count, chunks)),
            dma((4,)),
            dma((4,)),
        ],
        compiler_params=pltpu.CompilerParams(
            collective_id=0, has_side_effects=True, vmem_limit_bytes=60 * 1024 * 1024
        ),
        name="hyena",
    )(
        projected.transpose(1, 0, 2), short_weight, skip_gain[None], pole_rate, residue, out_weight
    )


PARTS = 4
LEAD = 8


def lag_table(rate_ref, res_ref, lag_rows):
    rate, res = rate_ref[...], res_ref[...]
    modes, groups = rate.shape
    back = ((BLOCK - iota((BLOCK, groups), 0)) % BLOCK).astype(jnp.float32)
    total = jnp.zeros((BLOCK, groups), jnp.float32)
    for n in range(modes):
        total = total + res[n : n + 1] * jnp.exp(-rate[n : n + 1] * back)
    lag_rows[...] = total.T


def by_channel(table, t):
    index = t * PER_TILE + iota(table.shape, 1) // GROUP
    return jnp.take_along_axis(table, index, axis=1)


def by_mode(spread):
    diagonal = iota(spread.shape, 0) == iota(spread.shape, 1) % GROUP
    return jnp.sum(jnp.where(diagonal, spread, 0.0), axis=0, keepdims=True)


def fill(ext, xbuf, s, cols, rows):
    ext[LEAD : LEAD + rows, :] = xbuf[s, :rows, cols].astype(jnp.float32)


def lead(ext, halo, s, cols):
    ext[LEAD - 2 : LEAD, :] = halo[2 * s : 2 * s + 2, cols]


def short(ext, sw_ref, s, cols, b):
    start = LEAD + b * BLOCK
    total = sw_ref[s, 0:1, cols] * ext[start : start + BLOCK, :]
    for j in (1, 2):
        total = total + sw_ref[s, j : j + 1, cols] * ext[start - j : start - j + BLOCK, :]
    return total


def own_modes(every):
    lane_group = iota((GROUP, LANES), 1) // GROUP
    own = jnp.zeros((GROUP, LANES), jnp.float32)
    for g in range(PER_TILE):
        own = jnp.where(lane_group == g, every[g * GROUP : (g + 1) * GROUP], own)
    return own


def later_blocks(t, xbuf, sw_ref, rate_ref, ext, ext2, product, made, intakes):
    cols = pl.ds(pl.multiple_of(t * LANES, LANES), LANES)
    tok = xbuf.shape[1]
    blocks = tok // BLOCK
    fill(ext, xbuf, 1, cols, tok)
    fill(ext2, xbuf, 2, cols, tok)
    rate_row = by_mode(by_channel(rate_ref[...], t))
    behind = (BLOCK - 1 - iota((BLOCK, LANES), 0)).astype(jnp.float32)
    intake = jnp.exp(-rate_row * behind).T.astype(jnp.bfloat16)
    intakes[t] = intake
    parts = []
    for b in range(1, blocks):
        p = short(ext, sw_ref, 1, cols, b) * short(ext2, sw_ref, 2, cols, b)
        product[b * BLOCK : (b + 1) * BLOCK, cols] = p
        parts.append(p.astype(jnp.bfloat16))
    every = jnp.dot(
        intake, jnp.concatenate(parts, axis=1), preferred_element_type=jnp.float32
    )
    for b in range(1, blocks):
        made[b, :, cols] = own_modes(every[:, (b - 1) * LANES : b * LANES])


def first_block(t, xbuf, halo, sw_ref, rate_ref, ext, ext2, product, made, intakes, own_end):
    cols = pl.ds(pl.multiple_of(t * LANES, LANES), LANES)
    blocks = xbuf.shape[1] // BLOCK
    for e, s in ((ext, 1), (ext2, 2)):
        fill(e, xbuf, s, cols, BLOCK)
        lead(e, halo, s, cols)
    p = short(ext, sw_ref, 1, cols, 0) * short(ext2, sw_ref, 2, cols, 0)
    product[:BLOCK, cols] = p
    state = own_modes(
        jnp.dot(intakes[t], p.astype(jnp.bfloat16), preferred_element_type=jnp.float32)
    )
    made[0, :, cols] = state
    decay = jnp.exp(-by_channel(rate_ref[...], t) * BLOCK)
    for b in range(1, blocks):
        state = decay * state + made[b, :, cols]
    own_end[:, cols] = state


def whole_intake(t, xbuf, halo, sw_ref, rate_ref, ext, ext2, product, made, own_end):
    cols = pl.ds(pl.multiple_of(t * LANES, LANES), LANES)
    tok = xbuf.shape[1]
    blocks = tok // BLOCK
    for e, s in ((ext, 1), (ext2, 2)):
        fill(e, xbuf, s, cols, tok)
        lead(e, halo, s, cols)
    rate_c = by_channel(rate_ref[...], t)
    behind = (BLOCK - 1 - iota((BLOCK, LANES), 0)).astype(jnp.float32)
    intake = jnp.exp(-by_mode(rate_c) * behind).T.astype(jnp.bfloat16)
    parts = []
    for b in range(blocks):
        p = short(ext, sw_ref, 1, cols, b) * short(ext2, sw_ref, 2, cols, b)
        product[b * BLOCK : (b + 1) * BLOCK, cols] = p
        parts.append(p.astype(jnp.bfloat16))
    every = jnp.dot(
        intake, jnp.concatenate(parts, axis=1), preferred_element_type=jnp.float32
    )
    decay = jnp.exp(-rate_c * BLOCK)
    state = jnp.zeros_like(decay)
    for b in range(blocks):
        own = own_modes(every[:, b * LANES : (b + 1) * LANES])
        made[b, :, cols] = own
        state = decay * state + own
    own_end[:, cols] = state


def table_tile(t, lag_rows, tables):
    lower = iota((BLOCK, BLOCK), 1) <= iota((BLOCK, BLOCK), 0)
    rows = lag_rows[pl.ds(pl.multiple_of(t * PER_TILE, PER_TILE), PER_TILE), :]
    for g in range(PER_TILE):
        wide = jnp.broadcast_to(rows[g : g + 1], (BLOCK, BLOCK))
        table = pltpu.roll(wide, 0, 1, stride=1, stride_axis=0)
        tables[t, :, g * BLOCK : (g + 1) * BLOCK] = jnp.where(lower, table, 0.0).astype(
            jnp.bfloat16
        )


def gate_tile(t, xbuf, halo, sw_ref, skip_ref, rate_ref, res_ref, tables, ext, product, made,
              prior, dst, dst_cols):
    cols = pl.ds(pl.multiple_of(t * LANES, LANES), LANES)
    blocks = xbuf.shape[1] // BLOCK
    fill(ext, xbuf, 0, cols, blocks * BLOCK)
    lead(ext, halo, 0, cols)
    rate_c = by_channel(rate_ref[...], t)
    rate_row, res_row = by_mode(rate_c), by_mode(by_channel(res_ref[...], t))
    ahead = (iota((BLOCK, LANES), 0) + 1).astype(jnp.float32)
    read = (res_row * jnp.exp(-rate_row * ahead)).astype(jnp.bfloat16)
    lhs = jnp.concatenate([tables[t], read], axis=1)
    decay = jnp.exp(-rate_c * BLOCK)
    state = prior[:, cols]
    for pair in range(0, blocks, 2):
        sides = []
        for b in range(pair, pair + 2):
            p = product[b * BLOCK : (b + 1) * BLOCK, cols].astype(jnp.bfloat16)
            sides.append(
                jnp.concatenate([masked_rows(p), masked_rows(state.astype(jnp.bfloat16))], axis=0)
            )
            if b < blocks - 1:
                state = decay * state + made[b, :, cols]
        value = jnp.dot(lhs, jnp.concatenate(sides, axis=1), preferred_element_type=jnp.float32)
        for b in range(pair, pair + 2):
            rows_b = slice(b * BLOCK, (b + 1) * BLOCK)
            v = value[:, (b - pair) * LANES : (b - pair + 1) * LANES]
            v = v + skip_ref[:, cols] * product[rows_b, cols]
            dst[rows_b, dst_cols] = (short(ext, sw_ref, 0, cols, b) * v).astype(jnp.bfloat16)


def half_kernel(x_hbm, sw_ref, skip_ref, rate_ref, res_ref, w_hbm, out_ref,
                xbuf, tail, halo_out, halo, ext, ext2, product, made, intakes, own_end, prior,
                lag_rows, tables, away, held, wbuf, mine, theirs, peer, outgoing, incoming,
                local_sem, halo_sem, end_send, end_recv, wz_send, wz_recv, wy_send, wy_recv,
                own_send, own_recv, z_send, z_recv, x_send, x_recv,
                core_send, core_recv, back_send, back_recv):
    count = 4
    tok, chans = product.shape
    half = chans // 2
    local_rows, out_cols = w_hbm.shape[2], w_hbm.shape[3]
    out_half = out_cols // 2
    wide = out_half // PARTS
    tiles = half // LANES
    slab = lax.axis_index("groups")
    seq = lax.axis_index("seq")
    chan = lax.axis_index("chan")
    rep = lax.axis_index("rep")
    side = seq // 2
    mate = seq + 1 - 2 * (seq % 2)
    worker = 2 - side
    is_worker = jnp.logical_or(seq == 1, seq == 2)
    is_far = jnp.logical_or(seq == 0, seq == 3)
    sources = (3 - seq, 6 - 3 * seq)
    to_slot = jnp.where(is_worker, 0, 1)

    barrier = pltpu.get_barrier_semaphore()

    def greet(target):
        pl.semaphore_signal(barrier, inc=1, device_id=target, device_id_type=MESH)

    def span(start, size):
        return pl.ds(pl.multiple_of(start, LANES), size)

    def remote(src, dst, send, recv, target):
        return pltpu.make_async_remote_copy(
            src_ref=src, dst_ref=dst, send_sem=send, recv_sem=recv,
            device_id=target, device_id_type=MESH,
        )

    def on(condition, steps):
        @pl.when(condition)
        def _():
            for step, *args in steps:
                step(*args)

    def x_copy(h):
        cols = span(h * half, half)
        return pltpu.make_async_copy(x_hbm.at[:, :, cols], xbuf.at[:, :, cols], local_sem.at[h])

    tail_copy = pltpu.make_async_copy(
        x_hbm.at[:, pl.ds(tok - HALO, HALO), :], tail, local_sem.at[3]
    )
    tail_copy.start()
    x_copy(0).start()
    x_copy(1).start()

    for d in range(1, count):
        greet({"seq": lax.rem(seq + d, count)})
    greet({"chan": 1 - chan})
    greet({"groups": 1 - slab})
    greet({"rep": 1 - rep})
    tail_copy.wait()
    halo_out[...] = jnp.zeros_like(halo_out)
    for s in range(3):
        halo_out[2 * s : 2 * s + 2, :] = tail[s].astype(jnp.float32)[HALO - 2 :]
    def take_later(h):
        x_copy(h).wait()

        def one(t, carry):
            later_blocks(
                h * tiles + t, xbuf, sw_ref, rate_ref, ext, ext2, product, made, intakes
            )
            return carry

        lax.fori_loop(0, tiles, one, 0)

    def take_whole(h):
        x_copy(h).wait()

        def one(t, carry):
            whole_intake(
                h * tiles + t, xbuf, halo, sw_ref, rate_ref, ext, ext2, product, made, own_end
            )
            return carry

        lax.fori_loop(0, tiles, one, 0)

    def take_first(h):
        def one(t, carry):
            first_block(
                h * tiles + t, xbuf, halo, sw_ref, rate_ref, ext, ext2, product, made, intakes,
                own_end,
            )
            return carry

        lax.fori_loop(0, tiles, one, 0)

    @pl.when(seq == 0)
    def _():
        halo[...] = jnp.zeros_like(halo)
        prior[...] = jnp.zeros_like(prior)

    def make_tables(h):
        def one(t, carry):
            table_tile(h * tiles + t, lag_rows, tables)
            return carry

        lax.fori_loop(0, tiles, one, 0)

    def first_tables():
        lag_table(rate_ref, res_ref, lag_rows)
        make_tables(1 - side)

    on(seq == 0, [(take_whole, 0)])
    on(seq > 0, [(first_tables,)])
    pl.semaphore_wait(barrier, count + 2)

    def w_cols(h, j):
        return span(h * out_half + j * wide, wide)

    rows = local_rows // 2
    weight_parts = [(j, c, h) for j in range(PARTS) for c in range(2) for h in range(2)]
    last = len(weight_parts)

    def w_rows(owner, h):
        return pl.ds(pl.multiple_of((owner % 2) * local_rows + h * rows, rows), rows)

    def wz_copy(i):
        j, c, h = weight_parts[i]
        return remote(
            w_hbm.at[c, 0, pl.ds(h * rows, rows), w_cols(slab, j)],
            wbuf.at[c, w_rows(seq, h), w_cols(slab, j)],
            wz_send.at[i], wz_recv.at[i], {"seq": mate},
        )

    def wz_arrived(i):
        j, c, h = weight_parts[i]
        ref = wbuf.at[c, w_rows(mate, h), w_cols(slab, j)]
        return remote(ref, ref, wz_send.at[i], wz_recv.at[i], {"seq": mate})

    def wy_copy(i, side_cols):
        j, c, h = weight_parts[i]
        ref = wbuf.at[c, w_rows(mate, h), w_cols(side_cols, j)]
        return remote(ref, ref, wy_send.at[i], wy_recv.at[i], {"groups": 1 - slab})

    def pass_weight(k):
        for i in (2 * k, 2 * k + 1):
            wz_arrived(i).wait_recv()
            wy_copy(i, slab).start()

    def send_weights(start, stop):
        for i in range(start, stop):
            wz_copy(i).start()

    def halo_copy():
        return remote(halo_out, halo, halo_sem.at[0], halo_sem.at[1], {"seq": seq + 1})

    @pl.when(seq < count - 1)
    def _():
        halo_copy().start()

    w_copy = pltpu.make_async_copy(
        w_hbm.at[:, 0],
        wbuf.at[:, pl.ds(pl.multiple_of((seq % 2) * local_rows, local_rows), local_rows), :],
        local_sem.at[2],
    )

    def halo_ready():
        remote(halo, halo, halo_sem.at[0], halo_sem.at[1], {"seq": seq - 1}).wait_recv()

    def end_copy(h):
        cols = span(h * half, half)
        return remote(
            own_end.at[:, cols], prior.at[:, cols], end_send.at[h], end_recv.at[h],
            {"seq": seq + 1},
        )

    def hand_on(h):
        cols = span(h * half, half)
        ref = prior.at[:, cols]

        @pl.when(seq > 0)
        def _():
            remote(ref, ref, end_send.at[h], end_recv.at[h], {"seq": seq - 1}).wait_recv()

        @pl.when(seq == 0)
        def _():
            end_copy(h).start()

        @pl.when(is_worker)
        def _():
            rate_c = jnp.concatenate(
                [by_channel(rate_ref[...], h * tiles + t) for t in range(tiles)], axis=1
            )
            own_end[:, cols] = own_end[:, cols] + prior[:, cols] * jnp.exp(-rate_c * tok)
            end_copy(h).start()

    def z_copy(i):
        cols = span(i * LANES, LANES)
        return remote(
            away.at[:, cols], held.at[to_slot, 0, :, cols], z_send.at[i],
            z_recv.at[to_slot, i], {"seq": worker},
        )

    def z_arrived(slot, i):
        ref = held.at[slot, 0, :, pl.ds(i * LANES, LANES)]
        return remote(ref, ref, z_send.at[i], z_recv.at[slot, i], {"seq": sources[slot]})

    def own_copy(i):
        cols = span(i * LANES, LANES)
        return remote(
            held.at[2, 0, :, cols], held.at[2, 1, :, cols], own_send.at[i], own_recv.at[i],
            {"chan": 1 - chan},
        )

    def across_copy(slot, i):
        cols = pl.ds(i * LANES, LANES)
        return remote(
            held.at[slot, 0, :, cols], held.at[slot, 1, :, cols], x_send.at[slot, i],
            x_recv.at[slot, i], {"chan": 1 - chan},
        )

    def pass_gated(slot, start, stop):
        for i in range(start, stop):
            z_arrived(slot, i).wait_recv()
            across_copy(slot, i).start()

    def send_away(start, stop):
        for i in range(start, stop):
            z_copy(i).start()

    def send_own(start, stop):
        for i in range(start, stop):
            own_copy(i).start()

    def gate(h, start, stop, dst, sent=False):
        def one(t, carry):
            gate_tile(
                h * tiles + t, xbuf, halo, sw_ref, skip_ref, rate_ref, res_ref, tables, ext,
                product, made, prior, dst, span(t * LANES, LANES),
            )
            if sent:
                @pl.when(is_worker)
                def _():
                    z_copy(t).start()

            return carry

        lax.fori_loop(start, stop, one, 0)

    on(seq == 0, [(hand_on, 0), (send_weights, 0, 1)])
    on(seq == 1, [(send_weights, 0, last)])
    on(seq == 2, [(send_weights, 0, 5)])
    on(seq == 3, [(send_weights, 0, 12)])
    w_copy.start()
    on(seq > 0, [(take_later, 0)])
    on(seq == 0, [(take_whole, 1), (hand_on, 1), (send_weights, 1, 10)])
    on(seq > 0, [(take_later, 1), (halo_ready,), (take_first, 0)])
    on(seq == 1, [(hand_on, 0), (take_first, 1)])
    on(seq == 0, [(first_tables,)])
    on(seq == 1, [(hand_on, 1)])
    on(seq >= 2, [(hand_on, 0)])
    gate(1 - side, 0, tiles, away, True)
    on(seq == 0, [(send_away, 0, 8), (send_weights, 10, last)])
    on(seq == 3, [(send_away, 0, 8), (send_weights, 12, last)])
    on(seq >= 2, [(take_first, 1), (hand_on, 1)])
    on(seq == 2, [(send_weights, 5, last)])
    make_tables(side)
    on(is_worker, [(pass_gated, 0, 0, 1)])
    pass_weight(0)
    gate(side, 0, tiles // 2, held.at[2, 0])
    on(is_worker, [(pass_gated, 0, 1, 2)])
    gate(side, tiles // 2, tiles, held.at[2, 0])

    def core_copy(slot, j):
        return remote(
            theirs.at[slot, :, span(j * wide, wide)], peer.at[slot, :, span(j * wide, wide)],
            core_send.at[slot, j], core_recv.at[slot, j], {"rep": 1 - rep},
        )

    def multiply(slot, j):
        cols = span(j * wide, wide)

        def one(h, dst):
            w_at = w_cols(h, j)
            total = jnp.dot(
                held[slot, 0], wbuf[chan, :, w_at], preferred_element_type=jnp.float32
            )
            dst[slot, :, cols] = total + jnp.dot(
                held[slot, 1], wbuf[1 - chan, :, w_at], preferred_element_type=jnp.float32
            )

        one(1 - rep, theirs)
        core_copy(slot, j).start()
        one(rep, mine)

    def back_copy(slot, j):
        cols = pl.ds(j * wide, wide)
        return remote(
            outgoing.at[slot, :, cols], incoming.at[:, cols], back_send.at[slot, j],
            back_recv.at[j], {"seq": sources[slot]},
        )

    def back_arrived(j):
        ref = incoming.at[:, pl.ds(j * wide, wide)]
        return remote(ref, ref, back_send.at[0, j], back_recv.at[j], {"seq": worker})

    def finish(slot, j):
        cols = span(j * wide, wide)
        core_copy(slot, j).wait_recv()
        total = mine[slot, :, cols] + peer[slot, :, cols]
        if slot == 2:
            mine[slot, :, cols] = total
        else:
            outgoing[slot, :, cols] = total.astype(jnp.bfloat16)
            back_copy(slot, j).start()

    def weight_ready(j):
        for i, (part, _, _) in enumerate(weight_parts):
            if part == j:
                wy_copy(i, 1 - slab).wait_recv()

    def gated_ready(slot):
        for i in range(tiles):
            across_copy(slot, i).wait_recv()

    def own_ready():
        for i in range(tiles):
            own_copy(i).wait_recv()

    far = [(send_own, 0, tiles)] + [(pass_weight, i) for i in range(1, 2 * PARTS)]
    far += [(w_copy.wait,)] + [(weight_ready, j) for j in range(PARTS)]
    on(is_far, far)

    near = [
        (pass_gated, 0, 2, 3), (pass_weight, 1), (pass_gated, 0, 3, 5), (pass_weight, 2),
        (pass_gated, 0, 5, 7), (pass_weight, 3), (pass_gated, 0, 7, 8), (w_copy.wait,),
        (pass_weight, 4), (pass_gated, 1, 0, 2),
        (gated_ready, 0), (weight_ready, 0), (multiply, 0, 0), (finish, 0, 0),
        (pass_gated, 1, 2, 4), (weight_ready, 1), (multiply, 0, 1), (finish, 0, 1),
        (pass_gated, 1, 4, 8), (pass_weight, 5), (gated_ready, 1), (send_own, 0, 8),
        (multiply, 1, 0), (finish, 1, 0), (pass_weight, 6), (multiply, 1, 1), (finish, 1, 1),
        (weight_ready, 2), (multiply, 0, 2), (finish, 0, 2), (multiply, 1, 2), (finish, 1, 2),
        (pass_weight, 7), (weight_ready, 3),
        (multiply, 0, 3), (multiply, 1, 3), (finish, 0, 3), (finish, 1, 3),
    ]
    on(is_worker, near)
    own_ready()

    def own_multiply(j, carry):
        multiply(2, j)

        @pl.when(j > 0)
        def _():
            finish(2, j - 1)

        return carry

    lax.fori_loop(0, PARTS, own_multiply, 0)
    finish(2, PARTS - 1)

    for j in range(PARTS):
        cols = pl.ds(j * wide, wide)
        back_arrived(j).wait_recv()
        out_ref[:, cols] = (mine[2, :, cols] + incoming[:, cols].astype(jnp.float32)).astype(
            jnp.bfloat16
        )

    @pl.when(seq < count - 1)
    def _():
        halo_copy().wait_send()
        for h in range(2):
            end_copy(h).wait_send()

    for i in range(last):
        wz_copy(i).wait_send()
        wy_copy(i, slab).wait_send()
    for i in range(tiles):
        own_copy(i).wait_send()
        z_copy(i).wait_send()
    for j in range(PARTS):
        core_copy(2, j).wait_send()

    @pl.when(is_worker)
    def _():
        for slot in range(2):
            for i in range(tiles):
                across_copy(slot, i).wait_send()
            for j in range(PARTS):
                core_copy(slot, j).wait_send()
                back_copy(slot, j).wait_send()


def by_halves(projected, short_weight, skip_gain, pole_rate, residue, out_weight):
    tok, _, chans = projected.shape
    modes, groups = pole_rate.shape
    local_rows, out_cols = out_weight.shape[2], out_weight.shape[3]
    half, out_half = chans // 2, out_cols // 2
    tiles = half // LANES
    blocks = tok // BLOCK
    f32, bf16 = jnp.float32, jnp.bfloat16
    dma = pltpu.SemaphoreType.DMA
    anywhere = pl.BlockSpec(memory_space=pl.ANY)
    vmem = pl.BlockSpec(memory_space=pltpu.VMEM)
    return pl.pallas_call(
        half_kernel,
        in_specs=[anywhere, vmem, vmem, vmem, vmem, anywhere],
        out_specs=vmem,
        out_shape=jax.ShapeDtypeStruct((tok, out_half), bf16),
        scratch_shapes=[
            pltpu.VMEM((3, tok, chans), bf16),
            pltpu.VMEM((3, HALO, chans), bf16),
            pltpu.VMEM((8, chans), f32),
            pltpu.VMEM((8, chans), f32),
            pltpu.VMEM((tok + LEAD, LANES), f32),
            pltpu.VMEM((tok + LEAD, LANES), f32),
            pltpu.VMEM((tok, chans), f32),
            pltpu.VMEM((blocks, modes, chans), f32),
            pltpu.VMEM((chans // LANES, LANES, BLOCK), bf16),
            pltpu.VMEM((modes, chans), f32),
            pltpu.VMEM((modes, chans), f32),
            pltpu.VMEM((groups, BLOCK), f32),
            pltpu.VMEM((chans // LANES, BLOCK, WIDE), bf16),
            pltpu.VMEM((tok, half), bf16),
            pltpu.VMEM((3, 2, tok, half), bf16),
            pltpu.VMEM((2, half, out_cols), bf16),
            pltpu.VMEM((3, tok, out_half), f32),
            pltpu.VMEM((3, tok, out_half), f32),
            pltpu.VMEM((3, tok, out_half), f32),
            pltpu.VMEM((2, tok, out_half), bf16),
            pltpu.VMEM((tok, out_half), bf16),
            dma((4,)),
            dma((2,)),
            dma((2,)),
            dma((2,)),
            dma((4 * PARTS,)),
            dma((4 * PARTS,)),
            dma((4 * PARTS,)),
            dma((4 * PARTS,)),
            dma((tiles,)),
            dma((tiles,)),
            dma((tiles,)),
            dma((2, tiles)),
            dma((2, tiles)),
            dma((2, tiles)),
            dma((3, PARTS)),
            dma((3, PARTS)),
            dma((2, PARTS)),
            dma((PARTS,)),
        ],
        compiler_params=pltpu.CompilerParams(
            collective_id=0, has_side_effects=True, vmem_limit_bytes=60 * 1024 * 1024
        ),
        name="hyena_halves",
    )(
        projected.transpose(1, 0, 2), short_weight, skip_gain[None], pole_rate, residue, out_weight
    )


def solution(mesh):
    sizes = tuple(mesh.shape[name] for name in ("groups", "seq", "chan", "rep"))
    return jax.shard_map(
        by_halves if sizes == (2, 4, 2, 2) else per_device,
        mesh=mesh,
        in_specs=(
            P(("groups", "seq"), None, ("chan", "rep")),
            P(None, None, ("chan", "rep")),
            P(("chan", "rep")),
            P(None, ("chan", "rep")),
            P(None, ("chan", "rep")),
            P(None, "rep", "seq", "chan"),
        ),
        out_specs=P(("groups", "seq"), ("chan", "rep")),
        check_vma=False,
    )
```

```python
import functools

import jax
import jax.numpy as jnp
from jax import lax
from jax.experimental import pallas as pl
from jax.experimental.pallas import tpu as pltpu
from jax.sharding import PartitionSpec as P

GROUP = 16
LANES = 128
BLOCK = 128
PER_TILE = LANES // GROUP
WIDE = PER_TILE * BLOCK
HALO = 16
Y_SHARE = 7
GATE_PARTS = 4
MESH = pl.DeviceIdType.MESH
HIGHEST = lax.Precision.HIGHEST


def iota(shape, dim):
    return lax.broadcasted_iota(jnp.int32, shape, dim)


def masked_rows(rows):
    lane_group = iota(rows.shape, 1) // GROUP
    zero = jnp.zeros_like(rows)
    return jnp.concatenate(
        [jnp.where(lane_group == g, rows, zero) for g in range(PER_TILE)], axis=0
    )


def kernel(dims, x_hbm, sw_ref, skip_ref, rate_ref, res_ref, w_hbm, out_ref,
           xbuf, halo, ext, lhs, q_buf, base, ends, own_end, prior, rate_ch, readout, gated, wbuf,
           acc, peer, local_sem, halo_sem, end_send, end_recv, gate_send, gate_recv,
           zsend, zrecv, ysend, yrecv, rep_send, rep_recv):
    count, slabs, n_chan, n_rep, chunks, row_chunks = dims
    tok, chans = gated.shape[1], gated.shape[2]
    modes, groups = rate_ref.shape
    tiles = chans // LANES
    blocks = tok // BLOCK
    local_rows, out_cols = w_hbm.shape[2], w_hbm.shape[3]
    half = out_cols // slabs
    y_cols = out_cols // LANES * Y_SHARE // 16 * LANES
    z_cols = out_cols - y_cols
    rows = local_rows // row_chunks
    out_half = out_cols // n_rep
    slab = lax.axis_index("groups")
    seq = lax.axis_index("seq")
    chan = lax.axis_index("chan")
    rep = lax.axis_index("rep")
    other_slab = 1 - slab
    other_rep = 1 - rep

    barrier = pltpu.get_barrier_semaphore()

    def greet(target):
        pl.semaphore_signal(barrier, inc=1, device_id=target, device_id_type=MESH)

    for d in range(1, count):
        greet({"seq": lax.rem(seq + d, count)})
    for d in range(1, n_chan):
        greet({"chan": lax.rem(chan + d, n_chan)})
    greet({"groups": other_slab})
    greet({"rep": other_rep})
    pl.semaphore_wait(barrier, count + n_chan)

    def z_span(h):
        return pl.ds(pl.multiple_of(h * y_cols, LANES), z_cols)

    def y_span(h):
        return pl.ds(pl.multiple_of(h * z_cols, LANES), y_cols)

    def piece(ref, c, r, cols):
        if chunks == 1:
            return ref.at[:, :, cols]
        return ref.at[c, pl.ds(pl.multiple_of(r * rows, rows), rows), cols]

    def split(ch):
        return ch // row_chunks, ch % row_chunks

    def own_piece(ch):
        c, r = split(ch)
        return piece(w_hbm.at[:, 0], c, r, z_span(slab))

    def block_piece(b, ch, cols):
        c, r = split(ch)
        return piece(wbuf.at[b], c, r, cols)

    def target_of(direction):
        return seq + 1 if direction == 0 else seq - 1

    def can_send(direction):
        return seq < count - 1 if direction == 0 else seq > 0

    def origin(direction, k):
        return seq - 1 - k if direction == 0 else seq + 1 + k

    def has(direction, k):
        return seq - 1 - k >= 0 if direction == 0 else seq + 1 + k < count

    def z_copy(direction, k, ch, src, b):
        return pltpu.make_async_remote_copy(
            src_ref=src, dst_ref=block_piece(b, ch, z_span(slab)),
            send_sem=zsend.at[direction, k, ch], recv_sem=zrecv.at[direction, k, ch],
            device_id={"seq": target_of(direction)}, device_id_type=MESH,
        )

    def y_copy(direction, k, ch, h):
        b = origin(direction, k)
        ref = block_piece(b, ch, y_span(h))
        return pltpu.make_async_remote_copy(
            src_ref=ref, dst_ref=ref,
            send_sem=ysend.at[direction, k, ch], recv_sem=yrecv.at[direction, k, ch],
            device_id={"groups": other_slab}, device_id_type=MESH,
        )

    def halo_copy():
        return pltpu.make_async_remote_copy(
            src_ref=x_hbm.at[:, pl.ds(tok - HALO, HALO), :], dst_ref=halo,
            send_sem=halo_sem.at[0], recv_sem=halo_sem.at[1],
            device_id={"seq": seq + 1}, device_id_type=MESH,
        )

    @pl.when(seq < count - 1)
    def _():
        halo_copy().start()

    for ch in range(chunks):
        for direction in (0, 1):
            @pl.when(can_send(direction))
            def _():
                z_copy(direction, 0, ch, own_piece(ch), seq).start()

    x_copy = pltpu.make_async_copy(x_hbm, xbuf, local_sem.at[0])
    x_copy.start()
    w_copy = pltpu.make_async_copy(w_hbm.at[:, 0], wbuf.at[seq], local_sem.at[1])
    w_copy.start()
    x_copy.wait()

    @pl.when(seq > 0)
    def _():
        halo_copy().wait_recv()

    @pl.when(seq == 0)
    def _():
        halo[...] = jnp.zeros_like(halo)

    def pump(k, ch):
        for direction in (0, 1):
            @pl.when(has(direction, k))
            def _():
                b = origin(direction, k)
                landed = block_piece(b, ch, z_span(slab))
                z_copy(direction, k, ch, landed, b).wait_recv()

                @pl.when(can_send(direction))
                def _():
                    z_copy(direction, k + 1, ch, landed, b).start()

                y_copy(direction, k, ch, slab).start()

    def conv_tile(t, carry):
        cols = pl.ds(pl.multiple_of(t * LANES, LANES), LANES)

        def short(s):
            x = xbuf[s, :, cols].astype(jnp.float32)
            ext[HALO:, :] = x
            ext[:HALO, :] = halo[s, :, cols].astype(jnp.float32)
            return (
                sw_ref[s, 0:1, cols] * x
                + sw_ref[s, 1:2, cols] * ext[HALO - 1 : tok + HALO - 1, :]
                + sw_ref[s, 2:3, cols] * ext[HALO - 2 : tok + HALO - 2, :]
            )

        q_buf[:, cols] = short(0)
        product = short(1)
        product = product * short(2)

        pick_wide = (
            iota((groups, WIDE), 0) == t * PER_TILE + iota((groups, WIDE), 1) // BLOCK
        ).astype(jnp.float32)
        pick = (
            iota((groups, LANES), 0) == t * PER_TILE + iota((groups, LANES), 1) // GROUP
        ).astype(jnp.float32)

        def spread(table, which):
            return jnp.dot(table, which, precision=HIGHEST, preferred_element_type=jnp.float32)

        rate, res = rate_ref[...], res_ref[...]
        rate_rep, res_rep = spread(rate, pick_wide), spread(res, pick_wide)
        rate_c, res_c = spread(rate, pick), spread(res, pick)
        diagonal = iota((modes, LANES), 0) == iota((modes, LANES), 1) % GROUP
        rate_row = jnp.sum(jnp.where(diagonal, rate_c, 0.0), axis=0, keepdims=True)
        res_row = jnp.sum(jnp.where(diagonal, res_c, 0.0), axis=0, keepdims=True)
        ahead = (iota((BLOCK, LANES), 0) + 1).astype(jnp.float32)
        read = (res_row * jnp.exp(-rate_row * ahead)).astype(jnp.bfloat16)

        lane = iota((modes, WIDE), 1) % BLOCK
        back = ((BLOCK - lane) % BLOCK).astype(jnp.float32)
        row = jnp.sum(res_rep * jnp.exp(-rate_rep * back), axis=0, keepdims=True)
        lower = iota((BLOCK, BLOCK), 1) <= iota((BLOCK, BLOCK), 0)
        for g in range(PER_TILE):
            part = slice(g * BLOCK, (g + 1) * BLOCK)
            wide = jnp.broadcast_to(row[:, part], (BLOCK, BLOCK))
            table = pltpu.roll(wide, 0, 1, stride=1, stride_axis=0)
            lhs[:BLOCK, part] = jnp.where(lower, table, 0.0).astype(jnp.bfloat16)
        lhs[BLOCK:, :] = jnp.exp(-rate_rep * (BLOCK - 1 - lane).astype(jnp.float32)).astype(
            jnp.bfloat16
        )

        decay = jnp.exp(-rate_c * BLOCK)
        state = jnp.zeros((modes, LANES), jnp.float32)
        for b in range(blocks):
            rows_b = slice(b * BLOCK, (b + 1) * BLOCK)
            p_b = product[rows_b]
            made = jnp.dot(
                lhs[...], masked_rows(p_b.astype(jnp.bfloat16)), preferred_element_type=jnp.float32
            )
            value = made[:BLOCK] + skip_ref[:, cols] * p_b
            if b > 0:
                value = value + jnp.dot(
                    read, masked_rows(state.astype(jnp.bfloat16)), preferred_element_type=jnp.float32
                )
            base[rows_b, cols] = value
            state = decay * state + made[BLOCK:]
        own_end[:, cols] = state
        rate_ch[:, cols] = rate_c
        readout[:, cols] = read
        return carry

    steps = [(k, ch) for k in range(count - 1) for ch in range(chunks)]
    total = len(steps)
    early = 1
    part = tiles // (early + 1)
    for e in range(early + 1):
        stop = tiles if e == early else (e + 1) * part
        lax.fori_loop(e * part, stop, conv_tile, 0)
        if e < early:
            pump(*steps[e])

    def end_copy(d):
        return pltpu.make_async_remote_copy(
            src_ref=own_end, dst_ref=ends.at[seq],
            send_sem=end_send.at[d], recv_sem=end_recv.at[seq],
            device_id={"seq": seq + d}, device_id_type=MESH,
        )

    def arrived_end(source):
        return pltpu.make_async_remote_copy(
            src_ref=own_end, dst_ref=ends.at[source],
            send_sem=end_send.at[0], recv_sem=end_recv.at[source],
            device_id={"seq": seq - 1}, device_id_type=MESH,
        )

    for d in range(1, count):
        @pl.when(seq + d < count)
        def _():
            end_copy(d).start()

    pump(*steps[early])
    prior[...] = jnp.zeros_like(prior)
    for source in range(count - 1):
        @pl.when(source < seq)
        def _():
            arrived_end(source).wait_recv()
            prior[...] = prior[...] * jnp.exp(-rate_ch[...] * tok) + ends[source]

    def gate_tile(t, carry):
        cols = pl.ds(pl.multiple_of(t * LANES, LANES), LANES)
        read = readout[:, cols]
        decay = jnp.exp(-rate_ch[:, cols] * BLOCK)
        state = prior[:, cols]
        for b in range(blocks):
            rows_b = slice(b * BLOCK, (b + 1) * BLOCK)
            across = jnp.dot(
                read, masked_rows(state.astype(jnp.bfloat16)), preferred_element_type=jnp.float32
            )
            gated[chan, rows_b, cols] = (
                q_buf[rows_b, cols] * (base[rows_b, cols] + across)
            ).astype(jnp.bfloat16)
            state = decay * state
        return carry

    share = chans // GATE_PARTS

    def gate_copy(d, i):
        part_ref = gated.at[chan, :, pl.ds(i * share, share)]
        return pltpu.make_async_remote_copy(
            src_ref=part_ref, dst_ref=part_ref,
            send_sem=gate_send.at[d, i], recv_sem=gate_recv.at[chan, i],
            device_id={"chan": lax.rem(chan + d, n_chan)}, device_id_type=MESH,
        )

    def arrived_gate(d, i):
        source = lax.rem(chan + d, n_chan)
        part_ref = gated.at[source, :, pl.ds(i * share, share)]
        return pltpu.make_async_remote_copy(
            src_ref=part_ref, dst_ref=part_ref,
            send_sem=gate_send.at[0, i], recv_sem=gate_recv.at[source, i],
            device_id={"chan": source}, device_id_type=MESH,
        )

    for i in range(GATE_PARTS):
        lax.fori_loop(i * tiles // GATE_PARTS, (i + 1) * tiles // GATE_PARTS, gate_tile, 0)
        for d in range(1, n_chan):
            gate_copy(d, i).start()

    middle = max(min(2, total), total * 2 // 3)
    for e in range(early + 1, middle):
        pump(*steps[e])
    acc[...] = jnp.zeros_like(acc)
    w_copy.wait()
    for d in range(1, n_chan):
        for i in range(GATE_PARTS):
            arrived_gate(d, i).wait_recv()

    streamed = chunks > 1
    col_tile = min(512, out_cols)

    def multiply(b, ch):
        c, r = split(ch)
        a = gated[c, :, pl.ds(pl.multiple_of(b * local_rows + r * rows, LANES), rows)]

        def column(n, carry):
            cols = pl.ds(pl.multiple_of(n * col_tile, col_tile), col_tile)
            w = wbuf[b, c, pl.ds(pl.multiple_of(r * rows, rows), rows), cols]
            acc[:, cols] += jnp.dot(a, w, preferred_element_type=jnp.float32)
            return carry

        lax.fori_loop(0, out_cols // col_tile, column, 0)

    def consume(k, ch):
        for direction in (0, 1):
            @pl.when(has(direction, k))
            def _():
                y_copy(direction, k, ch, other_slab).wait_recv()
                if streamed:
                    multiply(origin(direction, k), ch)

    left_over = total - middle
    own_per = -(-chunks // left_over)
    per = -(-total // left_over)

    def both(j, carry):
        pump(j // chunks, j % chunks)
        if streamed:
            for i in range(own_per):
                ch = (j - middle) * own_per + i

                @pl.when(ch < chunks)
                def _():
                    multiply(seq, ch)

        def late(i, inner):
            old = (j - middle) * per + i

            @pl.when(old < total)
            def _():
                consume(old // chunks, old % chunks)

            return inner

        lax.fori_loop(0, per, late, 0)
        return carry

    lax.fori_loop(middle, total, both, 0)

    if not streamed:
        def whole_column(n, carry):
            cols = pl.ds(pl.multiple_of(n * half, half), half)
            for c in range(n_chan):
                w = wbuf[:, c, :, cols].reshape(count * local_rows, half)
                acc[:, cols] += jnp.dot(gated[c], w, preferred_element_type=jnp.float32)
            return carry

        lax.fori_loop(0, slabs, whole_column, 0)

    quarter = tok // 4

    def rep_copy(i, side):
        return pltpu.make_async_remote_copy(
            src_ref=acc.at[
                pl.ds(i * quarter, quarter), pl.ds(pl.multiple_of(side * out_half, LANES), out_half)
            ],
            dst_ref=peer.at[pl.ds(i * quarter, quarter), :],
            send_sem=rep_send.at[i], recv_sem=rep_recv.at[i],
            device_id={"rep": other_rep}, device_id_type=MESH,
        )

    for i in range(4):
        rep_copy(i, other_rep).start()
    mine = pl.ds(pl.multiple_of(rep * out_half, LANES), out_half)
    for i in range(4):
        rep_copy(i, other_rep).wait_recv()
        rows_i = pl.ds(i * quarter, quarter)
        out_ref[rows_i, :] = (acc[rows_i, mine] + peer[rows_i, :]).astype(jnp.bfloat16)

    for i in range(4):
        rep_copy(i, other_rep).wait_send()
    for d in range(1, n_chan):
        for i in range(GATE_PARTS):
            gate_copy(d, i).wait_send()
    for d in range(1, count):
        @pl.when(seq + d < count)
        def _():
            end_copy(d).wait_send()

    @pl.when(seq < count - 1)
    def _():
        halo_copy().wait_send()

    for ch in range(chunks):
        for direction in (0, 1):
            @pl.when(can_send(direction))
            def _():
                z_copy(direction, 0, ch, own_piece(ch), seq).wait_send()

    def drain(j, carry):
        k, ch = j // chunks, j % chunks
        for direction in (0, 1):
            @pl.when(has(direction, k))
            def _():
                y_copy(direction, k, ch, slab).wait_send()

                @pl.when(can_send(direction))
                def _():
                    b = origin(direction, k)
                    z_copy(direction, k + 1, ch, block_piece(b, ch, z_span(slab)), b).wait_send()
        return carry

    lax.fori_loop(0, total, drain, 0)


def per_device(projected, short_weight, skip_gain, pole_rate, residue, out_weight):
    tok, _, chans = projected.shape
    modes, groups = pole_rate.shape
    n_chan, _, local_rows, out_cols = out_weight.shape
    count, slabs = lax.axis_size("seq"), lax.axis_size("groups")
    n_rep = lax.axis_size("rep")
    row_chunks = max(1, local_rows // 256)
    chunks = n_chan * row_chunks if local_rows % LANES == 0 else 1
    dims = (count, slabs, n_chan, n_rep, chunks, row_chunks)
    f32, bf16 = jnp.float32, jnp.bfloat16
    dma = pltpu.SemaphoreType.DMA
    anywhere = pl.BlockSpec(memory_space=pl.ANY)
    vmem = pl.BlockSpec(memory_space=pltpu.VMEM)
    return pl.pallas_call(
        functools.partial(kernel, dims),
        in_specs=[anywhere, vmem, vmem, vmem, vmem, anywhere],
        out_specs=vmem,
        out_shape=jax.ShapeDtypeStruct((tok, out_cols // n_rep), bf16),
        scratch_shapes=[
            pltpu.VMEM((3, tok, chans), bf16),
            pltpu.VMEM((3, HALO, chans), bf16),
            pltpu.VMEM((tok + HALO, LANES), f32),
            pltpu.VMEM((BLOCK + modes, WIDE), bf16),
            pltpu.VMEM((tok, chans), f32),
            pltpu.VMEM((tok, chans), f32),
            pltpu.VMEM((count, modes, chans), f32),
            pltpu.VMEM((modes, chans), f32),
            pltpu.VMEM((modes, chans), f32),
            pltpu.VMEM((modes, chans), f32),
            pltpu.VMEM((BLOCK, chans), bf16),
            pltpu.VMEM((n_chan, tok, chans), bf16),
            pltpu.VMEM((count, n_chan, local_rows, out_cols), bf16),
            pltpu.VMEM((tok, out_cols), f32),
            pltpu.VMEM((tok, out_cols // n_rep), f32),
            dma((2,)),
            dma((2,)),
            dma((count,)),
            dma((count,)),
            dma((n_chan, GATE_PARTS)),
            dma((n_chan, GATE_PARTS)),
            dma((2, count, chunks)),
            dma((2, count, chunks)),
            dma((2, count, chunks)),
            dma((2, count, chunks)),
            dma((4,)),
            dma((4,)),
        ],
        compiler_params=pltpu.CompilerParams(
            collective_id=0, has_side_effects=True, vmem_limit_bytes=60 * 1024 * 1024
        ),
        name="hyena",
    )(
        projected.transpose(1, 0, 2), short_weight, skip_gain[None], pole_rate, residue, out_weight
    )


PARTS = 4
LEAD = 8


def lag_table(rate_ref, res_ref, lag_rows):
    rate, res = rate_ref[...], res_ref[...]
    modes, groups = rate.shape
    back = ((BLOCK - iota((BLOCK, groups), 0)) % BLOCK).astype(jnp.float32)
    total = jnp.zeros((BLOCK, groups), jnp.float32)
    for n in range(modes):
        total = total + res[n : n + 1] * jnp.exp(-rate[n : n + 1] * back)
    lag_rows[...] = total.T


def by_channel(table, t):
    index = t * PER_TILE + iota(table.shape, 1) // GROUP
    return jnp.take_along_axis(table, index, axis=1)


def by_mode(spread):
    diagonal = iota(spread.shape, 0) == iota(spread.shape, 1) % GROUP
    return jnp.sum(jnp.where(diagonal, spread, 0.0), axis=0, keepdims=True)


def fill(ext, xbuf, s, cols, rows):
    ext[LEAD : LEAD + rows, :] = xbuf[s, :rows, cols].astype(jnp.float32)


def lead(ext, halo, s, cols):
    ext[LEAD - 2 : LEAD, :] = halo[2 * s : 2 * s + 2, cols]


def short(ext, sw_ref, s, cols, b):
    start = LEAD + b * BLOCK
    total = sw_ref[s, 0:1, cols] * ext[start : start + BLOCK, :]
    for j in (1, 2):
        total = total + sw_ref[s, j : j + 1, cols] * ext[start - j : start - j + BLOCK, :]
    return total


def own_modes(every):
    lane_group = iota((GROUP, LANES), 1) // GROUP
    own = jnp.zeros((GROUP, LANES), jnp.float32)
    for g in range(PER_TILE):
        own = jnp.where(lane_group == g, every[g * GROUP : (g + 1) * GROUP], own)
    return own


def later_blocks(t, xbuf, sw_ref, rate_ref, ext, ext2, product, made, intakes):
    cols = pl.ds(pl.multiple_of(t * LANES, LANES), LANES)
    tok = xbuf.shape[1]
    blocks = tok // BLOCK
    fill(ext, xbuf, 1, cols, tok)
    fill(ext2, xbuf, 2, cols, tok)
    rate_row = by_mode(by_channel(rate_ref[...], t))
    behind = (BLOCK - 1 - iota((BLOCK, LANES), 0)).astype(jnp.float32)
    intake = jnp.exp(-rate_row * behind).T.astype(jnp.bfloat16)
    intakes[t] = intake
    parts = []
    for b in range(1, blocks):
        p = short(ext, sw_ref, 1, cols, b) * short(ext2, sw_ref, 2, cols, b)
        product[b * BLOCK : (b + 1) * BLOCK, cols] = p
        parts.append(p.astype(jnp.bfloat16))
    every = jnp.dot(
        intake, jnp.concatenate(parts, axis=1), preferred_element_type=jnp.float32
    )
    for b in range(1, blocks):
        made[b, :, cols] = own_modes(every[:, (b - 1) * LANES : b * LANES])


def first_block(t, xbuf, halo, sw_ref, rate_ref, ext, ext2, product, made, intakes, own_end):
    cols = pl.ds(pl.multiple_of(t * LANES, LANES), LANES)
    blocks = xbuf.shape[1] // BLOCK
    for e, s in ((ext, 1), (ext2, 2)):
        fill(e, xbuf, s, cols, BLOCK)
        lead(e, halo, s, cols)
    p = short(ext, sw_ref, 1, cols, 0) * short(ext2, sw_ref, 2, cols, 0)
    product[:BLOCK, cols] = p
    state = own_modes(
        jnp.dot(intakes[t], p.astype(jnp.bfloat16), preferred_element_type=jnp.float32)
    )
    made[0, :, cols] = state
    decay = jnp.exp(-by_channel(rate_ref[...], t) * BLOCK)
    for b in range(1, blocks):
        state = decay * state + made[b, :, cols]
    own_end[:, cols] = state


def whole_intake(t, xbuf, halo, sw_ref, rate_ref, ext, ext2, product, made, own_end):
    cols = pl.ds(pl.multiple_of(t * LANES, LANES), LANES)
    tok = xbuf.shape[1]
    blocks = tok // BLOCK
    for e, s in ((ext, 1), (ext2, 2)):
        fill(e, xbuf, s, cols, tok)
        lead(e, halo, s, cols)
    rate_c = by_channel(rate_ref[...], t)
    behind = (BLOCK - 1 - iota((BLOCK, LANES), 0)).astype(jnp.float32)
    intake = jnp.exp(-by_mode(rate_c) * behind).T.astype(jnp.bfloat16)
    parts = []
    for b in range(blocks):
        p = short(ext, sw_ref, 1, cols, b) * short(ext2, sw_ref, 2, cols, b)
        product[b * BLOCK : (b + 1) * BLOCK, cols] = p
        parts.append(p.astype(jnp.bfloat16))
    every = jnp.dot(
        intake, jnp.concatenate(parts, axis=1), preferred_element_type=jnp.float32
    )
    decay = jnp.exp(-rate_c * BLOCK)
    state = jnp.zeros_like(decay)
    for b in range(blocks):
        own = own_modes(every[:, b * LANES : (b + 1) * LANES])
        made[b, :, cols] = own
        state = decay * state + own
    own_end[:, cols] = state


def table_tile(t, lag_rows, tables):
    lower = iota((BLOCK, BLOCK), 1) <= iota((BLOCK, BLOCK), 0)
    rows = lag_rows[pl.ds(pl.multiple_of(t * PER_TILE, PER_TILE), PER_TILE), :]
    for g in range(PER_TILE):
        wide = jnp.broadcast_to(rows[g : g + 1], (BLOCK, BLOCK))
        table = pltpu.roll(wide, 0, 1, stride=1, stride_axis=0)
        tables[t, :, g * BLOCK : (g + 1) * BLOCK] = jnp.where(lower, table, 0.0).astype(
            jnp.bfloat16
        )


def gate_tile(t, xbuf, halo, sw_ref, skip_ref, rate_ref, res_ref, tables, ext, product, made,
              prior, dst, dst_cols):
    cols = pl.ds(pl.multiple_of(t * LANES, LANES), LANES)
    blocks = xbuf.shape[1] // BLOCK
    fill(ext, xbuf, 0, cols, blocks * BLOCK)
    lead(ext, halo, 0, cols)
    rate_c = by_channel(rate_ref[...], t)
    rate_row, res_row = by_mode(rate_c), by_mode(by_channel(res_ref[...], t))
    ahead = (iota((BLOCK, LANES), 0) + 1).astype(jnp.float32)
    read = (res_row * jnp.exp(-rate_row * ahead)).astype(jnp.bfloat16)
    lhs = jnp.concatenate([tables[t], read], axis=1)
    decay = jnp.exp(-rate_c * BLOCK)
    state = prior[:, cols]
    for pair in range(0, blocks, 2):
        sides = []
        for b in range(pair, pair + 2):
            p = product[b * BLOCK : (b + 1) * BLOCK, cols].astype(jnp.bfloat16)
            sides.append(
                jnp.concatenate([masked_rows(p), masked_rows(state.astype(jnp.bfloat16))], axis=0)
            )
            if b < blocks - 1:
                state = decay * state + made[b, :, cols]
        value = jnp.dot(lhs, jnp.concatenate(sides, axis=1), preferred_element_type=jnp.float32)
        for b in range(pair, pair + 2):
            rows_b = slice(b * BLOCK, (b + 1) * BLOCK)
            v = value[:, (b - pair) * LANES : (b - pair + 1) * LANES]
            v = v + skip_ref[:, cols] * product[rows_b, cols]
            dst[rows_b, dst_cols] = (short(ext, sw_ref, 0, cols, b) * v).astype(jnp.bfloat16)


def half_kernel(x_hbm, sw_ref, skip_ref, rate_ref, res_ref, w_hbm, out_ref,
                xbuf, tail, halo_out, halo, ext, ext2, product, made, intakes, own_end, prior,
                lag_rows, tables, away, held, wbuf, mine, theirs, peer, outgoing, incoming, done,
                local_sem, halo_sem, end_send, end_recv, wz_send, wz_recv, wy_send, wy_recv,
                own_send, own_recv, z_send, z_recv, x_send, x_recv,
                core_send, core_recv, back_send, back_recv, out_sem):
    count = 4
    tok, chans = product.shape
    half = chans // 2
    local_rows, out_cols = w_hbm.shape[2], w_hbm.shape[3]
    out_half = out_cols // 2
    wide = out_half // PARTS
    tiles = half // LANES
    slab = lax.axis_index("groups")
    seq = lax.axis_index("seq")
    chan = lax.axis_index("chan")
    rep = lax.axis_index("rep")
    side = seq // 2
    mate = seq + 1 - 2 * (seq % 2)
    worker = 2 - side
    is_worker = jnp.logical_or(seq == 1, seq == 2)
    is_far = jnp.logical_or(seq == 0, seq == 3)
    sources = (3 - seq, 6 - 3 * seq)
    to_slot = jnp.where(is_worker, 0, 1)

    barrier = pltpu.get_barrier_semaphore()

    def greet(target):
        pl.semaphore_signal(barrier, inc=1, device_id=target, device_id_type=MESH)

    def span(start, size):
        return pl.ds(pl.multiple_of(start, LANES), size)

    def remote(src, dst, send, recv, target):
        return pltpu.make_async_remote_copy(
            src_ref=src, dst_ref=dst, send_sem=send, recv_sem=recv,
            device_id=target, device_id_type=MESH,
        )

    def on(condition, steps):
        @pl.when(condition)
        def _():
            for step, *args in steps:
                step(*args)

    def x_copy(h):
        cols = span(h * half, half)
        return pltpu.make_async_copy(x_hbm.at[:, :, cols], xbuf.at[:, :, cols], local_sem.at[h])

    tail_copy = pltpu.make_async_copy(
        x_hbm.at[:, pl.ds(tok - HALO, HALO), :], tail, local_sem.at[3]
    )
    tail_copy.start()
    x_copy(0).start()
    x_copy(1).start()

    for d in range(1, count):
        greet({"seq": lax.rem(seq + d, count)})
    greet({"chan": 1 - chan})
    greet({"groups": 1 - slab})
    greet({"rep": 1 - rep})
    tail_copy.wait()
    halo_out[...] = jnp.zeros_like(halo_out)
    for s in range(3):
        halo_out[2 * s : 2 * s + 2, :] = tail[s].astype(jnp.float32)[HALO - 2 :]
    def take_later(h):
        x_copy(h).wait()

        def one(t, carry):
            later_blocks(
                h * tiles + t, xbuf, sw_ref, rate_ref, ext, ext2, product, made, intakes
            )
            return carry

        lax.fori_loop(0, tiles, one, 0)

    def take_whole(h):
        x_copy(h).wait()

        def one(t, carry):
            whole_intake(
                h * tiles + t, xbuf, halo, sw_ref, rate_ref, ext, ext2, product, made, own_end
            )
            return carry

        lax.fori_loop(0, tiles, one, 0)

    def take_first(h):
        def one(t, carry):
            first_block(
                h * tiles + t, xbuf, halo, sw_ref, rate_ref, ext, ext2, product, made, intakes,
                own_end,
            )
            return carry

        lax.fori_loop(0, tiles, one, 0)

    @pl.when(seq == 0)
    def _():
        halo[...] = jnp.zeros_like(halo)
        prior[...] = jnp.zeros_like(prior)

    def make_tables(h):
        def one(t, carry):
            table_tile(h * tiles + t, lag_rows, tables)
            return carry

        lax.fori_loop(0, tiles, one, 0)

    def first_tables():
        lag_table(rate_ref, res_ref, lag_rows)
        make_tables(1 - side)

    on(seq == 0, [(take_whole, 0)])
    on(seq > 0, [(first_tables,)])
    pl.semaphore_wait(barrier, count + 2)

    def w_cols(h, j):
        return span(h * out_half + j * wide, wide)

    rows = local_rows // 2
    weight_parts = [(j, c, h) for j in range(PARTS) for c in range(2) for h in range(2)]
    last = len(weight_parts)

    def w_rows(owner, h):
        return pl.ds(pl.multiple_of((owner % 2) * local_rows + h * rows, rows), rows)

    def wz_copy(i):
        j, c, h = weight_parts[i]
        return remote(
            w_hbm.at[c, 0, pl.ds(h * rows, rows), w_cols(slab, j)],
            wbuf.at[c, w_rows(seq, h), w_cols(slab, j)],
            wz_send.at[i], wz_recv.at[i], {"seq": mate},
        )

    def wz_arrived(i):
        j, c, h = weight_parts[i]
        ref = wbuf.at[c, w_rows(mate, h), w_cols(slab, j)]
        return remote(ref, ref, wz_send.at[i], wz_recv.at[i], {"seq": mate})

    def wy_copy(i, side_cols):
        j, c, h = weight_parts[i]
        ref = wbuf.at[c, w_rows(mate, h), w_cols(side_cols, j)]
        return remote(ref, ref, wy_send.at[i], wy_recv.at[i], {"groups": 1 - slab})

    def pass_weight(k):
        for i in (2 * k, 2 * k + 1):
            wz_arrived(i).wait_recv()
            wy_copy(i, slab).start()

    def send_weights(start, stop):
        for i in range(start, stop):
            wz_copy(i).start()

    def halo_copy():
        return remote(halo_out, halo, halo_sem.at[0], halo_sem.at[1], {"seq": seq + 1})

    @pl.when(seq < count - 1)
    def _():
        halo_copy().start()

    w_copy = pltpu.make_async_copy(
        w_hbm.at[:, 0],
        wbuf.at[:, pl.ds(pl.multiple_of((seq % 2) * local_rows, local_rows), local_rows), :],
        local_sem.at[2],
    )

    def halo_ready():
        remote(halo, halo, halo_sem.at[0], halo_sem.at[1], {"seq": seq - 1}).wait_recv()

    def end_copy(h):
        cols = span(h * half, half)
        return remote(
            own_end.at[:, cols], prior.at[:, cols], end_send.at[h], end_recv.at[h],
            {"seq": seq + 1},
        )

    def hand_on(h):
        cols = span(h * half, half)
        ref = prior.at[:, cols]

        @pl.when(seq > 0)
        def _():
            remote(ref, ref, end_send.at[h], end_recv.at[h], {"seq": seq - 1}).wait_recv()

        @pl.when(seq == 0)
        def _():
            end_copy(h).start()

        @pl.when(is_worker)
        def _():
            rate_c = jnp.concatenate(
                [by_channel(rate_ref[...], h * tiles + t) for t in range(tiles)], axis=1
            )
            own_end[:, cols] = own_end[:, cols] + prior[:, cols] * jnp.exp(-rate_c * tok)
            end_copy(h).start()

    def z_copy(i):
        cols = span(i * LANES, LANES)
        return remote(
            away.at[:, cols], held.at[to_slot, 0, :, cols], z_send.at[i],
            z_recv.at[to_slot, i], {"seq": worker},
        )

    def z_arrived(slot, i):
        ref = held.at[slot, 0, :, pl.ds(i * LANES, LANES)]
        return remote(ref, ref, z_send.at[i], z_recv.at[slot, i], {"seq": sources[slot]})

    def own_copy(i):
        cols = span(i * LANES, LANES)
        return remote(
            held.at[2, 0, :, cols], held.at[2, 1, :, cols], own_send.at[i], own_recv.at[i],
            {"chan": 1 - chan},
        )

    def across_copy(slot, i):
        cols = pl.ds(i * LANES, LANES)
        return remote(
            held.at[slot, 0, :, cols], held.at[slot, 1, :, cols], x_send.at[slot, i],
            x_recv.at[slot, i], {"chan": 1 - chan},
        )

    def pass_gated(slot, start, stop):
        for i in range(start, stop):
            z_arrived(slot, i).wait_recv()
            across_copy(slot, i).start()

    def send_away(start, stop):
        for i in range(start, stop):
            z_copy(i).start()

    def send_own(start, stop):
        for i in range(start, stop):
            own_copy(i).start()

    def gate(h, start, stop, dst, sent=False):
        def one(t, carry):
            gate_tile(
                h * tiles + t, xbuf, halo, sw_ref, skip_ref, rate_ref, res_ref, tables, ext,
                product, made, prior, dst, span(t * LANES, LANES),
            )
            if sent:
                @pl.when(is_worker)
                def _():
                    z_copy(t).start()

            return carry

        lax.fori_loop(start, stop, one, 0)

    on(seq == 0, [(hand_on, 0), (send_weights, 0, 1)])
    on(seq == 1, [(send_weights, 0, last)])
    on(seq == 2, [(send_weights, 0, 5)])
    on(seq == 3, [(send_weights, 0, 12)])
    w_copy.start()
    on(seq > 0, [(take_later, 0)])
    on(seq == 0, [(take_whole, 1), (hand_on, 1), (send_weights, 1, 10)])
    on(seq > 0, [(take_later, 1), (halo_ready,), (take_first, 0)])
    on(seq == 1, [(hand_on, 0), (take_first, 1)])
    on(seq == 0, [(first_tables,)])
    on(seq == 1, [(hand_on, 1)])
    on(seq >= 2, [(hand_on, 0)])
    gate(1 - side, 0, tiles, away, True)
    on(seq == 0, [(send_away, 0, 8), (send_weights, 10, last)])
    on(seq == 3, [(send_away, 0, 8), (send_weights, 12, last)])
    on(seq >= 2, [(take_first, 1), (hand_on, 1)])
    on(seq == 2, [(send_weights, 5, last)])
    make_tables(side)
    on(is_worker, [(pass_gated, 0, 0, 1)])
    pass_weight(0)
    gate(side, 0, tiles // 2, held.at[2, 0])
    on(is_worker, [(pass_gated, 0, 1, 2)])
    gate(side, tiles // 2, tiles, held.at[2, 0])

    def core_copy(slot, j):
        return remote(
            theirs.at[slot, :, span(j * wide, wide)], peer.at[slot, :, span(j * wide, wide)],
            core_send.at[slot, j], core_recv.at[slot, j], {"rep": 1 - rep},
        )

    def multiply(slot, j):
        cols = span(j * wide, wide)

        def one(h, dst):
            w_at = w_cols(h, j)
            total = jnp.dot(
                held[slot, 0], wbuf[chan, :, w_at], preferred_element_type=jnp.float32
            )
            dst[slot, :, cols] = total + jnp.dot(
                held[slot, 1], wbuf[1 - chan, :, w_at], preferred_element_type=jnp.float32
            )

        one(1 - rep, theirs)
        core_copy(slot, j).start()
        one(rep, mine)

    def back_copy(slot, j):
        cols = pl.ds(j * wide, wide)
        return remote(
            outgoing.at[slot, :, cols], incoming.at[:, cols], back_send.at[slot, j],
            back_recv.at[j], {"seq": sources[slot]},
        )

    def back_arrived(j):
        ref = incoming.at[:, pl.ds(j * wide, wide)]
        return remote(ref, ref, back_send.at[0, j], back_recv.at[j], {"seq": worker})

    def finish(slot, j):
        cols = span(j * wide, wide)
        core_copy(slot, j).wait_recv()
        total = mine[slot, :, cols] + peer[slot, :, cols]
        if slot == 2:
            mine[slot, :, cols] = total
        else:
            outgoing[slot, :, cols] = total.astype(jnp.bfloat16)
            back_copy(slot, j).start()

    def weight_ready(j):
        for i, (part, _, _) in enumerate(weight_parts):
            if part == j:
                wy_copy(i, 1 - slab).wait_recv()

    def gated_ready(slot):
        for i in range(tiles):
            across_copy(slot, i).wait_recv()

    def own_ready():
        for i in range(tiles):
            own_copy(i).wait_recv()

    far = [(send_own, 0, tiles)] + [(pass_weight, i) for i in range(1, 2 * PARTS)]
    far += [(w_copy.wait,)] + [(weight_ready, j) for j in range(PARTS)]
    on(is_far, far)

    near = [
        (pass_gated, 0, 2, 3), (pass_weight, 1), (pass_gated, 0, 3, 5), (pass_weight, 2),
        (pass_gated, 0, 5, 7), (pass_weight, 3), (pass_gated, 0, 7, 8), (w_copy.wait,),
        (pass_weight, 4), (pass_gated, 1, 0, 2),
        (gated_ready, 0), (weight_ready, 0), (multiply, 0, 0), (finish, 0, 0),
        (pass_gated, 1, 2, 4), (weight_ready, 1), (multiply, 0, 1), (finish, 0, 1),
        (pass_gated, 1, 4, 8), (pass_weight, 5), (gated_ready, 1), (send_own, 0, 8),
        (multiply, 1, 0), (finish, 1, 0), (pass_weight, 6), (multiply, 1, 1), (finish, 1, 1),
        (weight_ready, 2), (multiply, 0, 2), (finish, 0, 2), (multiply, 1, 2), (finish, 1, 2),
        (pass_weight, 7), (weight_ready, 3),
        (multiply, 0, 3), (multiply, 1, 3), (finish, 0, 3), (finish, 1, 3),
    ]
    on(is_worker, near)
    own_ready()

    def own_multiply(j, carry):
        multiply(2, j)

        @pl.when(j > 0)
        def _():
            finish(2, j - 1)

        return carry

    lax.fori_loop(0, PARTS, own_multiply, 0)
    finish(2, PARTS - 1)

    def out_copy(j):
        cols = pl.ds(j * wide, wide)
        return pltpu.make_async_copy(done.at[:, cols], out_ref.at[:, cols], out_sem.at[j])

    for j in range(PARTS):
        cols = pl.ds(j * wide, wide)
        back_arrived(j).wait_recv()
        done[:, cols] = (mine[2, :, cols] + incoming[:, cols].astype(jnp.float32)).astype(
            jnp.bfloat16
        )
        out_copy(j).start()

    @pl.when(seq < count - 1)
    def _():
        halo_copy().wait_send()
        for h in range(2):
            end_copy(h).wait_send()

    for i in range(last):
        wz_copy(i).wait_send()
        wy_copy(i, slab).wait_send()
    for i in range(tiles):
        own_copy(i).wait_send()
        z_copy(i).wait_send()
    for j in range(PARTS):
        core_copy(2, j).wait_send()

    @pl.when(is_worker)
    def _():
        for slot in range(2):
            for i in range(tiles):
                across_copy(slot, i).wait_send()
            for j in range(PARTS):
                core_copy(slot, j).wait_send()
                back_copy(slot, j).wait_send()

    for j in range(PARTS):
        out_copy(j).wait()


def by_halves(projected, short_weight, skip_gain, pole_rate, residue, out_weight):
    tok, _, chans = projected.shape
    modes, groups = pole_rate.shape
    local_rows, out_cols = out_weight.shape[2], out_weight.shape[3]
    half, out_half = chans // 2, out_cols // 2
    tiles = half // LANES
    blocks = tok // BLOCK
    f32, bf16 = jnp.float32, jnp.bfloat16
    dma = pltpu.SemaphoreType.DMA
    anywhere = pl.BlockSpec(memory_space=pl.ANY)
    vmem = pl.BlockSpec(memory_space=pltpu.VMEM)
    return pl.pallas_call(
        half_kernel,
        in_specs=[anywhere, vmem, vmem, vmem, vmem, anywhere],
        out_specs=anywhere,
        out_shape=jax.ShapeDtypeStruct((tok, out_half), bf16),
        scratch_shapes=[
            pltpu.VMEM((3, tok, chans), bf16),
            pltpu.VMEM((3, HALO, chans), bf16),
            pltpu.VMEM((8, chans), f32),
            pltpu.VMEM((8, chans), f32),
            pltpu.VMEM((tok + LEAD, LANES), f32),
            pltpu.VMEM((tok + LEAD, LANES), f32),
            pltpu.VMEM((tok, chans), f32),
            pltpu.VMEM((blocks, modes, chans), f32),
            pltpu.VMEM((chans // LANES, LANES, BLOCK), bf16),
            pltpu.VMEM((modes, chans), f32),
            pltpu.VMEM((modes, chans), f32),
            pltpu.VMEM((groups, BLOCK), f32),
            pltpu.VMEM((chans // LANES, BLOCK, WIDE), bf16),
            pltpu.VMEM((tok, half), bf16),
            pltpu.VMEM((3, 2, tok, half), bf16),
            pltpu.VMEM((2, half, out_cols), bf16),
            pltpu.VMEM((3, tok, out_half), f32),
            pltpu.VMEM((3, tok, out_half), f32),
            pltpu.VMEM((3, tok, out_half), f32),
            pltpu.VMEM((2, tok, out_half), bf16),
            pltpu.VMEM((tok, out_half), bf16),
            pltpu.VMEM((tok, out_half), bf16),
            dma((4,)),
            dma((2,)),
            dma((2,)),
            dma((2,)),
            dma((4 * PARTS,)),
            dma((4 * PARTS,)),
            dma((4 * PARTS,)),
            dma((4 * PARTS,)),
            dma((tiles,)),
            dma((tiles,)),
            dma((tiles,)),
            dma((2, tiles)),
            dma((2, tiles)),
            dma((2, tiles)),
            dma((3, PARTS)),
            dma((3, PARTS)),
            dma((2, PARTS)),
            dma((PARTS,)),
            dma((PARTS,)),
        ],
        compiler_params=pltpu.CompilerParams(
            collective_id=0, has_side_effects=True, vmem_limit_bytes=60 * 1024 * 1024
        ),
        name="hyena_halves",
    )(
        projected.transpose(1, 0, 2), short_weight, skip_gain[None], pole_rate, residue, out_weight
    )


def solution(mesh):
    sizes = tuple(mesh.shape[name] for name in ("groups", "seq", "chan", "rep"))
    return jax.shard_map(
        by_halves if sizes == (2, 4, 2, 2) else per_device,
        mesh=mesh,
        in_specs=(
            P(("groups", "seq"), None, ("chan", "rep")),
            P(None, None, ("chan", "rep")),
            P(("chan", "rep")),
            P(None, ("chan", "rep")),
            P(None, ("chan", "rep")),
            P(None, "rep", "seq", "chan"),
        ),
        out_specs=P(("groups", "seq"), ("chan", "rep")),
        check_vma=False,
    )
```

```python
import functools

import jax
import jax.numpy as jnp
from jax import lax
from jax.experimental import pallas as pl
from jax.experimental.pallas import tpu as pltpu
from jax.sharding import PartitionSpec as P

GROUP = 16
LANES = 128
BLOCK = 128
PER_TILE = LANES // GROUP
WIDE = PER_TILE * BLOCK
HALO = 16
Y_SHARE = 7
GATE_PARTS = 4
MESH = pl.DeviceIdType.MESH
HIGHEST = lax.Precision.HIGHEST


def iota(shape, dim):
    return lax.broadcasted_iota(jnp.int32, shape, dim)


def masked_rows(rows):
    lane_group = iota(rows.shape, 1) // GROUP
    zero = jnp.zeros_like(rows)
    return jnp.concatenate(
        [jnp.where(lane_group == g, rows, zero) for g in range(PER_TILE)], axis=0
    )


def kernel(dims, x_hbm, sw_ref, skip_ref, rate_ref, res_ref, w_hbm, out_ref,
           xbuf, halo, ext, lhs, q_buf, base, ends, own_end, prior, rate_ch, readout, gated, wbuf,
           acc, peer, local_sem, halo_sem, end_send, end_recv, gate_send, gate_recv,
           zsend, zrecv, ysend, yrecv, rep_send, rep_recv):
    count, slabs, n_chan, n_rep, chunks, row_chunks = dims
    tok, chans = gated.shape[1], gated.shape[2]
    modes, groups = rate_ref.shape
    tiles = chans // LANES
    blocks = tok // BLOCK
    local_rows, out_cols = w_hbm.shape[2], w_hbm.shape[3]
    half = out_cols // slabs
    y_cols = out_cols // LANES * Y_SHARE // 16 * LANES
    z_cols = out_cols - y_cols
    rows = local_rows // row_chunks
    out_half = out_cols // n_rep
    slab = lax.axis_index("groups")
    seq = lax.axis_index("seq")
    chan = lax.axis_index("chan")
    rep = lax.axis_index("rep")
    other_slab = 1 - slab
    other_rep = 1 - rep

    barrier = pltpu.get_barrier_semaphore()

    def greet(target):
        pl.semaphore_signal(barrier, inc=1, device_id=target, device_id_type=MESH)

    for d in range(1, count):
        greet({"seq": lax.rem(seq + d, count)})
    for d in range(1, n_chan):
        greet({"chan": lax.rem(chan + d, n_chan)})
    greet({"groups": other_slab})
    greet({"rep": other_rep})
    pl.semaphore_wait(barrier, count + n_chan)

    def z_span(h):
        return pl.ds(pl.multiple_of(h * y_cols, LANES), z_cols)

    def y_span(h):
        return pl.ds(pl.multiple_of(h * z_cols, LANES), y_cols)

    def piece(ref, c, r, cols):
        if chunks == 1:
            return ref.at[:, :, cols]
        return ref.at[c, pl.ds(pl.multiple_of(r * rows, rows), rows), cols]

    def split(ch):
        return ch // row_chunks, ch % row_chunks

    def own_piece(ch):
        c, r = split(ch)
        return piece(w_hbm.at[:, 0], c, r, z_span(slab))

    def block_piece(b, ch, cols):
        c, r = split(ch)
        return piece(wbuf.at[b], c, r, cols)

    def target_of(direction):
        return seq + 1 if direction == 0 else seq - 1

    def can_send(direction):
        return seq < count - 1 if direction == 0 else seq > 0

    def origin(direction, k):
        return seq - 1 - k if direction == 0 else seq + 1 + k

    def has(direction, k):
        return seq - 1 - k >= 0 if direction == 0 else seq + 1 + k < count

    def z_copy(direction, k, ch, src, b):
        return pltpu.make_async_remote_copy(
            src_ref=src, dst_ref=block_piece(b, ch, z_span(slab)),
            send_sem=zsend.at[direction, k, ch], recv_sem=zrecv.at[direction, k, ch],
            device_id={"seq": target_of(direction)}, device_id_type=MESH,
        )

    def y_copy(direction, k, ch, h):
        b = origin(direction, k)
        ref = block_piece(b, ch, y_span(h))
        return pltpu.make_async_remote_copy(
            src_ref=ref, dst_ref=ref,
            send_sem=ysend.at[direction, k, ch], recv_sem=yrecv.at[direction, k, ch],
            device_id={"groups": other_slab}, device_id_type=MESH,
        )

    def halo_copy():
        return pltpu.make_async_remote_copy(
            src_ref=x_hbm.at[:, pl.ds(tok - HALO, HALO), :], dst_ref=halo,
            send_sem=halo_sem.at[0], recv_sem=halo_sem.at[1],
            device_id={"seq": seq + 1}, device_id_type=MESH,
        )

    @pl.when(seq < count - 1)
    def _():
        halo_copy().start()

    for ch in range(chunks):
        for direction in (0, 1):
            @pl.when(can_send(direction))
            def _():
                z_copy(direction, 0, ch, own_piece(ch), seq).start()

    x_copy = pltpu.make_async_copy(x_hbm, xbuf, local_sem.at[0])
    x_copy.start()
    w_copy = pltpu.make_async_copy(w_hbm.at[:, 0], wbuf.at[seq], local_sem.at[1])
    w_copy.start()
    x_copy.wait()

    @pl.when(seq > 0)
    def _():
        halo_copy().wait_recv()

    @pl.when(seq == 0)
    def _():
        halo[...] = jnp.zeros_like(halo)

    def pump(k, ch):
        for direction in (0, 1):
            @pl.when(has(direction, k))
            def _():
                b = origin(direction, k)
                landed = block_piece(b, ch, z_span(slab))
                z_copy(direction, k, ch, landed, b).wait_recv()

                @pl.when(can_send(direction))
                def _():
                    z_copy(direction, k + 1, ch, landed, b).start()

                y_copy(direction, k, ch, slab).start()

    def conv_tile(t, carry):
        cols = pl.ds(pl.multiple_of(t * LANES, LANES), LANES)

        def short(s):
            x = xbuf[s, :, cols].astype(jnp.float32)
            ext[HALO:, :] = x
            ext[:HALO, :] = halo[s, :, cols].astype(jnp.float32)
            return (
                sw_ref[s, 0:1, cols] * x
                + sw_ref[s, 1:2, cols] * ext[HALO - 1 : tok + HALO - 1, :]
                + sw_ref[s, 2:3, cols] * ext[HALO - 2 : tok + HALO - 2, :]
            )

        q_buf[:, cols] = short(0)
        product = short(1)
        product = product * short(2)

        pick_wide = (
            iota((groups, WIDE), 0) == t * PER_TILE + iota((groups, WIDE), 1) // BLOCK
        ).astype(jnp.float32)
        pick = (
            iota((groups, LANES), 0) == t * PER_TILE + iota((groups, LANES), 1) // GROUP
        ).astype(jnp.float32)

        def spread(table, which):
            return jnp.dot(table, which, precision=HIGHEST, preferred_element_type=jnp.float32)

        rate, res = rate_ref[...], res_ref[...]
        rate_rep, res_rep = spread(rate, pick_wide), spread(res, pick_wide)
        rate_c, res_c = spread(rate, pick), spread(res, pick)
        diagonal = iota((modes, LANES), 0) == iota((modes, LANES), 1) % GROUP
        rate_row = jnp.sum(jnp.where(diagonal, rate_c, 0.0), axis=0, keepdims=True)
        res_row = jnp.sum(jnp.where(diagonal, res_c, 0.0), axis=0, keepdims=True)
        ahead = (iota((BLOCK, LANES), 0) + 1).astype(jnp.float32)
        read = (res_row * jnp.exp(-rate_row * ahead)).astype(jnp.bfloat16)

        lane = iota((modes, WIDE), 1) % BLOCK
        back = ((BLOCK - lane) % BLOCK).astype(jnp.float32)
        row = jnp.sum(res_rep * jnp.exp(-rate_rep * back), axis=0, keepdims=True)
        lower = iota((BLOCK, BLOCK), 1) <= iota((BLOCK, BLOCK), 0)
        for g in range(PER_TILE):
            part = slice(g * BLOCK, (g + 1) * BLOCK)
            wide = jnp.broadcast_to(row[:, part], (BLOCK, BLOCK))
            table = pltpu.roll(wide, 0, 1, stride=1, stride_axis=0)
            lhs[:BLOCK, part] = jnp.where(lower, table, 0.0).astype(jnp.bfloat16)
        lhs[BLOCK:, :] = jnp.exp(-rate_rep * (BLOCK - 1 - lane).astype(jnp.float32)).astype(
            jnp.bfloat16
        )

        decay = jnp.exp(-rate_c * BLOCK)
        state = jnp.zeros((modes, LANES), jnp.float32)
        for b in range(blocks):
            rows_b = slice(b * BLOCK, (b + 1) * BLOCK)
            p_b = product[rows_b]
            made = jnp.dot(
                lhs[...], masked_rows(p_b.astype(jnp.bfloat16)), preferred_element_type=jnp.float32
            )
            value = made[:BLOCK] + skip_ref[:, cols] * p_b
            if b > 0:
                value = value + jnp.dot(
                    read, masked_rows(state.astype(jnp.bfloat16)), preferred_element_type=jnp.float32
                )
            base[rows_b, cols] = value
            state = decay * state + made[BLOCK:]
        own_end[:, cols] = state
        rate_ch[:, cols] = rate_c
        readout[:, cols] = read
        return carry

    steps = [(k, ch) for k in range(count - 1) for ch in range(chunks)]
    total = len(steps)
    early = 1
    part = tiles // (early + 1)
    for e in range(early + 1):
        stop = tiles if e == early else (e + 1) * part
        lax.fori_loop(e * part, stop, conv_tile, 0)
        if e < early:
            pump(*steps[e])

    def end_copy(d):
        return pltpu.make_async_remote_copy(
            src_ref=own_end, dst_ref=ends.at[seq],
            send_sem=end_send.at[d], recv_sem=end_recv.at[seq],
            device_id={"seq": seq + d}, device_id_type=MESH,
        )

    def arrived_end(source):
        return pltpu.make_async_remote_copy(
            src_ref=own_end, dst_ref=ends.at[source],
            send_sem=end_send.at[0], recv_sem=end_recv.at[source],
            device_id={"seq": seq - 1}, device_id_type=MESH,
        )

    for d in range(1, count):
        @pl.when(seq + d < count)
        def _():
            end_copy(d).start()

    pump(*steps[early])
    prior[...] = jnp.zeros_like(prior)
    for source in range(count - 1):
        @pl.when(source < seq)
        def _():
            arrived_end(source).wait_recv()
            prior[...] = prior[...] * jnp.exp(-rate_ch[...] * tok) + ends[source]

    def gate_tile(t, carry):
        cols = pl.ds(pl.multiple_of(t * LANES, LANES), LANES)
        read = readout[:, cols]
        decay = jnp.exp(-rate_ch[:, cols] * BLOCK)
        state = prior[:, cols]
        for b in range(blocks):
            rows_b = slice(b * BLOCK, (b + 1) * BLOCK)
            across = jnp.dot(
                read, masked_rows(state.astype(jnp.bfloat16)), preferred_element_type=jnp.float32
            )
            gated[chan, rows_b, cols] = (
                q_buf[rows_b, cols] * (base[rows_b, cols] + across)
            ).astype(jnp.bfloat16)
            state = decay * state
        return carry

    share = chans // GATE_PARTS

    def gate_copy(d, i):
        part_ref = gated.at[chan, :, pl.ds(i * share, share)]
        return pltpu.make_async_remote_copy(
            src_ref=part_ref, dst_ref=part_ref,
            send_sem=gate_send.at[d, i], recv_sem=gate_recv.at[chan, i],
            device_id={"chan": lax.rem(chan + d, n_chan)}, device_id_type=MESH,
        )

    def arrived_gate(d, i):
        source = lax.rem(chan + d, n_chan)
        part_ref = gated.at[source, :, pl.ds(i * share, share)]
        return pltpu.make_async_remote_copy(
            src_ref=part_ref, dst_ref=part_ref,
            send_sem=gate_send.at[0, i], recv_sem=gate_recv.at[source, i],
            device_id={"chan": source}, device_id_type=MESH,
        )

    for i in range(GATE_PARTS):
        lax.fori_loop(i * tiles // GATE_PARTS, (i + 1) * tiles // GATE_PARTS, gate_tile, 0)
        for d in range(1, n_chan):
            gate_copy(d, i).start()

    middle = max(min(2, total), total * 2 // 3)
    for e in range(early + 1, middle):
        pump(*steps[e])
    acc[...] = jnp.zeros_like(acc)
    w_copy.wait()
    for d in range(1, n_chan):
        for i in range(GATE_PARTS):
            arrived_gate(d, i).wait_recv()

    streamed = chunks > 1
    col_tile = min(512, out_cols)

    def multiply(b, ch):
        c, r = split(ch)
        a = gated[c, :, pl.ds(pl.multiple_of(b * local_rows + r * rows, LANES), rows)]

        def column(n, carry):
            cols = pl.ds(pl.multiple_of(n * col_tile, col_tile), col_tile)
            w = wbuf[b, c, pl.ds(pl.multiple_of(r * rows, rows), rows), cols]
            acc[:, cols] += jnp.dot(a, w, preferred_element_type=jnp.float32)
            return carry

        lax.fori_loop(0, out_cols // col_tile, column, 0)

    def consume(k, ch):
        for direction in (0, 1):
            @pl.when(has(direction, k))
            def _():
                y_copy(direction, k, ch, other_slab).wait_recv()
                if streamed:
                    multiply(origin(direction, k), ch)

    left_over = total - middle
    own_per = -(-chunks // left_over)
    per = -(-total // left_over)

    def both(j, carry):
        pump(j // chunks, j % chunks)
        if streamed:
            for i in range(own_per):
                ch = (j - middle) * own_per + i

                @pl.when(ch < chunks)
                def _():
                    multiply(seq, ch)

        def late(i, inner):
            old = (j - middle) * per + i

            @pl.when(old < total)
            def _():
                consume(old // chunks, old % chunks)

            return inner

        lax.fori_loop(0, per, late, 0)
        return carry

    lax.fori_loop(middle, total, both, 0)

    if not streamed:
        def whole_column(n, carry):
            cols = pl.ds(pl.multiple_of(n * half, half), half)
            for c in range(n_chan):
                w = wbuf[:, c, :, cols].reshape(count * local_rows, half)
                acc[:, cols] += jnp.dot(gated[c], w, preferred_element_type=jnp.float32)
            return carry

        lax.fori_loop(0, slabs, whole_column, 0)

    quarter = tok // 4

    def rep_copy(i, side):
        return pltpu.make_async_remote_copy(
            src_ref=acc.at[
                pl.ds(i * quarter, quarter), pl.ds(pl.multiple_of(side * out_half, LANES), out_half)
            ],
            dst_ref=peer.at[pl.ds(i * quarter, quarter), :],
            send_sem=rep_send.at[i], recv_sem=rep_recv.at[i],
            device_id={"rep": other_rep}, device_id_type=MESH,
        )

    for i in range(4):
        rep_copy(i, other_rep).start()
    mine = pl.ds(pl.multiple_of(rep * out_half, LANES), out_half)
    for i in range(4):
        rep_copy(i, other_rep).wait_recv()
        rows_i = pl.ds(i * quarter, quarter)
        out_ref[rows_i, :] = (acc[rows_i, mine] + peer[rows_i, :]).astype(jnp.bfloat16)

    for i in range(4):
        rep_copy(i, other_rep).wait_send()
    for d in range(1, n_chan):
        for i in range(GATE_PARTS):
            gate_copy(d, i).wait_send()
    for d in range(1, count):
        @pl.when(seq + d < count)
        def _():
            end_copy(d).wait_send()

    @pl.when(seq < count - 1)
    def _():
        halo_copy().wait_send()

    for ch in range(chunks):
        for direction in (0, 1):
            @pl.when(can_send(direction))
            def _():
                z_copy(direction, 0, ch, own_piece(ch), seq).wait_send()

    def drain(j, carry):
        k, ch = j // chunks, j % chunks
        for direction in (0, 1):
            @pl.when(has(direction, k))
            def _():
                y_copy(direction, k, ch, slab).wait_send()

                @pl.when(can_send(direction))
                def _():
                    b = origin(direction, k)
                    z_copy(direction, k + 1, ch, block_piece(b, ch, z_span(slab)), b).wait_send()
        return carry

    lax.fori_loop(0, total, drain, 0)


def per_device(projected, short_weight, skip_gain, pole_rate, residue, out_weight):
    tok, _, chans = projected.shape
    modes, groups = pole_rate.shape
    n_chan, _, local_rows, out_cols = out_weight.shape
    count, slabs = lax.axis_size("seq"), lax.axis_size("groups")
    n_rep = lax.axis_size("rep")
    row_chunks = max(1, local_rows // 256)
    chunks = n_chan * row_chunks if local_rows % LANES == 0 else 1
    dims = (count, slabs, n_chan, n_rep, chunks, row_chunks)
    f32, bf16 = jnp.float32, jnp.bfloat16
    dma = pltpu.SemaphoreType.DMA
    anywhere = pl.BlockSpec(memory_space=pl.ANY)
    vmem = pl.BlockSpec(memory_space=pltpu.VMEM)
    return pl.pallas_call(
        functools.partial(kernel, dims),
        in_specs=[anywhere, vmem, vmem, vmem, vmem, anywhere],
        out_specs=vmem,
        out_shape=jax.ShapeDtypeStruct((tok, out_cols // n_rep), bf16),
        scratch_shapes=[
            pltpu.VMEM((3, tok, chans), bf16),
            pltpu.VMEM((3, HALO, chans), bf16),
            pltpu.VMEM((tok + HALO, LANES), f32),
            pltpu.VMEM((BLOCK + modes, WIDE), bf16),
            pltpu.VMEM((tok, chans), f32),
            pltpu.VMEM((tok, chans), f32),
            pltpu.VMEM((count, modes, chans), f32),
            pltpu.VMEM((modes, chans), f32),
            pltpu.VMEM((modes, chans), f32),
            pltpu.VMEM((modes, chans), f32),
            pltpu.VMEM((BLOCK, chans), bf16),
            pltpu.VMEM((n_chan, tok, chans), bf16),
            pltpu.VMEM((count, n_chan, local_rows, out_cols), bf16),
            pltpu.VMEM((tok, out_cols), f32),
            pltpu.VMEM((tok, out_cols // n_rep), f32),
            dma((2,)),
            dma((2,)),
            dma((count,)),
            dma((count,)),
            dma((n_chan, GATE_PARTS)),
            dma((n_chan, GATE_PARTS)),
            dma((2, count, chunks)),
            dma((2, count, chunks)),
            dma((2, count, chunks)),
            dma((2, count, chunks)),
            dma((4,)),
            dma((4,)),
        ],
        compiler_params=pltpu.CompilerParams(
            collective_id=0, has_side_effects=True, vmem_limit_bytes=60 * 1024 * 1024
        ),
        name="hyena",
    )(
        projected.transpose(1, 0, 2), short_weight, skip_gain[None], pole_rate, residue, out_weight
    )


PARTS = 4
LEAD = 8


def lag_table(rate_ref, res_ref, lag_rows):
    rate, res = rate_ref[...], res_ref[...]
    modes, groups = rate.shape
    back = ((BLOCK - iota((BLOCK, groups), 0)) % BLOCK).astype(jnp.float32)
    total = jnp.zeros((BLOCK, groups), jnp.float32)
    for n in range(modes):
        total = total + res[n : n + 1] * jnp.exp(-rate[n : n + 1] * back)
    lag_rows[...] = total.T


def by_channel(table, t):
    index = t * PER_TILE + iota(table.shape, 1) // GROUP
    return jnp.take_along_axis(table, index, axis=1)


def by_mode(spread):
    diagonal = iota(spread.shape, 0) == iota(spread.shape, 1) % GROUP
    return jnp.sum(jnp.where(diagonal, spread, 0.0), axis=0, keepdims=True)


def fill(ext, xbuf, s, cols, rows):
    ext[LEAD : LEAD + rows, :] = xbuf[s, :rows, cols].astype(jnp.float32)


def lead(ext, halo, s, cols):
    ext[LEAD - 2 : LEAD, :] = halo[2 * s : 2 * s + 2, cols]


def short(ext, sw_ref, s, cols, b):
    start = LEAD + b * BLOCK
    total = sw_ref[s, 0:1, cols] * ext[start : start + BLOCK, :]
    for j in (1, 2):
        total = total + sw_ref[s, j : j + 1, cols] * ext[start - j : start - j + BLOCK, :]
    return total


def own_modes(every):
    lane_group = iota((GROUP, LANES), 1) // GROUP
    own = jnp.zeros((GROUP, LANES), jnp.float32)
    for g in range(PER_TILE):
        own = jnp.where(lane_group == g, every[g * GROUP : (g + 1) * GROUP], own)
    return own


def later_blocks(t, xbuf, sw_ref, rate_ref, ext, ext2, product, made, intakes):
    cols = pl.ds(pl.multiple_of(t * LANES, LANES), LANES)
    tok = xbuf.shape[1]
    blocks = tok // BLOCK
    fill(ext, xbuf, 1, cols, tok)
    fill(ext2, xbuf, 2, cols, tok)
    rate_row = by_mode(by_channel(rate_ref[...], t))
    behind = (BLOCK - 1 - iota((BLOCK, LANES), 0)).astype(jnp.float32)
    intake = jnp.exp(-rate_row * behind).T.astype(jnp.bfloat16)
    intakes[t] = intake
    parts = []
    for b in range(1, blocks):
        p = short(ext, sw_ref, 1, cols, b) * short(ext2, sw_ref, 2, cols, b)
        product[b * BLOCK : (b + 1) * BLOCK, cols] = p
        parts.append(p.astype(jnp.bfloat16))
    every = jnp.dot(
        intake, jnp.concatenate(parts, axis=1), preferred_element_type=jnp.float32
    )
    for b in range(1, blocks):
        made[b, :, cols] = own_modes(every[:, (b - 1) * LANES : b * LANES])


def first_block(t, xbuf, halo, sw_ref, rate_ref, ext, ext2, product, made, intakes, own_end):
    cols = pl.ds(pl.multiple_of(t * LANES, LANES), LANES)
    blocks = xbuf.shape[1] // BLOCK
    for e, s in ((ext, 1), (ext2, 2)):
        fill(e, xbuf, s, cols, BLOCK)
        lead(e, halo, s, cols)
    p = short(ext, sw_ref, 1, cols, 0) * short(ext2, sw_ref, 2, cols, 0)
    product[:BLOCK, cols] = p
    state = own_modes(
        jnp.dot(intakes[t], p.astype(jnp.bfloat16), preferred_element_type=jnp.float32)
    )
    made[0, :, cols] = state
    decay = jnp.exp(-by_channel(rate_ref[...], t) * BLOCK)
    for b in range(1, blocks):
        state = decay * state + made[b, :, cols]
    own_end[:, cols] = state


def whole_intake(t, xbuf, halo, sw_ref, rate_ref, ext, ext2, product, made, own_end):
    cols = pl.ds(pl.multiple_of(t * LANES, LANES), LANES)
    tok = xbuf.shape[1]
    blocks = tok // BLOCK
    for e, s in ((ext, 1), (ext2, 2)):
        fill(e, xbuf, s, cols, tok)
        lead(e, halo, s, cols)
    rate_c = by_channel(rate_ref[...], t)
    behind = (BLOCK - 1 - iota((BLOCK, LANES), 0)).astype(jnp.float32)
    intake = jnp.exp(-by_mode(rate_c) * behind).T.astype(jnp.bfloat16)
    parts = []
    for b in range(blocks):
        p = short(ext, sw_ref, 1, cols, b) * short(ext2, sw_ref, 2, cols, b)
        product[b * BLOCK : (b + 1) * BLOCK, cols] = p
        parts.append(p.astype(jnp.bfloat16))
    every = jnp.dot(
        intake, jnp.concatenate(parts, axis=1), preferred_element_type=jnp.float32
    )
    decay = jnp.exp(-rate_c * BLOCK)
    state = jnp.zeros_like(decay)
    for b in range(blocks):
        own = own_modes(every[:, b * LANES : (b + 1) * LANES])
        made[b, :, cols] = own
        state = decay * state + own
    own_end[:, cols] = state


def table_tile(t, lag_rows, tables):
    lower = iota((BLOCK, BLOCK), 1) <= iota((BLOCK, BLOCK), 0)
    rows = lag_rows[pl.ds(pl.multiple_of(t * PER_TILE, PER_TILE), PER_TILE), :]
    for g in range(PER_TILE):
        wide = jnp.broadcast_to(rows[g : g + 1], (BLOCK, BLOCK))
        table = pltpu.roll(wide, 0, 1, stride=1, stride_axis=0)
        tables[t, :, g * BLOCK : (g + 1) * BLOCK] = jnp.where(lower, table, 0.0).astype(
            jnp.bfloat16
        )


def gate_tile(t, xbuf, halo, sw_ref, skip_ref, rate_ref, res_ref, tables, ext, product, made,
              prior, dst, dst_cols):
    cols = pl.ds(pl.multiple_of(t * LANES, LANES), LANES)
    blocks = xbuf.shape[1] // BLOCK
    fill(ext, xbuf, 0, cols, blocks * BLOCK)
    lead(ext, halo, 0, cols)
    rate_c = by_channel(rate_ref[...], t)
    rate_row, res_row = by_mode(rate_c), by_mode(by_channel(res_ref[...], t))
    ahead = (iota((BLOCK, LANES), 0) + 1).astype(jnp.float32)
    read = (res_row * jnp.exp(-rate_row * ahead)).astype(jnp.bfloat16)
    lhs = jnp.concatenate([tables[t], read], axis=1)
    decay = jnp.exp(-rate_c * BLOCK)
    state = prior[:, cols]
    for pair in range(0, blocks, 2):
        sides = []
        for b in range(pair, pair + 2):
            p = product[b * BLOCK : (b + 1) * BLOCK, cols].astype(jnp.bfloat16)
            sides.append(
                jnp.concatenate([masked_rows(p), masked_rows(state.astype(jnp.bfloat16))], axis=0)
            )
            if b < blocks - 1:
                state = decay * state + made[b, :, cols]
        value = jnp.dot(lhs, jnp.concatenate(sides, axis=1), preferred_element_type=jnp.float32)
        for b in range(pair, pair + 2):
            rows_b = slice(b * BLOCK, (b + 1) * BLOCK)
            v = value[:, (b - pair) * LANES : (b - pair + 1) * LANES]
            v = v + skip_ref[:, cols] * product[rows_b, cols]
            dst[rows_b, dst_cols] = (short(ext, sw_ref, 0, cols, b) * v).astype(jnp.bfloat16)


def half_kernel(x_hbm, sw_ref, skip_ref, rate_ref, res_ref, w_hbm, out_ref,
                xbuf, tail, halo_out, halo, ext, ext2, product, made, intakes, own_end, prior,
                lag_rows, tables, away, held, wbuf, mine, theirs, peer, outgoing, incoming, done,
                local_sem, halo_sem, end_send, end_recv, wz_send, wz_recv, wy_send, wy_recv,
                own_send, own_recv, z_send, z_recv, x_send, x_recv,
                core_send, core_recv, back_send, back_recv, out_sem):
    count = 4
    tok, chans = product.shape
    half = chans // 2
    local_rows, out_cols = w_hbm.shape[2], w_hbm.shape[3]
    out_half = out_cols // 2
    wide = out_half // PARTS
    tiles = half // LANES
    slab = lax.axis_index("groups")
    seq = lax.axis_index("seq")
    chan = lax.axis_index("chan")
    rep = lax.axis_index("rep")
    side = seq // 2
    mate = seq + 1 - 2 * (seq % 2)
    worker = 2 - side
    is_worker = jnp.logical_or(seq == 1, seq == 2)
    is_far = jnp.logical_or(seq == 0, seq == 3)
    sources = (3 - seq, 6 - 3 * seq)
    to_slot = jnp.where(is_worker, 0, 1)

    barrier = pltpu.get_barrier_semaphore()

    def greet(target):
        pl.semaphore_signal(barrier, inc=1, device_id=target, device_id_type=MESH)

    def span(start, size):
        return pl.ds(pl.multiple_of(start, LANES), size)

    def remote(src, dst, send, recv, target):
        return pltpu.make_async_remote_copy(
            src_ref=src, dst_ref=dst, send_sem=send, recv_sem=recv,
            device_id=target, device_id_type=MESH,
        )

    def on(condition, steps):
        @pl.when(condition)
        def _():
            for step, *args in steps:
                step(*args)

    def x_copy(h):
        cols = span(h * half, half)
        return pltpu.make_async_copy(x_hbm.at[:, :, cols], xbuf.at[:, :, cols], local_sem.at[h])

    tail_copy = pltpu.make_async_copy(
        x_hbm.at[:, pl.ds(tok - HALO, HALO), :], tail, local_sem.at[3]
    )
    tail_copy.start()
    x_copy(0).start()
    x_copy(1).start()

    for d in range(1, count):
        greet({"seq": lax.rem(seq + d, count)})
    greet({"chan": 1 - chan})
    greet({"groups": 1 - slab})
    greet({"rep": 1 - rep})
    tail_copy.wait()
    halo_out[...] = jnp.zeros_like(halo_out)
    for s in range(3):
        halo_out[2 * s : 2 * s + 2, :] = tail[s].astype(jnp.float32)[HALO - 2 :]
    def take_later(h):
        x_copy(h).wait()

        def one(t, carry):
            later_blocks(
                h * tiles + t, xbuf, sw_ref, rate_ref, ext, ext2, product, made, intakes
            )
            return carry

        lax.fori_loop(0, tiles, one, 0)

    def take_whole(h):
        x_copy(h).wait()

        def one(t, carry):
            whole_intake(
                h * tiles + t, xbuf, halo, sw_ref, rate_ref, ext, ext2, product, made, own_end
            )
            return carry

        lax.fori_loop(0, tiles, one, 0)

    def take_first(h):
        def one(t, carry):
            first_block(
                h * tiles + t, xbuf, halo, sw_ref, rate_ref, ext, ext2, product, made, intakes,
                own_end,
            )
            return carry

        lax.fori_loop(0, tiles, one, 0)

    @pl.when(seq == 0)
    def _():
        halo[...] = jnp.zeros_like(halo)
        prior[...] = jnp.zeros_like(prior)

    def make_tables(h):
        def one(t, carry):
            table_tile(h * tiles + t, lag_rows, tables)
            return carry

        lax.fori_loop(0, tiles, one, 0)

    def first_tables():
        lag_table(rate_ref, res_ref, lag_rows)
        make_tables(1 - side)

    on(seq == 0, [(take_whole, 0)])
    on(seq > 0, [(first_tables,)])
    pl.semaphore_wait(barrier, count + 2)

    def w_cols(h, j):
        return span(h * out_half + j * wide, wide)

    rows = local_rows // 2
    weight_parts = [(j, c, h) for j in range(PARTS) for c in range(2) for h in range(2)]
    last = len(weight_parts)

    def w_rows(owner, h):
        return pl.ds(pl.multiple_of((owner % 2) * local_rows + h * rows, rows), rows)

    def wz_copy(i):
        j, c, h = weight_parts[i]
        return remote(
            w_hbm.at[c, 0, pl.ds(h * rows, rows), w_cols(slab, j)],
            wbuf.at[c, w_rows(seq, h), w_cols(slab, j)],
            wz_send.at[i], wz_recv.at[i], {"seq": mate},
        )

    def wz_arrived(i):
        j, c, h = weight_parts[i]
        ref = wbuf.at[c, w_rows(mate, h), w_cols(slab, j)]
        return remote(ref, ref, wz_send.at[i], wz_recv.at[i], {"seq": mate})

    def wy_copy(i, side_cols):
        j, c, h = weight_parts[i]
        ref = wbuf.at[c, w_rows(mate, h), w_cols(side_cols, j)]
        return remote(ref, ref, wy_send.at[i], wy_recv.at[i], {"groups": 1 - slab})

    def pass_weight(k):
        for i in (2 * k, 2 * k + 1):
            wz_arrived(i).wait_recv()
            wy_copy(i, slab).start()

    def send_weights(start, stop):
        for i in range(start, stop):
            wz_copy(i).start()

    def halo_copy():
        return remote(halo_out, halo, halo_sem.at[0], halo_sem.at[1], {"seq": seq + 1})

    @pl.when(seq < count - 1)
    def _():
        halo_copy().start()

    w_copy = pltpu.make_async_copy(
        w_hbm.at[:, 0],
        wbuf.at[:, pl.ds(pl.multiple_of((seq % 2) * local_rows, local_rows), local_rows), :],
        local_sem.at[2],
    )

    def halo_ready():
        remote(halo, halo, halo_sem.at[0], halo_sem.at[1], {"seq": seq - 1}).wait_recv()

    def end_copy(h):
        cols = span(h * half, half)
        return remote(
            own_end.at[:, cols], prior.at[:, cols], end_send.at[h], end_recv.at[h],
            {"seq": seq + 1},
        )

    def hand_on(h):
        cols = span(h * half, half)
        ref = prior.at[:, cols]

        @pl.when(seq > 0)
        def _():
            remote(ref, ref, end_send.at[h], end_recv.at[h], {"seq": seq - 1}).wait_recv()

        @pl.when(seq == 0)
        def _():
            end_copy(h).start()

        @pl.when(is_worker)
        def _():
            rate_c = jnp.concatenate(
                [by_channel(rate_ref[...], h * tiles + t) for t in range(tiles)], axis=1
            )
            own_end[:, cols] = own_end[:, cols] + prior[:, cols] * jnp.exp(-rate_c * tok)
            end_copy(h).start()

    def z_copy(i):
        cols = span(i * LANES, LANES)
        return remote(
            away.at[:, cols], held.at[to_slot, 0, :, cols], z_send.at[i],
            z_recv.at[to_slot, i], {"seq": worker},
        )

    def z_arrived(slot, i):
        ref = held.at[slot, 0, :, pl.ds(i * LANES, LANES)]
        return remote(ref, ref, z_send.at[i], z_recv.at[slot, i], {"seq": sources[slot]})

    def own_copy(i):
        cols = span(i * LANES, LANES)
        return remote(
            held.at[2, 0, :, cols], held.at[2, 1, :, cols], own_send.at[i], own_recv.at[i],
            {"chan": 1 - chan},
        )

    def across_copy(slot, i):
        cols = pl.ds(i * LANES, LANES)
        return remote(
            held.at[slot, 0, :, cols], held.at[slot, 1, :, cols], x_send.at[slot, i],
            x_recv.at[slot, i], {"chan": 1 - chan},
        )

    def pass_gated(slot, start, stop):
        for i in range(start, stop):
            z_arrived(slot, i).wait_recv()
            across_copy(slot, i).start()

    def send_away(start, stop):
        for i in range(start, stop):
            z_copy(i).start()

    def send_own(start, stop):
        for i in range(start, stop):
            own_copy(i).start()

    def gate(h, start, stop, dst, sent=False):
        def one(t, carry):
            gate_tile(
                h * tiles + t, xbuf, halo, sw_ref, skip_ref, rate_ref, res_ref, tables, ext,
                product, made, prior, dst, span(t * LANES, LANES),
            )
            if sent:
                @pl.when(is_worker)
                def _():
                    z_copy(t).start()

            return carry

        lax.fori_loop(start, stop, one, 0)

    on(seq == 0, [(hand_on, 0), (send_weights, 0, 1)])
    on(seq == 1, [(send_weights, 0, last)])
    on(seq == 2, [(send_weights, 0, 5)])
    on(seq == 3, [(send_weights, 0, 12)])
    w_copy.start()
    on(seq > 0, [(take_later, 0)])
    on(seq == 0, [(take_whole, 1), (hand_on, 1), (send_weights, 1, 10)])
    on(seq > 0, [(take_later, 1), (halo_ready,), (take_first, 0)])
    on(seq == 1, [(hand_on, 0), (take_first, 1)])
    on(seq == 0, [(first_tables,)])
    on(seq == 1, [(hand_on, 1)])
    on(seq >= 2, [(take_first, 1), (hand_on, 0)])
    gate(1 - side, 0, tiles, away, True)
    on(seq == 0, [(send_away, 0, 8), (send_weights, 10, last)])
    on(seq == 3, [(send_away, 0, 8), (send_weights, 12, last)])
    on(seq >= 2, [(hand_on, 1)])
    on(seq == 2, [(send_weights, 5, last)])
    make_tables(side)
    on(is_worker, [(pass_gated, 0, 0, 1)])
    pass_weight(0)
    gate(side, 0, tiles // 2, held.at[2, 0])
    on(is_worker, [(pass_gated, 0, 1, 2)])
    gate(side, tiles // 2, tiles, held.at[2, 0])

    def core_copy(slot, j):
        return remote(
            theirs.at[slot, :, span(j * wide, wide)], peer.at[slot, :, span(j * wide, wide)],
            core_send.at[slot, j], core_recv.at[slot, j], {"rep": 1 - rep},
        )

    def multiply(slot, j):
        cols = span(j * wide, wide)

        def one(h, dst):
            w_at = w_cols(h, j)
            total = jnp.dot(
                held[slot, 0], wbuf[chan, :, w_at], preferred_element_type=jnp.float32
            )
            dst[slot, :, cols] = total + jnp.dot(
                held[slot, 1], wbuf[1 - chan, :, w_at], preferred_element_type=jnp.float32
            )

        one(1 - rep, theirs)
        core_copy(slot, j).start()
        one(rep, mine)

    def back_copy(slot, j):
        cols = pl.ds(j * wide, wide)
        return remote(
            outgoing.at[slot, :, cols], incoming.at[:, cols], back_send.at[slot, j],
            back_recv.at[j], {"seq": sources[slot]},
        )

    def back_arrived(j):
        ref = incoming.at[:, pl.ds(j * wide, wide)]
        return remote(ref, ref, back_send.at[0, j], back_recv.at[j], {"seq": worker})

    def finish(slot, j):
        cols = span(j * wide, wide)
        core_copy(slot, j).wait_recv()
        total = mine[slot, :, cols] + peer[slot, :, cols]
        if slot == 2:
            mine[slot, :, cols] = total
        else:
            outgoing[slot, :, cols] = total.astype(jnp.bfloat16)
            back_copy(slot, j).start()

    def weight_ready(j):
        for i, (part, _, _) in enumerate(weight_parts):
            if part == j:
                wy_copy(i, 1 - slab).wait_recv()

    def gated_ready(slot):
        for i in range(tiles):
            across_copy(slot, i).wait_recv()

    def own_ready():
        for i in range(tiles):
            own_copy(i).wait_recv()

    far = [(send_own, 0, tiles)] + [(pass_weight, i) for i in range(1, 2 * PARTS)]
    far += [(w_copy.wait,)] + [(weight_ready, j) for j in range(PARTS)]
    on(is_far, far)

    near = [
        (pass_gated, 0, 2, 3), (pass_weight, 1), (pass_gated, 0, 3, 5), (pass_weight, 2),
        (pass_gated, 0, 5, 7), (pass_weight, 3), (pass_gated, 0, 7, 8), (w_copy.wait,),
        (pass_weight, 4), (pass_gated, 1, 0, 2),
        (gated_ready, 0), (weight_ready, 0), (multiply, 0, 0), (finish, 0, 0),
        (pass_gated, 1, 2, 4), (weight_ready, 1), (multiply, 0, 1), (finish, 0, 1),
        (pass_gated, 1, 4, 8), (pass_weight, 5), (gated_ready, 1), (send_own, 0, 8),
        (multiply, 1, 0), (finish, 1, 0), (pass_weight, 6), (multiply, 1, 1), (finish, 1, 1),
        (weight_ready, 2), (multiply, 0, 2), (finish, 0, 2), (multiply, 1, 2), (finish, 1, 2),
        (pass_weight, 7), (weight_ready, 3),
        (multiply, 0, 3), (multiply, 1, 3), (finish, 0, 3), (finish, 1, 3),
    ]
    on(is_worker, near)
    own_ready()

    def own_multiply(j, carry):
        multiply(2, j)

        @pl.when(j > 0)
        def _():
            finish(2, j - 1)

        return carry

    lax.fori_loop(0, PARTS, own_multiply, 0)
    finish(2, PARTS - 1)

    def out_copy(j):
        cols = pl.ds(j * wide, wide)
        return pltpu.make_async_copy(done.at[:, cols], out_ref.at[:, cols], out_sem.at[j])

    for j in range(PARTS):
        cols = pl.ds(j * wide, wide)
        back_arrived(j).wait_recv()
        done[:, cols] = (mine[2, :, cols] + incoming[:, cols].astype(jnp.float32)).astype(
            jnp.bfloat16
        )
        out_copy(j).start()

    @pl.when(seq < count - 1)
    def _():
        halo_copy().wait_send()
        for h in range(2):
            end_copy(h).wait_send()

    for i in range(last):
        wz_copy(i).wait_send()
        wy_copy(i, slab).wait_send()
    for i in range(tiles):
        own_copy(i).wait_send()
        z_copy(i).wait_send()
    for j in range(PARTS):
        core_copy(2, j).wait_send()

    @pl.when(is_worker)
    def _():
        for slot in range(2):
            for i in range(tiles):
                across_copy(slot, i).wait_send()
            for j in range(PARTS):
                core_copy(slot, j).wait_send()
                back_copy(slot, j).wait_send()

    for j in range(PARTS):
        out_copy(j).wait()


def by_halves(projected, short_weight, skip_gain, pole_rate, residue, out_weight):
    tok, _, chans = projected.shape
    modes, groups = pole_rate.shape
    local_rows, out_cols = out_weight.shape[2], out_weight.shape[3]
    half, out_half = chans // 2, out_cols // 2
    tiles = half // LANES
    blocks = tok // BLOCK
    f32, bf16 = jnp.float32, jnp.bfloat16
    dma = pltpu.SemaphoreType.DMA
    anywhere = pl.BlockSpec(memory_space=pl.ANY)
    vmem = pl.BlockSpec(memory_space=pltpu.VMEM)
    return pl.pallas_call(
        half_kernel,
        in_specs=[anywhere, vmem, vmem, vmem, vmem, anywhere],
        out_specs=anywhere,
        out_shape=jax.ShapeDtypeStruct((tok, out_half), bf16),
        scratch_shapes=[
            pltpu.VMEM((3, tok, chans), bf16),
            pltpu.VMEM((3, HALO, chans), bf16),
            pltpu.VMEM((8, chans), f32),
            pltpu.VMEM((8, chans), f32),
            pltpu.VMEM((tok + LEAD, LANES), f32),
            pltpu.VMEM((tok + LEAD, LANES), f32),
            pltpu.VMEM((tok, chans), f32),
            pltpu.VMEM((blocks, modes, chans), f32),
            pltpu.VMEM((chans // LANES, LANES, BLOCK), bf16),
            pltpu.VMEM((modes, chans), f32),
            pltpu.VMEM((modes, chans), f32),
            pltpu.VMEM((groups, BLOCK), f32),
            pltpu.VMEM((chans // LANES, BLOCK, WIDE), bf16),
            pltpu.VMEM((tok, half), bf16),
            pltpu.VMEM((3, 2, tok, half), bf16),
            pltpu.VMEM((2, half, out_cols), bf16),
            pltpu.VMEM((3, tok, out_half), f32),
            pltpu.VMEM((3, tok, out_half), f32),
            pltpu.VMEM((3, tok, out_half), f32),
            pltpu.VMEM((2, tok, out_half), bf16),
            pltpu.VMEM((tok, out_half), bf16),
            pltpu.VMEM((tok, out_half), bf16),
            dma((4,)),
            dma((2,)),
            dma((2,)),
            dma((2,)),
            dma((4 * PARTS,)),
            dma((4 * PARTS,)),
            dma((4 * PARTS,)),
            dma((4 * PARTS,)),
            dma((tiles,)),
            dma((tiles,)),
            dma((tiles,)),
            dma((2, tiles)),
            dma((2, tiles)),
            dma((2, tiles)),
            dma((3, PARTS)),
            dma((3, PARTS)),
            dma((2, PARTS)),
            dma((PARTS,)),
            dma((PARTS,)),
        ],
        compiler_params=pltpu.CompilerParams(
            collective_id=0, has_side_effects=True, vmem_limit_bytes=60 * 1024 * 1024
        ),
        name="hyena_halves",
    )(
        projected.transpose(1, 0, 2), short_weight, skip_gain[None], pole_rate, residue, out_weight
    )


def solution(mesh):
    sizes = tuple(mesh.shape[name] for name in ("groups", "seq", "chan", "rep"))
    return jax.shard_map(
        by_halves if sizes == (2, 4, 2, 2) else per_device,
        mesh=mesh,
        in_specs=(
            P(("groups", "seq"), None, ("chan", "rep")),
            P(None, None, ("chan", "rep")),
            P(("chan", "rep")),
            P(None, ("chan", "rep")),
            P(None, ("chan", "rep")),
            P(None, "rep", "seq", "chan"),
        ),
        out_specs=P(("groups", "seq"), ("chan", "rep")),
        check_vma=False,
    )
```
